32 devices in a mesh: dp: 16 (over z, y, x), tensor: 2 (over core).
Axes of the slice: x: 2, y: 2, z: 4, core: 2. Of those that a mesh axis runs over, the one named last changes fastest.
Arguments:
- layer_in: bfloat16 [16384, 1024], P(('dp', 'tensor')), may hold values from -6 to 6
- w_qkv: bfloat16 [3, 1024, 1024], P(None, 'dp', 'tensor'), may hold values from -1 to 1
- b_qv: bfloat16 [2, 16, 64], P(None, 'tensor', 'dp'), may hold values from -3 to 3
- w_proj: bfloat16 [1024, 1024], P('tensor', 'dp'), may hold values from -0.5 to 0.5
- w_ff1: bfloat16 [1024, 4096], P('dp', 'tensor'), may hold values from -0.1875 to 0.1875
- b_ff1: bfloat16 [64, 64], P('tensor', 'dp'), may hold values from -3 to 3
- w_ff2: bfloat16 [4096, 1024], P('tensor', 'dp'), may hold values from -0.09375 to 0.09375
- norm_gains: float32 [2, 1024], P(None, ('dp', 'tensor')), may hold values from 0.5 to 1.5
- add_biases: float32 [4, 1024], P(None, ('dp', 'tensor')), may hold values from -3 to 3
- cotangent: bfloat16 [16384, 1024], P(('dp', 'tensor')), may hold values from -6 to 6
Outputs:
- layer_out: bfloat16 [16384, 1024], P(('dp', 'tensor'))
- grad_in: float32 [16384, 1024], P(('dp', 'tensor'))
- grad_w_qkv: float32 [3, 1024, 1024], P(None, 'dp', 'tensor')
- grad_b_qv: float32 [2, 16, 64], P(None, 'tensor', 'dp')
- grad_w_proj: float32 [1024, 1024], P('tensor', 'dp')
- grad_w_ff1: float32 [1024, 4096], P('dp', 'tensor')
- grad_b_ff1: float32 [64, 64], P('tensor', 'dp')
- grad_w_ff2: float32 [4096, 1024], P('tensor', 'dp')
- grad_gains: float32 [2, 1024], P(None, ('dp', 'tensor'))
- grad_biases: float32 [4, 1024], P(None, ('dp', 'tensor'))
The draws below stay inside these ranges and needn't reach their ends.
All inputs are finite; a program needn't handle non-finite values.
Results may differ from the reference program's by a relative error of at most 0.015.
Values may be sent and summed in bfloat16 or wider, within the bound.
A program may use at most 192 MiB of HBM per device.

```python
import math
import jax
import jax.numpy as jnp
from jax import lax

D = 1024
H = 16
HD = 64
FF = 4096
SEQ_LEN = 1024
TOKENS = 16384


def draw_w_qkv(key, part):
    base = jax.random.normal(key, (3, D, D), jnp.float32) * D ** (-0.5)
    return jnp.clip(base, -1.0, 1.0).astype(jnp.bfloat16)


def raised(drawn, stream_key, source, target, blocks, factor):
    def block_of(position):
        return (jnp.arange(drawn.shape[position]) // (drawn.shape[position] // blocks)).reshape((-1,) + (1,) * (drawn.ndim - 1 - position))

    one_side = jax.random.permutation(stream_key, blocks)[block_of(target)]
    far = (block_of(target) + blocks // 2) % blocks
    return jnp.where((block_of(source) == one_side) | (block_of(source) == far), factor * drawn, drawn)


def block_levels(stream_key, extent, split, low, high):
    factor_of = 1.0
    for axis_at, parts in split:
        draws = jax.random.uniform(jax.random.fold_in(jax.random.fold_in(stream_key, 6), axis_at), (parts,), jnp.float32, low / len(split), high / len(split))
        factor_of = factor_of * jnp.repeat(jnp.exp(draws), extent[axis_at] // parts).reshape((-1,) + (1,) * (len(extent) - 1 - axis_at))
    return factor_of


def normal_values(key, dims, deviation, most, pieces=(), kind=jnp.bfloat16):
    array = jax.random.normal(key, dims, jnp.float32) * deviation
    if len(pieces) > 0:
        array = block_levels(key, dims, pieces, -0.22, 0.18) * array
    return jnp.clip(array, min=-most, max=most).astype(kind)


def gaussian_with(stream_key, shape, scale, bound, pieces, heavy, held_as=jnp.bfloat16):
    drawn = scale * jax.random.normal(stream_key, shape, jnp.float32)
    if pieces:
        drawn = drawn * block_levels(stream_key, shape, pieces, -0.22, 0.18)
    return jnp.clip(raised(drawn, jax.random.fold_in(stream_key, 3), *heavy), -bound, bound).astype(held_as)


def setup_inputs(seed: int = 0) -> dict:
    key_list = jax.random.split(jax.random.key(seed), 11)
    layer_in = normal_values(key_list[0], (TOKENS, D), 1.0, 6.0, ((0, 32),))
    w_qkv = draw_w_qkv(jax.random.fold_in(key_list[10], 71), 0)
    b_qv = normal_values(key_list[2], (2, H, HD), 0.5, 3.0, ((1, 2), (2, 16)))
    w_proj = normal_values(key_list[3], (D, D), (D // 8) ** -0.5, 0.5, ((0, 2), (1, 16)))
    w_ff1 = normal_values(key_list[4], (D, FF), D ** -0.5, 0.1875, ((0, 16), (1, 2)))
    b_ff1 = normal_values(key_list[5], (FF // HD, HD), 0.5, 3.0, ((0, 2), (1, 16)))
    w_ff2 = normal_values(key_list[6], (FF, D), FF ** -0.5, 0.09375, ((0, 2), (1, 16)))
    norm_gains = jnp.clip(1.0 + 0.1 * jax.random.normal(key_list[7], (2, D), jnp.float32), 0.5, 1.5)
    add_biases = normal_values(key_list[8], (4, D), 0.5, 3.0, ((1, 32),), jnp.float32)
    cotangent = gaussian_with(key_list[9], (TOKENS, D), 1.0, 6.0, ((0, 32),), (0, 1, 32, 2.75))
    return {"layer_in": layer_in, "w_qkv": w_qkv, "b_qv": b_qv, "w_proj": w_proj, "w_ff1": w_ff1, "b_ff1": b_ff1, "w_ff2": w_ff2, "norm_gains": norm_gains, "add_biases": add_biases, "cotangent": cotangent}


epsilon = 1e-05
gelu_scale = 0.7978845608028654
highest = lax.Precision.HIGHEST

@jax.custom_vjp
def low(v):
    return lax.optimization_barrier(v.astype(jnp.bfloat16)).astype(jnp.float32)

@jax.custom_vjp
def low_back(v):
    return v

def low_keep(v):
    return (low(v), None)

def low_pass(kept, grad):
    return (grad,)

def back_keep(v):
    return (v, None)

def back_low(kept, grad):
    return (low(grad),)
low.defvjp(low_keep, low_pass)
low_back.defvjp(back_keep, back_low)

def product(form, left, right):
    return jnp.einsum(form, left, right, precision=highest)

def layer_norm(values, gain_row, shift_row):
    center = values - lax.optimization_barrier(jnp.mean(values, axis=-1, keepdims=True))
    spread = lax.optimization_barrier(jnp.mean(center * center, axis=-1, keepdims=True))
    return center * lax.rsqrt(spread + epsilon) * gain_row + shift_row

def gelu_tanh(inputs):
    return 0.5 * inputs * (1.0 + jnp.tanh(gelu_scale * (inputs + 0.044715 * inputs * inputs * inputs)))

def alibi_slopes():
    return 2.0 ** (-8.0 * jnp.arange(1, H + 1).astype(jnp.float32) / H)

def attend(queries, keys_all, values_all):
    block_len = min(512, SEQ_LEN)
    slopes = alibi_slopes()
    key_pos = jnp.arange(SEQ_LEN).astype(jnp.int32)

    def one_block(start):
        query_rows = lax.dynamic_slice_in_dim(queries, start, block_len, 1)
        query_pos = start + jnp.arange(block_len).astype(jnp.int32)
        scores = product('gqhd,gkhd->ghqk', query_rows, keys_all) * HD ** (-0.5)
        offsets = (key_pos[None, :] - query_pos[:, None]).astype(jnp.float32)
        scores = scores + slopes[:, None, None] * offsets
        scores = jnp.where(key_pos[None, :] <= query_pos[:, None], scores, -1e+30)
        weights = low(jax.nn.softmax(low_back(scores), axis=-1))
        return product('ghqk,gkhd->gqhd', weights, values_all)
    starts = (jnp.arange(SEQ_LEN // block_len) * block_len).astype(jnp.int32)
    blocks = lax.map(jax.checkpoint(one_block), starts)
    return jnp.moveaxis(blocks, 0, 1).reshape(queries.shape)

def forward(params, layer_rows):
    w_qkv, b_qv, w_proj, w_ff1, b_ff1, w_ff2, norm_gains, add_biases = params
    groups = layer_rows.shape[0]
    length = layer_rows.shape[1]
    act_one = low(layer_norm(layer_rows, norm_gains[0], add_biases[0]))
    queries = low_back(low(product('gld,de->gle', act_one, w_qkv[0]) + b_qv[0].reshape(D)))
    keys_all = low_back(low(product('gld,de->gle', act_one, w_qkv[1])))
    values_all = low_back(low(product('gld,de->gle', act_one, w_qkv[2]) + b_qv[1].reshape(D)))
    head_shape = (groups, length, H, HD)
    attended = attend(queries.reshape(head_shape), keys_all.reshape(head_shape), values_all.reshape(head_shape))
    attended = low_back(low(attended.reshape(groups, length, D)))
    middle = layer_rows + low_back(product('gle,ed->gld', attended, w_proj)) + add_biases[1]
    act_two = low(layer_norm(middle, norm_gains[1], add_biases[2]))
    hidden_pre = low_back(product('gld,df->glf', act_two, w_ff1) + b_ff1.reshape(FF))
    hidden = low(gelu_tanh(hidden_pre))
    return middle + product('glf,fd->gld', hidden, w_ff2) + add_biases[3]

def reference(layer_in, w_qkv, b_qv, w_proj, w_ff1, b_ff1, w_ff2, norm_gains, add_biases, cotangent):
    params = tuple((argument.astype(jnp.float32) for argument in (w_qkv, b_qv, w_proj, w_ff1, b_ff1, w_ff2, norm_gains, add_biases)))
    seq_count = layer_in.shape[0] // SEQ_LEN
    seq_group = math.gcd(seq_count, max(1, 4096 // SEQ_LEN))
    layer_rows = layer_in.astype(jnp.float32).reshape(seq_count // seq_group, seq_group, SEQ_LEN, D)
    cot_rows = cotangent.astype(jnp.float32).reshape(layer_rows.shape)

    def step_fn(totals, inputs_pair):
        output, pull_back = jax.vjp(forward, params, inputs_pair[0])
        grad_params, grad_rows = pull_back(inputs_pair[1])
        totals = jax.tree.map(jnp.add, totals, grad_params)
        return (totals, (output.astype(jnp.bfloat16), grad_rows))
    start_sum = jax.tree.map(jnp.zeros_like, params)
    totals, (outputs, grad_rows) = lax.scan(step_fn, start_sum, (layer_rows, cot_rows))
    full_shape = layer_in.shape
    return (outputs.reshape(full_shape), grad_rows.reshape(full_shape), totals[0], totals[1], totals[2], totals[3], totals[4], totals[5], totals[6], totals[7])
```

```python
import functools
import math
import jax
import jax.numpy as jnp
from jax import lax
from jax.experimental import pallas as pl
from jax.experimental.pallas import tpu as pltpu
from jax.sharding import PartitionSpec as P

MESH = pl.DeviceIdType.MESH
ANY = pl.BlockSpec(memory_space=pl.ANY)
VM = pl.BlockSpec(memory_space=pltpu.VMEM)


def bits_of(index, count):
    return [lax.rem(index // (1 << b), 2) for b in range(count)]


def partner_of(index, mine, b):
    return index + (1 - 2 * mine[b]) * (1 << b)


def halving_orders(count):
    return [[(start + i) % count for i in range(count)] for start in range(3)]


def enter(index, mine, count, other):
    barrier = pltpu.get_barrier_semaphore()
    for b in range(count):
        pl.semaphore_signal(barrier, inc=1, device_id={"dp": partner_of(index, mine, b)}, device_id_type=MESH)
    pl.semaphore_signal(barrier, inc=1, device_id={"tensor": other}, device_id_type=MESH)
    pl.semaphore_wait(barrier, count + 1)


def block_index(mine, held, count):
    return tuple(slice(None) if b in held else mine[b] for b in reversed(range(count)))


PATTERN = (0, 1, 0, 1, 0, 1, 0, 2)

def gather_kernel(count, chunks, qkv, proj, up, down, small, x, cot,
                  qkv_o, proj_o, up_o, down_o, small_o, x_o, cot_o,
                  send, recv, own_sem, pair_send, pair_recv):
    me = lax.axis_index("dp")
    t = lax.axis_index("tensor")
    other = 1 - t
    mine = bits_of(me, count)
    orders = [o[::-1] for o in halving_orders(count)]
    full = block_index(mine, (), count)

    def views(c):
        name, lead, lo, size = chunks[c]
        src = {"qkv": qkv, "proj": proj, "up": up, "down": down, "small": small}[name]
        dst = {"qkv": qkv_o, "proj": proj_o, "up": up_o, "down": down_o, "small": small_o}[name]
        if name == "small":
            return src, dst.at[t], (slice(None), slice(None))
        if lead is not None:
            src, dst = src.at[lead], dst.at[lead]
        return src.at[:, pl.ds(lo, size)], dst, (slice(None), pl.ds(lo, size))

    enter(me, mine, count, other)
    local_rows = x.shape[0]
    rows = pl.ds(t * local_rows, local_rows)
    pairs = []
    for i, (s, d) in enumerate(((x, x_o), (cot, cot_o))):
        cp = pltpu.make_async_remote_copy(s, d.at[rows], pair_send.at[i], pair_recv.at[i], device_id={"tensor": other}, device_id_type=MESH)
        cp.start()
        own = pltpu.make_async_copy(s, d.at[rows], own_sem.at[len(chunks) + i])
        own.start()
        pairs += [cp, own]
    owns = []
    for c in range(len(chunks)):
        src, dst, tail = views(c)
        cp = pltpu.make_async_copy(src, dst.at[(*full, *tail)], own_sem.at[c])
        cp.start()
        owns.append(cp)
    sent = {}
    steps = sorted(((c, s) for c in range(len(chunks)) for s in range(count)), key=lambda cs: (cs[0] + 2 * cs[1], cs[0]))
    for c, s in steps:
        order = orders[0] if chunks[c][0] == "small" else orders[PATTERN[c % 8]]
        src, dst, tail = views(c)
        if s == 1:
            owns[c].wait()
        if s > 0:
            sent[c, s - 1].wait_recv()
        at = (*block_index(mine, order[:s], count), *tail)
        cp = pltpu.make_async_remote_copy(src if s == 0 else dst.at[at], dst.at[at], send.at[c * count + s], recv.at[c * count + s],
                                          device_id={"dp": partner_of(me, mine, order[s])}, device_id_type=MESH)
        cp.start()
        sent[c, s] = cp
    for c in range(len(chunks)):
        sent[c, count - 1].wait_recv()
    last = pltpu.make_async_remote_copy(small_o.at[t], small_o.at[t], pair_send.at[2], pair_recv.at[2], device_id={"tensor": other}, device_id_type=MESH)
    last.start()
    for cp in sent.values():
        cp.wait_send()
    for cp in pairs:
        cp.wait()
    last.wait()


def gather_all(qkv, proj, up, down, small, x, cot, n, width=512):
    count = n.bit_length() - 1
    two = (2,) * count
    chunks = [("small", None, 0, 0)]
    for c in range(3):
        chunks += [("qkv", c, lo, width) for lo in range(0, qkv.shape[2], width)]
    for name, a in (("proj", proj), ("up", up), ("down", down)):
        chunks += [(name, None, lo, width) for lo in range(0, a.shape[1], width)]
    sd = lambda s, d: jax.ShapeDtypeStruct(s, d)
    outs = (sd((3, *two, *qkv.shape[1:]), jnp.bfloat16), sd((*two, *proj.shape), jnp.bfloat16), sd((*two, *up.shape), jnp.bfloat16),
            sd((*two, *down.shape), jnp.bfloat16), sd((2, *two, *small.shape), jnp.float32),
            sd((2 * x.shape[0], x.shape[1]), x.dtype), sd((2 * x.shape[0], x.shape[1]), x.dtype))
    k = len(chunks)
    res = pl.pallas_call(
        functools.partial(gather_kernel, count, chunks), out_shape=outs,
        in_specs=[VM] * 7, out_specs=[ANY] * 7,
        scratch_shapes=[pltpu.SemaphoreType.DMA((k * count,)), pltpu.SemaphoreType.DMA((k * count,)), pltpu.SemaphoreType.DMA((k + 2,)),
                        pltpu.SemaphoreType.DMA((3,)), pltpu.SemaphoreType.DMA((3,))],
        compiler_params=pltpu.CompilerParams(collective_id=0, has_side_effects=True), name="gather_all",
    )(qkv, proj, up, down, small, x, cot)
    return res


def scatter_kernel(count, chunks, width, qkv, proj, up, down, small, qkv_o, proj_o, up_o, down_o, small_o, pair_o,
                   acc, sacc, load_sem, send, recv, pair_sem, *landing):
    land, sland = landing[:count], landing[count:]
    me = lax.axis_index("dp")
    t = lax.axis_index("tensor")
    other = 1 - t
    mine = bits_of(me, count)
    orders = halving_orders(count)
    enter(me, mine, count, other)

    def src_view(c):
        name, lead, lo, size = chunks[c]
        if name == "small":
            return small, (slice(None), slice(None))
        ref = {"qkv": qkv, "proj": proj, "up": up, "down": down}[name]
        if lead is not None:
            ref = ref.at[lead]
        return ref, (slice(None), pl.ds(lo, size))

    def order_of(c):
        return orders[0] if chunks[c][0] == "small" else orders[PATTERN[c % 8]]

    def bufs(c):
        if chunks[c][0] == "small":
            return sacc, sland
        return acc.at[c - 1], tuple(r.at[c - 1] for r in land)

    def pick(c, s, flip):
        order = order_of(c)
        out = []
        for b in reversed(range(count)):
            if s > 0 and b == order[0]:
                continue
            if b == order[s]:
                out.append(1 - mine[b] if flip else mine[b])
            elif b in order[:s]:
                out.append(mine[b])
            else:
                out.append(slice(None))
        return tuple(out)

    loads = []
    for c in range(len(chunks)):
        ref, tail = src_view(c)
        cp = pltpu.make_async_copy(ref.at[(*pick(c, 0, False), *tail)], bufs(c)[0], load_sem.at[c])
        loads.append(cp)
    sent = {}
    steps = sorted(((c, s) for c in range(len(chunks)) for s in range(count + 1)), key=lambda cs: (cs[0] + 2 * cs[1], cs[0]))
    for c, s in steps:
        name, lead, lo, size = chunks[c]
        a, l = bufs(c)
        if s > 0:
            sent[c, s - 1].wait_recv()
            if s == 1:
                loads[c].wait()
            r = l[s - 1]
            left = count - s
            if s < count:
                base = pick(c, s - 1, False) if s > 1 else (slice(None),) * (count - 1)

                def add(i, carry, base=base, a=a, r=r, left=left):
                    sub = [lax.rem(i // (1 << (left - 1 - j)), 2) for j in range(left)]
                    it = iter(sub)
                    at = tuple(next(it) if isinstance(b, slice) else b for b in base)
                    a[at] = (a[at].astype(jnp.float32) + r[tuple(sub)].astype(jnp.float32)).astype(a.dtype)
                    return carry

                lax.fori_loop(0, 1 << left, add, 0)
            else:
                at = pick(c, s - 1, False)
                total = a[at].astype(jnp.float32) + r[...].astype(jnp.float32)
                if name == "small":
                    small_o[...] = total
                else:
                    ref = {"qkv": qkv_o, "proj": proj_o, "up": up_o, "down": down_o}[name]
                    if lead is not None:
                        ref = ref.at[lead]
                    ref[:, lo : lo + size] = total
        if s < count:
            if s == 0:
                loads[c].start()
                ref, tail = src_view(c)
                src = ref.at[(*pick(c, 0, True), *tail)]
            else:
                src = a.at[pick(c, s, True)]
            cp = pltpu.make_async_remote_copy(src, l[s], send.at[c * count + s], recv.at[c * count + s],
                                              device_id={"dp": partner_of(me, mine, order_of(c)[s])}, device_id_type=MESH)
            cp.start()
            sent[c, s] = cp
    last = pltpu.make_async_remote_copy(small_o, pair_o, pair_sem.at[0], pair_sem.at[1], device_id={"tensor": other}, device_id_type=MESH)
    last.start()
    for cp in sent.values():
        cp.wait_send()
    last.wait()


def scatter_all(qkv, proj, up, down, small, n, width=512):
    count = n.bit_length() - 1
    two = (2,) * count
    rows = up.shape[-2]
    chunks = [("small", None, 0, 0)]
    for name, a in (("down", down), ("up", up), ("proj", proj)):
        chunks += [(name, None, lo, width) for lo in range(0, a.shape[-1], width)]
    for c in range(3):
        chunks += [("qkv", c, lo, width) for lo in range(0, qkv.shape[-1], width)]
    k = len(chunks)
    f = lambda *s: jax.ShapeDtypeStruct(s, jnp.float32)
    outs = (f(3, rows, qkv.shape[-1]), f(rows, proj.shape[-1]), f(rows, up.shape[-1]), f(rows, down.shape[-1]), f(8, 128), f(8, 128))
    landing = [pltpu.VMEM((k - 1, *two[: count - 1 - s], rows, width), jnp.bfloat16) for s in range(count)]
    landing += [pltpu.VMEM((*two[: count - 1 - s], 8, 128), jnp.float32) for s in range(count)]
    return pl.pallas_call(
        functools.partial(scatter_kernel, count, chunks, width), out_shape=outs,
        in_specs=[ANY] * 5, out_specs=[VM] * 6,
        scratch_shapes=[pltpu.VMEM((k - 1, *two[:-1], rows, width), jnp.bfloat16), pltpu.VMEM((*two[:-1], 8, 128), jnp.float32),
                        pltpu.SemaphoreType.DMA((k,)), pltpu.SemaphoreType.DMA((k * count,)), pltpu.SemaphoreType.DMA((k * count,)),
                        pltpu.SemaphoreType.DMA((2,)), *landing],
        compiler_params=pltpu.CompilerParams(collective_id=1, has_side_effects=True, vmem_limit_bytes=48 * 2**20), name="scatter_all",
    )(qkv, proj, up, down, small)


def swap_kernel(half, src, dst, sems):
    me = lax.axis_index("dp")
    other = 1 - lax.axis_index("tensor")
    barrier = pltpu.get_barrier_semaphore()
    pl.semaphore_signal(barrier, inc=1, device_id={"tensor": other}, device_id_type=MESH)
    pl.semaphore_wait(barrier, 1)
    if half:
        rows = dst.shape[0]
        src = src.at[pl.ds(other * rows, rows)]
    cp = pltpu.make_async_remote_copy(src, dst, sems.at[0], sems.at[1], device_id={"tensor": other}, device_id_type=MESH)
    cp.start()
    cp.wait()


def swap(a, collective_id, half=False):
    shape = (a.shape[0] // 2 if half else a.shape[0], *a.shape[1:])
    return pl.pallas_call(
        functools.partial(swap_kernel, half), out_shape=jax.ShapeDtypeStruct(shape, a.dtype), in_specs=[ANY], out_specs=ANY,
        scratch_shapes=[pltpu.SemaphoreType.DMA((2,))],
        compiler_params=pltpu.CompilerParams(collective_id=collective_id, has_side_effects=True), name="swap%d" % collective_id)(a)


H = 16
HD = 64
SEQ_LEN = 1024
epsilon = 1e-05
gelu_scale = 0.7978845608028654
F32 = jnp.float32
BF = jnp.bfloat16


def gelu_tanh(inputs):
    return 0.5 * inputs * (1.0 + jnp.tanh(gelu_scale * (inputs + 0.044715 * inputs * inputs * inputs)))


def norm_rows(values, gain_row, shift_row):
    center = values - jnp.mean(values, axis=-1, keepdims=True)
    spread = jnp.mean(center * center, axis=-1, keepdims=True)
    inverse = lax.rsqrt(spread + epsilon)
    normed = center * inverse
    return (normed * gain_row + shift_row, normed, inverse)


def norm_back(grad_rows, normed, inverse, gain_row):
    scaled = grad_rows * gain_row
    return inverse * (
        scaled
        - jnp.mean(scaled, axis=-1, keepdims=True)
        - normed * jnp.mean(scaled * normed, axis=-1, keepdims=True)
    )


def contract(left, right, l, r):
    return lax.dot_general(left, right, (((l,), (r,)), ((), ())), preferred_element_type=F32)


def head_slopes(heads_dev):
    head_order = (
        lax.axis_index("tensor") * heads_dev + jnp.arange(heads_dev, dtype=jnp.int32) + 1
    ).astype(F32)
    return 2.0 ** (-8.0 * head_order / H)


def block_scores(queries, keys_all, slopes, q_start):
    block_len = queries.shape[1]
    key_count = keys_all.shape[1]
    scores = jnp.einsum("sqhd,skhd->shqk", queries, keys_all, preferred_element_type=F32) * HD ** (-0.5)
    query_pos = q_start + jnp.arange(block_len, dtype=jnp.int32)
    key_pos = jnp.arange(key_count, dtype=jnp.int32)
    offsets = (key_pos[None, :] - query_pos[:, None]).astype(F32)
    scores = scores + slopes[:, None, None] * offsets
    return jnp.where(key_pos[None, :] <= query_pos[:, None], scores, -1e30)


def attend(queries, keys_all, values_all, slopes):
    block_len = min(512, SEQ_LEN)
    outputs = []
    log_sums = []
    for q_start in range(0, SEQ_LEN, block_len):
        q_end = q_start + block_len
        scores = block_scores(queries[:, q_start:q_end], keys_all[:, :q_end], slopes, q_start)
        row_peak = jnp.max(scores, axis=-1, keepdims=True)
        expweights = jnp.exp(scores - row_peak)
        row_total = jnp.sum(expweights, axis=-1, keepdims=True)
        attn_probs = (expweights / row_total).astype(BF)
        block_out = jnp.einsum("shqk,skhd->sqhd", attn_probs, values_all[:, :q_end], preferred_element_type=F32)
        outputs.append(block_out.astype(BF))
        log_sums.append((row_peak + jnp.log(row_total))[..., 0])
    return (jnp.concatenate(outputs, axis=1), jnp.concatenate(log_sums, axis=2))


def attend_back(queries, keys_all, values_all, grad_out, log_sums, slopes):
    block_len = min(512, SEQ_LEN)
    grad_keys = jnp.zeros(keys_all.shape, F32)
    grad_values = jnp.zeros(values_all.shape, F32)
    grad_queries = []
    for q_start in range(0, SEQ_LEN, block_len):
        q_end = q_start + block_len
        query_part = queries[:, q_start:q_end]
        grad_part = grad_out[:, q_start:q_end]
        scores = block_scores(query_part, keys_all[:, :q_end], slopes, q_start)
        attn_probs = jnp.exp(scores - log_sums[:, :, q_start:q_end, None])
        probs_low = attn_probs.astype(BF)
        grad_probs = jnp.einsum("sqhd,skhd->shqk", grad_part, values_all[:, :q_end], preferred_element_type=F32)
        row_inner = jnp.sum(grad_probs * attn_probs, axis=-1, keepdims=True)
        grad_scores = (attn_probs * (grad_probs - row_inner)).astype(BF)
        grad_queries.append(
            jnp.einsum("shqk,skhd->sqhd", grad_scores, keys_all[:, :q_end], preferred_element_type=F32) * HD ** (-0.5)
        )
        key_term = jnp.einsum("shqk,sqhd->skhd", grad_scores, query_part, preferred_element_type=F32) * HD ** (-0.5)
        grad_keys = grad_keys.at[:, :q_end].add(key_term)
        value_term = jnp.einsum("shqk,sqhd->skhd", probs_low, grad_part, preferred_element_type=F32)
        grad_values = grad_values.at[:, :q_end].add(value_term)
    return (jnp.concatenate(grad_queries, axis=1), grad_keys, grad_values)


def lane_rows(flat, rows):
    gap = rows * 128 - flat.shape[-1]
    return jnp.pad(flat, [(0, 0)] * (flat.ndim - 1) + [(0, gap)]).reshape(*flat.shape[:-1], rows, 128)


def on_device(layer_in, w_qkv, b_qv, w_proj, w_ff1, b_ff1, w_ff2, norm_gains, add_biases, cotangent):
    n = lax.axis_size("dp")
    t = lax.axis_index("tensor")
    two = (2,) * (n.bit_length() - 1)
    local = layer_in.shape[0]
    rows = 2 * local
    seqs = rows // SEQ_LEN
    width = w_qkv.shape[2]
    model = layer_in.shape[1]
    hidden_dev = w_ff1.shape[1]
    heads = b_qv.shape[1]
    part = norm_gains.shape[1]
    mine = lambda a: lax.dynamic_slice_in_dim(a, t * local, local, 0)

    gains_flat = jnp.concatenate([norm_gains, add_biases]).reshape(-1)
    small = jnp.concatenate([
        lane_rows(gains_flat, 2), lane_rows(b_ff1.astype(F32).reshape(-1), 1), lane_rows(b_qv.astype(F32).reshape(-1), 1),
        jnp.zeros((4, 128), F32)])
    qkv_w, proj_w, up_w, down_w, small_all, x_low, cot = gather_all(
        w_qkv, w_proj.T, w_ff1, w_ff2.T, small, layer_in, cotangent, n)
    qkv_w = qkv_w.reshape(3, model, width)
    proj_w = proj_w.reshape(model, width)
    up_w = up_w.reshape(model, hidden_dev)
    down_w = down_w.reshape(model, hidden_dev)
    small_all = small_all.reshape(2, n, 8, 128)
    vectors = small_all[:, :, :2].reshape(2, n, 256)[:, :, : 6 * part].reshape(2, n, 6, part)
    vectors = vectors.transpose(2, 1, 0, 3).reshape(6, model)
    gains, shifts = vectors[:2], vectors[2:]
    here = lax.dynamic_index_in_dim(small_all, t, 0, keepdims=False)
    up_bias = here[:, 2, : b_ff1.size].reshape(n, *b_ff1.shape).transpose(1, 0, 2).reshape(-1)
    qv_bias = here[:, 3, : b_qv.size].reshape(n, *b_qv.shape).transpose(1, 2, 0, 3).reshape(2, width)

    resid = x_low.astype(F32)
    act_one, normed_one, inverse_one = norm_rows(resid, gains[0], shifts[0])
    full_one = act_one.astype(BF)
    mixed = jnp.einsum("rd,cde->cre", full_one, qkv_w, preferred_element_type=F32)
    head_shape = (seqs, SEQ_LEN, heads, HD)
    queries = (mixed[0] + qv_bias[0]).astype(BF).reshape(head_shape)
    keys_all = mixed[1].astype(BF).reshape(head_shape)
    values_all = (mixed[2] + qv_bias[1]).astype(BF).reshape(head_shape)
    slopes = head_slopes(heads)
    attended, log_sums = attend(queries, keys_all, values_all, slopes)
    attn_flat = attended.reshape(rows, width)

    projected = contract(attn_flat, proj_w, 1, 1).astype(BF)
    middle = resid + (projected.astype(F32) + swap(projected, 2).astype(F32)) + shifts[1]
    act_two, normed_two, inverse_two = norm_rows(middle, gains[1], shifts[2])
    full_two = act_two.astype(BF)
    hidden_pre = contract(full_two, up_w, 1, 0) + up_bias
    hidden = gelu_tanh(hidden_pre).astype(BF)
    lowered = contract(hidden, down_w, 1, 1).astype(BF)
    layer_out = (mine(middle) + (mine(lowered).astype(F32) + swap(lowered, 3, True).astype(F32)) + shifts[3]).astype(BF)

    grad_hidden = contract(cot, down_w, 1, 0)
    grad_down = contract(cot, hidden, 0, 0).astype(BF)
    unused_value, gelu_pull = jax.vjp(gelu_tanh, hidden_pre)
    grad_pre = gelu_pull(grad_hidden)[0].astype(BF)
    grad_up_bias = jnp.sum(grad_pre, axis=0, dtype=F32)
    grad_up = contract(full_two, grad_pre, 0, 0).astype(BF)
    back_two = contract(grad_pre, up_w, 1, 1).astype(BF)
    grad_act_two = back_two.astype(F32) + swap(back_two, 4).astype(F32)
    grad_mid = cot.astype(F32) + norm_back(grad_act_two, normed_two, inverse_two, gains[1])
    full_mid = grad_mid.astype(BF)
    grad_attn = contract(full_mid, proj_w, 1, 0).astype(BF).reshape(head_shape)
    grad_proj = contract(full_mid, attn_flat, 0, 0).astype(BF)
    grad_q, grad_k, grad_v = attend_back(queries, keys_all, values_all, grad_attn, log_sums, slopes)
    grad_qkv = [p.reshape(rows, width).astype(BF) for p in (grad_q, grad_k, grad_v)]
    grad_qkv_w = jnp.stack([contract(full_one, p, 0, 0).astype(BF) for p in grad_qkv])
    grad_qv_bias = jnp.stack([jnp.sum(grad_qkv[i], axis=0, dtype=F32) for i in (0, 2)])
    back_one = sum(contract(p, qkv_w[i], 1, 1) for i, p in enumerate(grad_qkv)).astype(BF)
    grad_act_one = mine(back_one).astype(F32) + swap(back_one, 5, True).astype(F32)
    grad_in = mine(grad_mid) + norm_back(grad_act_one, mine(normed_one), mine(inverse_one), gains[0])

    two_rows, mid_rows, cot_rows = mine(grad_act_two), mine(grad_mid), cotangent.astype(F32)
    sums = jnp.stack([
        jnp.sum(grad_act_one * mine(normed_one), axis=0), jnp.sum(two_rows * mine(normed_two), axis=0),
        jnp.sum(grad_act_one, axis=0), jnp.sum(mid_rows, axis=0), jnp.sum(two_rows, axis=0), jnp.sum(cot_rows, axis=0)])
    sums = sums.reshape(6, n, 2, part).transpose(1, 2, 0, 3).reshape(n, 2, 6 * part)
    up_sums = grad_up_bias.reshape(b_ff1.shape[0], n, -1).transpose(1, 0, 2).reshape(n, -1)
    qv_sums = grad_qv_bias.reshape(2, heads, n, -1).transpose(2, 0, 1, 3).reshape(n, -1)
    packed = jnp.concatenate([
        lane_rows(sums, 2).reshape(n, 4, 128), lane_rows(up_sums, 1), lane_rows(qv_sums, 1), jnp.zeros((n, 2, 128), F32)], axis=1)
    blocks = lambda a, lead=(): a.reshape(*lead, *two, model // n, a.shape[-1])
    out_qkv, out_proj, out_up, out_down, own, pair = scatter_all(
        blocks(grad_qkv_w, (3,)), blocks(grad_proj), blocks(grad_up), blocks(grad_down), packed.reshape(*two, 8, 128), n)
    both = lax.dynamic_slice_in_dim(own + pair, 2 * t, 2, 0).reshape(-1)[: 6 * part].reshape(6, part)
    return (
        layer_out,
        grad_in,
        out_qkv,
        own[5, : b_qv.size].reshape(b_qv.shape),
        out_proj.T,
        out_up,
        own[4, : b_ff1.size].reshape(b_ff1.shape),
        out_down.T,
        both[:2],
        both[2:],
    )


def solution(mesh):
    rows, cols = P(("dp", "tensor"), None), P(None, ("dp", "tensor"))
    return jax.shard_map(
        on_device,
        mesh=mesh,
        in_specs=(rows, P(None, "dp", "tensor"), P(None, "tensor", "dp"), P("tensor", "dp"), P("dp", "tensor"),
                  P("tensor", "dp"), P("tensor", "dp"), cols, cols, rows),
        out_specs=(rows, rows, P(None, "dp", "tensor"), P(None, "tensor", "dp"), P("tensor", "dp"), P("dp", "tensor"),
                   P("tensor", "dp"), P("tensor", "dp"), cols, cols),
        check_vma=False,
    )
```

```python
import functools
import math
import jax
import jax.numpy as jnp
from jax import lax
from jax.experimental import pallas as pl
from jax.experimental.pallas import tpu as pltpu
from jax.sharding import PartitionSpec as P

MESH = pl.DeviceIdType.MESH
ANY = pl.BlockSpec(memory_space=pl.ANY)
VM = pl.BlockSpec(memory_space=pltpu.VMEM)


def bits_of(index, count):
    return [lax.rem(index // (1 << b), 2) for b in range(count)]


def partner_of(index, mine, b):
    return index + (1 - 2 * mine[b]) * (1 << b)


def halving_orders(count):
    return [[(start + i) % count for i in range(count)] for start in range(3)]


def enter(index, mine, count, other):
    barrier = pltpu.get_barrier_semaphore()
    for b in range(count):
        pl.semaphore_signal(barrier, inc=1, device_id={"dp": partner_of(index, mine, b)}, device_id_type=MESH)
    pl.semaphore_signal(barrier, inc=1, device_id={"tensor": other}, device_id_type=MESH)
    pl.semaphore_wait(barrier, count + 1)


def block_index(mine, held, count):
    return tuple(slice(None) if b in held else mine[b] for b in reversed(range(count)))

SEQ_LEN = 1024
HD = 64
H = 16
epsilon = 1e-05
gelu_scale = 0.7978845608028654
F32 = jnp.float32
BF = jnp.bfloat16
TILE = 512
QB = 256
GATHER_MODES = (0, 1, 0, 1, 0, 1, 0, 2)
GATHER_LOOK = 4


def dot_nn(a, b):
    return lax.dot_general(a, b, (((1,), (0,)), ((), ())), preferred_element_type=F32)


def dot_nt(a, b):
    return lax.dot_general(a, b, (((1,), (1,)), ((), ())), preferred_element_type=F32)


def dot_tn(a, b):
    return lax.dot_general(a, b, (((0,), (0,)), ((), ())), preferred_element_type=F32)


def span(i, size):
    return pl.ds(pl.multiple_of(i * size, size), size)


def rows_loop(total, size, body):
    def step(i, carry):
        body(i, span(i, size))
        return carry

    lax.fori_loop(0, total // size, step, 0)


def forward_kernel(count, chunks, times, refs_in, refs_out, scratch, slopes):
    (qkv, proj, up, down, small, x, cot) = refs_in
    (qkv_o, proj_o, up_o, down_o, vec_o, cot_o, a1_o, q_o, k_o, v_o, o_o, lse_o, x2_o, a2_o, u_o, gp_o, gdown_o) = refs_out
    (qkv_w, proj_w, up_w, down_w, vec, vland, x_f, cot_f, a1, q, k, v, vt, ot, o, lse, part, part_r, x2, a2, u, gp, gdown, pos,
     send, recv, vsend, vrecv, psend, precv, own_sem, out_sem) = scratch
    me = lax.axis_index("dp")
    t = lax.axis_index("tensor")
    other = 1 - t
    mine = bits_of(me, count)
    orders = [order[::-1] for order in halving_orders(count)]
    full = block_index(mine, (), count)
    tokens, model = x_f.shape
    width = q.shape[1]
    hidden = u.shape[1]
    heads = width // HD
    local_rows = x.shape[0]
    mesh_copy = functools.partial(pltpu.make_async_remote_copy, device_id_type=MESH)

    enter(me, mine, count, other)
    waits = []

    def vec_step(s):
        to = {"dp": partner_of(me, mine, s)} if s < count else {"tensor": other}
        return mesh_copy(small if s == 0 else vec.at[s], vland.at[s], vsend.at[s], vrecv.at[s], device_id=to)

    vec[0] = small[...]
    vec_copies = [vec_step(s) for s in range(count + 1)]
    vec_copies[0].start()

    mine_rows = pl.ds(t * local_rows, local_rows)
    pair_copies = [mesh_copy(src, dst.at[mine_rows], psend.at[i], precv.at[i], device_id={"tensor": other})
                   for i, (src, dst) in enumerate(((x, x_f), (cot, cot_f)))]
    for copy in pair_copies:
        copy.start()

    names = {"qkv": (qkv, qkv_w), "proj": (proj, proj_w), "up": (up, up_w), "down": (down, down_w)}

    def views(c):
        name, lead, lo, size = chunks[c]
        src, dst = names[name]
        if lead is not None:
            src, dst = src.at[lead], dst.at[lead]
        return src.at[:, pl.ds(lo, size)], dst, (slice(None), pl.ds(lo, size))

    def copy_of(c, s):
        order = orders[GATHER_MODES[c % len(GATHER_MODES)]]
        src, dst, tail = views(c)
        at = (*block_index(mine, order[:s], count), *tail)
        return mesh_copy(src if s == 0 else dst.at[at], dst.at[at], send.at[c * count + s], recv.at[c * count + s],
                         device_id={"dp": partner_of(me, mine, order[s])})

    owns = [pltpu.make_async_copy(src, dst.at[full], own_sem.at[i]) for i, (src, dst) in enumerate(
        [(qkv.at[c], qkv_w.at[c]) for c in range(3)] + [(proj, proj_w), (up, up_w), (down, down_w)])]
    owns += [pltpu.make_async_copy(src, dst.at[mine_rows], own_sem.at[6 + i]) for i, (src, dst) in enumerate(((x, x_f), (cot, cot_f)))]
    for copy in owns:
        copy.start()
    for copy in owns:
        copy.wait()

    steps = sorted(((c, s) for c in range(len(chunks)) for s in range(count)), key=lambda cs: (cs[0] + GATHER_LOOK * cs[1], cs[0]))
    span_key = len(chunks) + GATHER_LOOK * count
    pace = lambda c, s: times["lead"] + (c + GATHER_LOOK * s) / span_key * times["gather"]
    queue = [(pace(c, s), c, s) for c, s in steps]
    done = set()
    clock = [0.0]

    def settle(c):
        if c not in done:
            while any(item[1] == c for item in queue):
                run(queue.pop(0))
            copy_of(c, count - 1).wait_recv()
            done.add(c)
            clock[0] = max(clock[0], pace(c, count))

    def run(item):
        at, c, s = item
        if s > 0:
            copy_of(c, s - 1).wait_recv()
        copy_of(c, s).start()

    def due(now):
        batch = []
        while queue and queue[0][0] <= now:
            batch.append(queue.pop(0))
        return batch

    def advance(cost):
        clock[0] += cost
        for item in due(clock[0]):
            run(item)

    outs = []

    def emit(src, dst):
        copy = pltpu.make_async_copy(src, dst, out_sem.at[len(outs)])
        copy.start()
        outs.append(copy)

    advance(times["lead"])
    for s in range(count):
        vec_copies[s].wait_recv()
        vec[s + 1] = vec[s] + vland[s]
        vec_copies[s + 1].start()
        advance(2.0)
    for copy in pair_copies:
        copy.wait_recv()
    emit(cot_f, cot_o)
    vec_copies[count].wait_recv()
    vec[count + 1, 0:8] = vec[count, 0:8] + vland[count, 0:8]
    vec[count + 1, 8:16] = vec[count, 8:16]
    emit(vec.at[count + 1], vec_o)
    table = vec.at[count + 1]

    def normed(rows_value, gain, shift):
        center = rows_value - jnp.mean(rows_value, axis=-1, keepdims=True)
        spread = jnp.mean(center * center, axis=-1, keepdims=True)
        return (center * lax.rsqrt(spread + epsilon)) * gain + shift

    def norm_one(i, rows):
        a1[rows, :] = normed(x_f[rows, :].astype(F32), table[0:1, :], table[2:3, :]).astype(BF)

    rows_loop(tokens, 256, norm_one)
    emit(a1, a1_o)
    pos[...] = lax.broadcasted_iota(jnp.int32, pos.shape, 0).astype(F32)
    advance(times["norm"])

    for c, dst in ((1, k), (0, q), (2, v)):
        for i, chunk in enumerate(chunks):
            if chunk[0] == "qkv" and chunk[1] == c:
                settle(i)

        def mix(i, rows, c=c, dst=dst):
            value = dot_nn(a1[rows, :], qkv_w[c].reshape(model, width))
            if c == 0:
                value = (value + table[10:11, 0:width]).astype(BF).astype(F32) * HD ** (-0.5)
            if c == 2:
                value = value + table[10:11, width : 2 * width]
            dst[rows, :] = value.astype(BF)
            if c == 2:
                vt[:, rows] = value.T.astype(BF)

        rows_loop(tokens, TILE, mix)
        advance(times["mix"])
    for src, dst in ((q, q_o), (k, k_o), (v, v_o), (qkv_w, qkv_o)):
        emit(src, dst)

    blocks = tokens // QB
    lane_half = lax.broadcasted_iota(jnp.int32, (QB, 2 * HD), 1) // HD
    batches = []
    for h in range(heads):
        batches.append(due(clock[0]))
        clock[0] += times["head"]

    def head_step(h, carry):
        for j in range(heads):
            if batches[j]:

                @pl.when(h == j)
                def _():
                    for item in batches[j]:
                        run(item)

        cols = span(h // 2, 2 * HD)
        slope = slopes[h]
        head_rows = span(h, HD)
        for b in range(blocks):
            end = (b + 1) * QB
            query = jnp.where(lane_half == lax.rem(h, 2), q[b * QB : end, cols], jnp.zeros((QB, 2 * HD), BF))
            bias = pos[0:end, :] * slope
            bias = jnp.concatenate([bias] * (QB // bias.shape[1]), axis=1)
            scores = dot_nt(k[0:end, cols], query) + bias
            diag = scores[b * QB : end, :]
            keep = lax.broadcasted_iota(jnp.int32, (QB, QB), 0) <= lax.broadcasted_iota(jnp.int32, (QB, QB), 1)
            diag = jnp.where(keep, diag, -1e30)
            scores = diag if b == 0 else jnp.concatenate([scores[0 : b * QB, :], diag], axis=0)
            peak = jnp.max(scores, axis=0, keepdims=True)
            weights = jnp.exp(scores - peak)
            total = jnp.sum(weights, axis=0, keepdims=True)
            out = dot_nn(vt[head_rows, 0:end], weights.astype(BF))
            ot[head_rows, b * QB : end] = (out / total).astype(BF)
            lse[pl.ds(h, 1), b * QB : end] = peak + jnp.log(total)
        return carry

    lax.fori_loop(0, heads, head_step, 0)
    for i, chunk in enumerate(chunks):
        if chunk[0] == "proj":
            settle(i)

    def turn(i, rows):
        o[rows, :] = ot[:, rows].astype(F32).T.astype(BF)

    rows_loop(tokens, TILE, turn)
    emit(o, o_o)
    emit(lse, lse_o)
    emit(proj_w, proj_o)

    def project(i, rows):
        part[rows, :] = dot_nt(o[rows, :], proj_w[...].reshape(model, width)).astype(BF)

    half = tokens // 2
    part_copies = []
    for j in range(2):
        project(j, pl.ds(j * half, half))
        copy = mesh_copy(part.at[pl.ds(j * half, half)], part_r.at[pl.ds(j * half, half)], psend.at[2 + j], precv.at[2 + j],
                         device_id={"tensor": other})
        copy.start()
        part_copies.append(copy)
    advance(times["proj"])
    for j in range(2):
        part_copies[j].wait_recv()

        def norm_two(i, rows, j=j):
            rows = pl.ds(pl.multiple_of(j * half + i * 256, 256), 256)
            middle = x_f[rows, :].astype(F32) + (part[rows, :].astype(F32) + part_r[rows, :].astype(F32)) + table[3:4, :]
            x2[rows, :] = middle
            a2[rows, :] = normed(middle, table[1:2, :], table[4:5, :]).astype(BF)

        rows_loop(half, 256, norm_two)
        advance(times["norm"])
    emit(x2, x2_o)
    emit(a2, a2_o)

    for j in range(hidden // TILE):
        cols = slice(j * TILE, (j + 1) * TILE)
        for i, chunk in enumerate(chunks):
            if chunk[0] == "up" and j * TILE <= chunk[2] < (j + 1) * TILE:
                settle(i)

        row = 8 + j * TILE // model
        bias_at = j * TILE % model

        def expand(i, rows, cols=cols, row=row, bias_at=bias_at):
            pre = dot_nn(a2[rows, :], up_w[..., cols].reshape(model, TILE)) + table[row : row + 1, bias_at : bias_at + TILE]
            square = pre * pre
            bent = jnp.tanh(pre * (gelu_scale + (gelu_scale * 0.044715) * square))
            rise = 0.5 + 0.5 * bent
            u[rows, cols] = (pre * rise).astype(BF)
            slope = 0.5 * pre * (1.0 - bent * bent) * (gelu_scale + (3 * 0.044715 * gelu_scale) * square)
            gp[rows, cols] = (rise + slope).astype(BF)

        rows_loop(tokens, 256, expand)
        advance(times["up"])

        def sum_down(i, rows, cols=cols):
            gdown[rows, cols] = dot_tn(cot_f[:, rows], u[:, cols]).astype(BF)

        rows_loop(model, TILE, sum_down)
        advance(times["down"])
    for src, dst in ((u, u_o), (gp, gp_o), (up_w, up_o), (gdown, gdown_o)):
        emit(src, dst)
    for i in range(len(chunks)):
        settle(i)
    emit(down_w, down_o)
    for c in range(len(chunks)):
        for s in range(count):
            copy_of(c, s).wait_send()
    for copy in vec_copies + pair_copies + part_copies:
        copy.wait_send()
    for copy in outs:
        copy.wait()


TIMES = {"gather": 115.0, "lead": 3.0, "mix": 1.5, "head": 2.0, "proj": 2.5, "norm": 2.5, "up": 3.0, "down": 1.5}


def forward_all(slopes, qkv, proj, up, down, small, x, cot, n, width=256, times=TIMES):
    count = n.bit_length() - 1
    two = (2,) * count
    chunks = []
    for c in (1, 0, 2):
        chunks += [("qkv", c, lo, width) for lo in range(0, qkv.shape[2], width)]
    for name, a in (("proj", proj), ("up", up), ("down", down)):
        chunks += [(name, None, lo, width) for lo in range(0, a.shape[1], width)]
    tokens, model = 2 * x.shape[0], x.shape[1]
    inner, hidden = qkv.shape[2], up.shape[1]
    heads = inner // HD
    weights = [((3, *two, *qkv.shape[1:]), BF), ((*two, *proj.shape), BF), ((*two, *up.shape), BF), ((*two, *down.shape), BF)]
    shapes = weights + [((16, model), F32), ((tokens, model), BF), ((tokens, model), BF)] + [((tokens, inner), BF)] * 4
    shapes += [((heads, tokens), F32), ((tokens, model), F32), ((tokens, model), BF), ((tokens, hidden), BF), ((tokens, hidden), BF), ((model, hidden), BF)]
    vm = lambda s, d: pltpu.VMEM(s, d)
    scratch = [vm(*w) for w in weights]
    scratch += [vm((count + 2, 16, model), F32), vm((count + 1, 16, model), F32), vm((tokens, model), BF), vm((tokens, model), BF), vm((tokens, model), BF)]
    scratch += [vm((tokens, inner), BF)] * 3 + [vm((inner, tokens), BF)] * 2 + [vm((tokens, inner), BF), vm((heads, tokens), F32)]
    scratch += [vm((tokens, model), BF)] * 2 + [vm((tokens, model), F32), vm((tokens, model), BF), vm((tokens, hidden), BF), vm((tokens, hidden), BF), vm((model, hidden), BF)]
    scratch += [vm((tokens, 128), F32)]
    sems = lambda k: pltpu.SemaphoreType.DMA((k,))
    k = len(chunks) * count
    scratch += [sems(k), sems(k), sems(count + 1), sems(count + 1), sems(4), sems(4), sems(8), sems(len(shapes))]

    def body(slopes_ref, *refs):
        forward_kernel(count, chunks, times, refs[:7], refs[7 : 7 + len(shapes)], refs[7 + len(shapes) :], slopes_ref)

    return pl.pallas_call(
        body, out_shape=tuple(jax.ShapeDtypeStruct(*s) for s in shapes),
        in_specs=[pl.BlockSpec(memory_space=pltpu.SMEM)] + [VM] * 7, out_specs=[ANY] * len(shapes), scratch_shapes=scratch,
        compiler_params=pltpu.CompilerParams(collective_id=0, has_side_effects=True, vmem_limit_bytes=62 * 2**20), name="forward_all",
    )(slopes, qkv, proj, up, down, small, x, cot)

PATTERN = (0, 1, 0, 1, 0, 1, 0, 2)


def scatter_kernel(count, chunks, width, qkv, proj, up, down, small, qkv_o, proj_o, up_o, down_o, small_o, pair_o,
                   acc, sacc, load_sem, send, recv, pair_sem, *landing):
    land, sland = landing[:count], landing[count:]
    me = lax.axis_index("dp")
    t = lax.axis_index("tensor")
    other = 1 - t
    mine = bits_of(me, count)
    orders = halving_orders(count)
    enter(me, mine, count, other)

    def src_view(c):
        name, lead, lo, size = chunks[c]
        if name == "small":
            return small, (slice(None), slice(None))
        ref = {"qkv": qkv, "proj": proj, "up": up, "down": down}[name]
        if lead is not None:
            ref = ref.at[lead]
        return ref, (slice(None), pl.ds(lo, size))

    def order_of(c):
        return orders[0] if chunks[c][0] == "small" else orders[PATTERN[c % len(PATTERN)]]

    def bufs(c):
        if chunks[c][0] == "small":
            return sacc, sland
        return acc.at[c - 1], tuple(r.at[c - 1] for r in land)

    def pick(c, s, flip):
        order = order_of(c)
        out = []
        for b in reversed(range(count)):
            if s > 0 and b == order[0]:
                continue
            if b == order[s]:
                out.append(1 - mine[b] if flip else mine[b])
            elif b in order[:s]:
                out.append(mine[b])
            else:
                out.append(slice(None))
        return tuple(out)

    loads = []
    for c in range(len(chunks)):
        ref, tail = src_view(c)
        cp = pltpu.make_async_copy(ref.at[(*pick(c, 0, False), *tail)], bufs(c)[0], load_sem.at[c])
        loads.append(cp)
    sent = {}
    steps = sorted(((c, s) for c in range(len(chunks)) for s in range(count + 1)), key=lambda cs: (cs[0] + 2 * cs[1], cs[0]))
    for c, s in steps:
        name, lead, lo, size = chunks[c]
        a, l = bufs(c)
        if s > 0:
            sent[c, s - 1].wait_recv()
            if s == 1:
                loads[c].wait()
            r = l[s - 1]
            left = count - s
            if s < count:
                base = pick(c, s - 1, False) if s > 1 else (slice(None),) * (count - 1)

                def add(i, carry, base=base, a=a, r=r, left=left):
                    sub = [lax.rem(i // (1 << (left - 1 - j)), 2) for j in range(left)]
                    it = iter(sub)
                    at = tuple(next(it) if isinstance(b, slice) else b for b in base)
                    a[at] = (a[at].astype(jnp.float32) + r[tuple(sub)].astype(jnp.float32)).astype(a.dtype)
                    return carry

                lax.fori_loop(0, 1 << left, add, 0)
            else:
                at = pick(c, s - 1, False)
                total = a[at].astype(jnp.float32) + r[...].astype(jnp.float32)
                if name == "small":
                    small_o[...] = total
                else:
                    ref = {"qkv": qkv_o, "proj": proj_o, "up": up_o, "down": down_o}[name]
                    if lead is not None:
                        ref = ref.at[lead]
                    ref[:, lo : lo + size] = total
        if s < count:
            if s == 0:
                loads[c].start()
                ref, tail = src_view(c)
                src = ref.at[(*pick(c, 0, True), *tail)]
            else:
                src = a.at[pick(c, s, True)]
            cp = pltpu.make_async_remote_copy(src, l[s], send.at[c * count + s], recv.at[c * count + s],
                                              device_id={"dp": partner_of(me, mine, order_of(c)[s])}, device_id_type=MESH)
            cp.start()
            sent[c, s] = cp
    last = pltpu.make_async_remote_copy(small_o, pair_o, pair_sem.at[0], pair_sem.at[1], device_id={"tensor": other}, device_id_type=MESH)
    last.start()
    for cp in sent.values():
        cp.wait_send()
    last.wait()


def scatter_all(qkv, proj, up, down, small, n, width=512):
    count = n.bit_length() - 1
    two = (2,) * count
    rows = up.shape[-2]
    chunks = [("small", None, 0, 0)]
    for name, a in (("down", down), ("up", up), ("proj", proj)):
        chunks += [(name, None, lo, width) for lo in range(0, a.shape[-1], width)]
    for c in range(3):
        chunks += [("qkv", c, lo, width) for lo in range(0, qkv.shape[-1], width)]
    k = len(chunks)
    f = lambda *s: jax.ShapeDtypeStruct(s, jnp.float32)
    outs = (f(3, rows, qkv.shape[-1]), f(rows, proj.shape[-1]), f(rows, up.shape[-1]), f(rows, down.shape[-1]), f(8, 128), f(8, 128))
    landing = [pltpu.VMEM((k - 1, *two[: count - 1 - s], rows, width), jnp.bfloat16) for s in range(count)]
    landing += [pltpu.VMEM((*two[: count - 1 - s], 8, 128), jnp.float32) for s in range(count)]
    return pl.pallas_call(
        functools.partial(scatter_kernel, count, chunks, width), out_shape=outs,
        in_specs=[ANY] * 5, out_specs=[VM] * 6,
        scratch_shapes=[pltpu.VMEM((k - 1, *two[:-1], rows, width), jnp.bfloat16), pltpu.VMEM((*two[:-1], 8, 128), jnp.float32),
                        pltpu.SemaphoreType.DMA((k,)), pltpu.SemaphoreType.DMA((k * count,)), pltpu.SemaphoreType.DMA((k * count,)),
                        pltpu.SemaphoreType.DMA((2,)), *landing],
        compiler_params=pltpu.CompilerParams(collective_id=1, has_side_effects=True, vmem_limit_bytes=48 * 2**20), name="scatter_all",
    )(qkv, proj, up, down, small)

def swap_kernel(half, src, dst, sems):
    me = lax.axis_index("dp")
    other = 1 - lax.axis_index("tensor")
    barrier = pltpu.get_barrier_semaphore()
    pl.semaphore_signal(barrier, inc=1, device_id={"tensor": other}, device_id_type=MESH)
    pl.semaphore_wait(barrier, 1)
    if half:
        rows = dst.shape[0]
        src = src.at[pl.ds(other * rows, rows)]
    cp = pltpu.make_async_remote_copy(src, dst, sems.at[0], sems.at[1], device_id={"tensor": other}, device_id_type=MESH)
    cp.start()
    cp.wait()


def swap(a, collective_id, half=False):
    shape = (a.shape[0] // 2 if half else a.shape[0], *a.shape[1:])
    return pl.pallas_call(
        functools.partial(swap_kernel, half), out_shape=jax.ShapeDtypeStruct(shape, a.dtype), in_specs=[ANY], out_specs=ANY,
        scratch_shapes=[pltpu.SemaphoreType.DMA((2,))],
        compiler_params=pltpu.CompilerParams(collective_id=collective_id, has_side_effects=True), name="swap%d" % collective_id)(a)

def norm_rows(values, gain_row, shift_row):
    center = values - jnp.mean(values, axis=-1, keepdims=True)
    spread = jnp.mean(center * center, axis=-1, keepdims=True)
    inverse = lax.rsqrt(spread + epsilon)
    normed = center * inverse
    return (normed * gain_row + shift_row, normed, inverse)


def norm_back(grad_rows, normed, inverse, gain_row):
    scaled = grad_rows * gain_row
    return inverse * (
        scaled
        - jnp.mean(scaled, axis=-1, keepdims=True)
        - normed * jnp.mean(scaled * normed, axis=-1, keepdims=True)
    )


def contract(left, right, l, r):
    return lax.dot_general(left, right, (((l,), (r,)), ((), ())), preferred_element_type=F32)


def head_slopes(heads_dev):
    head_order = (
        lax.axis_index("tensor") * heads_dev + jnp.arange(heads_dev, dtype=jnp.int32) + 1
    ).astype(F32)
    return 2.0 ** (-8.0 * head_order / H)


def block_scores(queries, keys_all, slopes, q_start):
    block_len = queries.shape[1]
    key_count = keys_all.shape[1]
    scores = jnp.einsum("sqhd,skhd->shqk", queries, keys_all, preferred_element_type=F32)
    query_pos = q_start + jnp.arange(block_len, dtype=jnp.int32)
    key_pos = jnp.arange(key_count, dtype=jnp.int32)
    scores = scores + slopes[:, None, None] * key_pos.astype(F32)
    return jnp.where(key_pos[None, :] <= query_pos[:, None], scores, -1e30)


def attend_back(queries, keys_all, values_all, grad_out, log_sums, slopes):
    block_len = min(512, SEQ_LEN)
    grad_keys = jnp.zeros(keys_all.shape, F32)
    grad_values = jnp.zeros(values_all.shape, F32)
    grad_queries = []
    for q_start in range(0, SEQ_LEN, block_len):
        q_end = q_start + block_len
        query_part = queries[:, q_start:q_end]
        grad_part = grad_out[:, q_start:q_end]
        scores = block_scores(query_part, keys_all[:, :q_end], slopes, q_start)
        attn_probs = jnp.exp(scores - log_sums[:, :, q_start:q_end, None])
        probs_low = attn_probs.astype(BF)
        grad_probs = jnp.einsum("sqhd,skhd->shqk", grad_part, values_all[:, :q_end], preferred_element_type=F32)
        row_inner = jnp.sum(grad_probs * attn_probs, axis=-1, keepdims=True)
        grad_scores = (attn_probs * (grad_probs - row_inner)).astype(BF)
        grad_queries.append(
            jnp.einsum("shqk,skhd->sqhd", grad_scores, keys_all[:, :q_end], preferred_element_type=F32) * HD ** (-0.5)
        )
        key_term = jnp.einsum("shqk,sqhd->skhd", grad_scores, query_part, preferred_element_type=F32)
        grad_keys = grad_keys.at[:, :q_end].add(key_term)
        value_term = jnp.einsum("shqk,sqhd->skhd", probs_low, grad_part, preferred_element_type=F32)
        grad_values = grad_values.at[:, :q_end].add(value_term)
    return (jnp.concatenate(grad_queries, axis=1), grad_keys, grad_values)


def lane_rows(flat, rows):
    gap = rows * 128 - flat.shape[-1]
    return jnp.pad(flat, [(0, 0)] * (flat.ndim - 1) + [(0, gap)]).reshape(*flat.shape[:-1], rows, 128)


def on_device(layer_in, w_qkv, b_qv, w_proj, w_ff1, b_ff1, w_ff2, norm_gains, add_biases, cotangent):
    n = lax.axis_size("dp")
    t = lax.axis_index("tensor")
    two = (2,) * (n.bit_length() - 1)
    local = layer_in.shape[0]
    rows = 2 * local
    seqs = rows // SEQ_LEN
    width = w_qkv.shape[2]
    model = layer_in.shape[1]
    hidden_dev = w_ff1.shape[1]
    heads = b_qv.shape[1]
    part = norm_gains.shape[1]
    mine = lambda a: lax.dynamic_slice_in_dim(a, t * local, local, 0)

    i = lax.axis_index("dp")
    put = lambda shape, a, at: lax.dynamic_update_slice(jnp.zeros(shape, F32), a.astype(F32), at)
    zero = jnp.int32(0)
    small = jnp.concatenate([
        put((8, model), jnp.concatenate([norm_gains, add_biases]), (zero, (2 * i + t) * part)),
        put((b_ff1.shape[0], n * b_ff1.shape[1]), b_ff1, (zero, i * b_ff1.shape[1])).reshape(-1, model),
        put((*b_qv.shape[:2], n * b_qv.shape[2]), b_qv, (zero, zero, i * b_qv.shape[2])).reshape(-1, model),
        jnp.zeros((16 - 8 - (hidden_dev + 2 * width) // model, model), F32)])
    slopes = head_slopes(heads)
    (qkv_w, proj_w, up_w, down_w, vectors, cot, full_one, q, k, v, attn_flat, log_sums, middle, full_two, hidden, rise, grad_down) = forward_all(
        slopes, w_qkv, w_proj.T, w_ff1, w_ff2.T, small, layer_in, cotangent, n)
    qkv_w = qkv_w.reshape(3, model, width)
    proj_w = proj_w.reshape(model, width)
    up_w = up_w.reshape(model, hidden_dev)
    down_w = down_w.reshape(model, hidden_dev)
    gains, shifts = vectors[:2], vectors[2:6]
    head_shape = (seqs, SEQ_LEN, heads, HD)
    queries, keys_all, values_all = (a.reshape(head_shape) for a in (q, k, v))
    log_sums = log_sums[None]
    act_one, normed_one, inverse_one = norm_rows(layer_in.astype(F32), gains[0], shifts[0])
    act_two, normed_two, inverse_two = norm_rows(middle, gains[1], shifts[2])
    lowered = contract(hidden, down_w, 1, 1).astype(BF)
    layer_out = (mine(middle) + (mine(lowered).astype(F32) + swap(lowered, 3, True).astype(F32)) + shifts[3]).astype(BF)

    grad_hidden = contract(cot, down_w, 1, 0)
    grad_pre = (grad_hidden * rise.astype(F32)).astype(BF)
    grad_up_bias = jnp.sum(grad_pre, axis=0, dtype=F32)
    grad_up = contract(full_two, grad_pre, 0, 0).astype(BF)
    back_two = contract(grad_pre, up_w, 1, 1).astype(BF)
    grad_act_two = back_two.astype(F32) + swap(back_two, 4).astype(F32)
    grad_mid = cot.astype(F32) + norm_back(grad_act_two, normed_two, inverse_two, gains[1])
    full_mid = grad_mid.astype(BF)
    grad_attn = contract(full_mid, proj_w, 1, 0).astype(BF).reshape(head_shape)
    grad_proj = contract(full_mid, attn_flat, 0, 0).astype(BF)
    grad_q, grad_k, grad_v = attend_back(queries, keys_all, values_all, grad_attn, log_sums, slopes)
    grad_qkv = [p.reshape(rows, width).astype(BF) for p in (grad_q, grad_k, grad_v)]
    grad_qkv_w = jnp.stack([contract(full_one, p, 0, 0).astype(BF) for p in grad_qkv])
    grad_qv_bias = jnp.stack([jnp.sum(grad_qkv[i], axis=0, dtype=F32) for i in (0, 2)])
    back_one = sum(contract(p, qkv_w[i], 1, 1) for i, p in enumerate(grad_qkv)).astype(BF)
    grad_act_one = mine(back_one).astype(F32) + swap(back_one, 5, True).astype(F32)
    grad_in = mine(grad_mid) + norm_back(grad_act_one, normed_one, inverse_one, gains[0])

    two_rows, mid_rows, cot_rows = mine(grad_act_two), mine(grad_mid), cotangent.astype(F32)
    sums = jnp.stack([
        jnp.sum(grad_act_one * normed_one, axis=0), jnp.sum(two_rows * mine(normed_two), axis=0),
        jnp.sum(grad_act_one, axis=0), jnp.sum(mid_rows, axis=0), jnp.sum(two_rows, axis=0), jnp.sum(cot_rows, axis=0)])
    sums = sums.reshape(6, n, 2, part).transpose(1, 2, 0, 3).reshape(n, 2, 6 * part)
    up_sums = grad_up_bias.reshape(b_ff1.shape[0], n, -1).transpose(1, 0, 2).reshape(n, -1)
    qv_sums = grad_qv_bias.reshape(2, heads, n, -1).transpose(2, 0, 1, 3).reshape(n, -1)
    packed = jnp.concatenate([
        lane_rows(sums, 2).reshape(n, 4, 128), lane_rows(up_sums, 1), lane_rows(qv_sums, 1), jnp.zeros((n, 2, 128), F32)], axis=1)
    blocks = lambda a, lead=(): a.reshape(*lead, *two, model // n, a.shape[-1])
    out_qkv, out_proj, out_up, out_down, own, pair = scatter_all(
        blocks(grad_qkv_w, (3,)), blocks(grad_proj), blocks(grad_up), blocks(grad_down), packed.reshape(*two, 8, 128), n)
    both = lax.dynamic_slice_in_dim(own + pair, 2 * t, 2, 0).reshape(-1)[: 6 * part].reshape(6, part)
    return (
        layer_out,
        grad_in,
        out_qkv,
        own[5, : b_qv.size].reshape(b_qv.shape),
        out_proj.T,
        out_up,
        own[4, : b_ff1.size].reshape(b_ff1.shape),
        out_down.T,
        both[:2],
        both[2:],
    )


def solution(mesh):
    rows, cols = P(("dp", "tensor"), None), P(None, ("dp", "tensor"))
    return jax.shard_map(
        on_device,
        mesh=mesh,
        in_specs=(rows, P(None, "dp", "tensor"), P(None, "tensor", "dp"), P("tensor", "dp"), P("dp", "tensor"),
                  P("tensor", "dp"), P("tensor", "dp"), cols, cols, rows),
        out_specs=(rows, rows, P(None, "dp", "tensor"), P(None, "tensor", "dp"), P("tensor", "dp"), P("dp", "tensor"),
                   P("tensor", "dp"), P("tensor", "dp"), cols, cols),
        check_vma=False,
    )
```

```python
import functools
import math
import jax
import jax.numpy as jnp
from jax import lax
from jax.experimental import pallas as pl
from jax.experimental.pallas import tpu as pltpu
from jax.sharding import PartitionSpec as P

MESH = pl.DeviceIdType.MESH
ANY = pl.BlockSpec(memory_space=pl.ANY)
VM = pl.BlockSpec(memory_space=pltpu.VMEM)


def bits_of(index, count):
    return [lax.rem(index // (1 << b), 2) for b in range(count)]


def partner_of(index, mine, b):
    return index + (1 - 2 * mine[b]) * (1 << b)


def halving_orders(count):
    return [[(start + i) % count for i in range(count)] for start in range(3)]


def enter(index, mine, count, other):
    barrier = pltpu.get_barrier_semaphore()
    for b in range(count):
        pl.semaphore_signal(barrier, inc=1, device_id={"dp": partner_of(index, mine, b)}, device_id_type=MESH)
    pl.semaphore_signal(barrier, inc=1, device_id={"tensor": other}, device_id_type=MESH)
    pl.semaphore_wait(barrier, count + 1)


def block_index(mine, held, count):
    return tuple(slice(None) if b in held else mine[b] for b in reversed(range(count)))

SEQ_LEN = 1024
HD = 64
H = 16
epsilon = 1e-05
gelu_scale = 0.7978845608028654
F32 = jnp.float32
BF = jnp.bfloat16
TILE = 512
QB = 256
GATHER_MODES = (0, 1, 0, 1, 0, 1, 0, 2)
GATHER_LOOK = 4


def dot_nn(a, b):
    return lax.dot_general(a, b, (((1,), (0,)), ((), ())), preferred_element_type=F32)


def dot_nt(a, b):
    return lax.dot_general(a, b, (((1,), (1,)), ((), ())), preferred_element_type=F32)


def dot_tn(a, b):
    return lax.dot_general(a, b, (((0,), (0,)), ((), ())), preferred_element_type=F32)


def span(i, size):
    return pl.ds(pl.multiple_of(i * size, size), size)


def rows_loop(total, size, body):
    def step(i, carry):
        body(i, span(i, size))
        return carry

    lax.fori_loop(0, total // size, step, 0)


def forward_kernel(count, chunks, times, refs_in, refs_out, scratch, slopes):
    (qkv, proj, up, down, small, x, cot) = refs_in
    (qkv_o, proj_o, up_o, down_o, vec_o, cot_o, a1_o, q_o, k_o, v_o, o_o, lse_o, x2_o, a2_o, u_o, gp_o, gdown_o) = refs_out
    (qkv_w, proj_w, up_w, down_w, vec, vland, x_f, cot_f, a1, q, k, v, vt, ot, o, lse, part, part_r, x2, a2, u, gp, gdown, pos,
     send, recv, vsend, vrecv, psend, precv, own_sem, out_sem) = scratch
    me = lax.axis_index("dp")
    t = lax.axis_index("tensor")
    other = 1 - t
    mine = bits_of(me, count)
    orders = [order[::-1] for order in halving_orders(count)]
    full = block_index(mine, (), count)
    tokens, model = x_f.shape
    width = q.shape[1]
    hidden = u.shape[1]
    heads = width // HD
    local_rows = x.shape[0]
    mesh_copy = functools.partial(pltpu.make_async_remote_copy, device_id_type=MESH)

    enter(me, mine, count, other)
    waits = []

    def vec_step(s):
        to = {"dp": partner_of(me, mine, s)} if s < count else {"tensor": other}
        return mesh_copy(small if s == 0 else vec.at[s], vland.at[s], vsend.at[s], vrecv.at[s], device_id=to)

    vec[0] = small[...]
    vec_copies = [vec_step(s) for s in range(count + 1)]
    vec_copies[0].start()

    mine_rows = pl.ds(t * local_rows, local_rows)
    pair_copies = [mesh_copy(src, dst.at[mine_rows], psend.at[i], precv.at[i], device_id={"tensor": other})
                   for i, (src, dst) in enumerate(((x, x_f), (cot, cot_f)))]
    for copy in pair_copies:
        copy.start()

    names = {"qkv": (qkv, qkv_w), "proj": (proj, proj_w), "up": (up, up_w), "down": (down, down_w)}

    def views(c):
        name, lead, lo, size = chunks[c]
        src, dst = names[name]
        if lead is not None:
            src, dst = src.at[lead], dst.at[lead]
        return src.at[:, pl.ds(lo, size)], dst, (slice(None), pl.ds(lo, size))

    def copy_of(c, s):
        order = orders[GATHER_MODES[c % len(GATHER_MODES)]]
        src, dst, tail = views(c)
        at = (*block_index(mine, order[:s], count), *tail)
        return mesh_copy(src if s == 0 else dst.at[at], dst.at[at], send.at[c * count + s], recv.at[c * count + s],
                         device_id={"dp": partner_of(me, mine, order[s])})

    owns = [pltpu.make_async_copy(src, dst.at[full], own_sem.at[i]) for i, (src, dst) in enumerate(
        [(qkv.at[c], qkv_w.at[c]) for c in range(3)] + [(proj, proj_w), (up, up_w), (down, down_w)])]
    owns += [pltpu.make_async_copy(src, dst.at[mine_rows], own_sem.at[6 + i]) for i, (src, dst) in enumerate(((x, x_f), (cot, cot_f)))]
    for copy in owns:
        copy.start()
    for copy in owns:
        copy.wait()

    steps = sorted(((c, s) for c in range(len(chunks)) for s in range(count)), key=lambda cs: (cs[0] + GATHER_LOOK * cs[1], cs[0]))
    span_key = len(chunks) + GATHER_LOOK * count
    pace = lambda c, s: times["lead"] + (c + GATHER_LOOK * s) / span_key * times["gather"]
    queue = [(pace(c, s), c, s) for c, s in steps]
    done = set()
    clock = [0.0]

    def settle(c):
        if c not in done:
            while any(item[1] == c for item in queue):
                run(queue.pop(0))
            copy_of(c, count - 1).wait_recv()
            done.add(c)
            clock[0] = max(clock[0], pace(c, count))

    def run(item):
        at, c, s = item
        if s > 0:
            copy_of(c, s - 1).wait_recv()
        copy_of(c, s).start()

    def due(now):
        batch = []
        while queue and queue[0][0] <= now:
            batch.append(queue.pop(0))
        return batch

    def advance(cost):
        clock[0] += cost
        for item in due(clock[0]):
            run(item)

    outs = []

    def emit(src, dst):
        copy = pltpu.make_async_copy(src, dst, out_sem.at[len(outs)])
        copy.start()
        outs.append(copy)

    advance(times["lead"])
    for s in range(count):
        vec_copies[s].wait_recv()
        vec[s + 1] = vec[s] + vland[s]
        vec_copies[s + 1].start()
        advance(2.0)
    for copy in pair_copies:
        copy.wait_recv()
    emit(cot_f, cot_o)
    vec_copies[count].wait_recv()
    vec[count + 1, 0:8] = vec[count, 0:8] + vland[count, 0:8]
    vec[count + 1, 8:16] = vec[count, 8:16]
    emit(vec.at[count + 1], vec_o)
    table = vec.at[count + 1]

    def normed(rows_value, gain, shift):
        center = rows_value - jnp.mean(rows_value, axis=-1, keepdims=True)
        spread = jnp.mean(center * center, axis=-1, keepdims=True)
        return (center * lax.rsqrt(spread + epsilon)) * gain + shift

    def norm_one(i, rows):
        a1[rows, :] = normed(x_f[rows, :].astype(F32), table[0:1, :], table[2:3, :]).astype(BF)

    rows_loop(tokens, 256, norm_one)
    emit(a1, a1_o)
    pos[...] = lax.broadcasted_iota(jnp.int32, pos.shape, 0).astype(F32)
    advance(times["norm"])

    for c, dst in ((1, k), (0, q), (2, v)):
        for i, chunk in enumerate(chunks):
            if chunk[0] == "qkv" and chunk[1] == c:
                settle(i)

        def mix(i, rows, c=c, dst=dst):
            value = dot_nn(a1[rows, :], qkv_w[c].reshape(model, width))
            if c == 0:
                value = (value + table[10:11, 0:width]).astype(BF).astype(F32) * HD ** (-0.5)
            if c == 2:
                value = value + table[10:11, width : 2 * width]
            dst[rows, :] = value.astype(BF)
            if c == 2:
                vt[:, rows] = value.T.astype(BF)

        rows_loop(tokens, TILE, mix)
        advance(times["mix"])
    for src, dst in ((q, q_o), (k, k_o), (v, v_o), (qkv_w, qkv_o)):
        emit(src, dst)

    blocks = tokens // QB
    lane_half = lax.broadcasted_iota(jnp.int32, (QB, 2 * HD), 1) // HD
    batches = []
    for h in range(heads):
        batches.append(due(clock[0]))
        clock[0] += times["head"]

    def head_step(h, carry):
        for j in range(heads):
            if batches[j]:

                @pl.when(h == j)
                def _():
                    for item in batches[j]:
                        run(item)

        cols = span(h // 2, 2 * HD)
        slope = slopes[h]
        head_rows = span(h, HD)
        for b in range(blocks):
            end = (b + 1) * QB
            query = jnp.where(lane_half == lax.rem(h, 2), q[b * QB : end, cols], jnp.zeros((QB, 2 * HD), BF))
            bias = pos[0:end, :] * slope
            bias = jnp.concatenate([bias] * (QB // bias.shape[1]), axis=1)
            scores = dot_nt(k[0:end, cols], query) + bias
            diag = scores[b * QB : end, :]
            keep = lax.broadcasted_iota(jnp.int32, (QB, QB), 0) <= lax.broadcasted_iota(jnp.int32, (QB, QB), 1)
            diag = jnp.where(keep, diag, -1e30)
            scores = diag if b == 0 else jnp.concatenate([scores[0 : b * QB, :], diag], axis=0)
            peak = jnp.max(scores, axis=0, keepdims=True)
            weights = jnp.exp(scores - peak)
            total = jnp.sum(weights, axis=0, keepdims=True)
            out = dot_nn(vt[head_rows, 0:end], weights.astype(BF))
            ot[head_rows, b * QB : end] = (out / total).astype(BF)
            lse[pl.ds(h, 1), b * QB : end] = peak + jnp.log(total)
        return carry

    lax.fori_loop(0, heads, head_step, 0)
    for i, chunk in enumerate(chunks):
        if chunk[0] == "proj":
            settle(i)

    def turn(i, rows):
        o[rows, :] = ot[:, rows].astype(F32).T.astype(BF)

    rows_loop(tokens, TILE, turn)
    emit(o, o_o)
    emit(lse, lse_o)
    emit(proj_w, proj_o)

    def project(i, rows):
        part[rows, :] = dot_nt(o[rows, :], proj_w[...].reshape(model, width)).astype(BF)

    half = tokens // 2
    part_copies = []
    for j in range(2):
        project(j, pl.ds(j * half, half))
        copy = mesh_copy(part.at[pl.ds(j * half, half)], part_r.at[pl.ds(j * half, half)], psend.at[2 + j], precv.at[2 + j],
                         device_id={"tensor": other})
        copy.start()
        part_copies.append(copy)
    advance(times["proj"])
    for j in range(2):
        part_copies[j].wait_recv()

        def norm_two(i, rows, j=j):
            rows = pl.ds(pl.multiple_of(j * half + i * 256, 256), 256)
            middle = x_f[rows, :].astype(F32) + (part[rows, :].astype(F32) + part_r[rows, :].astype(F32)) + table[3:4, :]
            x2[rows, :] = middle
            a2[rows, :] = normed(middle, table[1:2, :], table[4:5, :]).astype(BF)

        rows_loop(half, 256, norm_two)
        advance(times["norm"])
    emit(x2, x2_o)
    emit(a2, a2_o)

    for j in range(hidden // TILE):
        cols = slice(j * TILE, (j + 1) * TILE)
        for i, chunk in enumerate(chunks):
            if chunk[0] == "up" and j * TILE <= chunk[2] < (j + 1) * TILE:
                settle(i)

        row = 8 + j * TILE // model
        bias_at = j * TILE % model

        def expand(i, rows, cols=cols, row=row, bias_at=bias_at):
            pre = dot_nn(a2[rows, :], up_w[..., cols].reshape(model, TILE)) + table[row : row + 1, bias_at : bias_at + TILE]
            square = pre * pre
            bent = jnp.tanh(pre * (gelu_scale + (gelu_scale * 0.044715) * square))
            rise = 0.5 + 0.5 * bent
            u[rows, cols] = (pre * rise).astype(BF)
            slope = 0.5 * pre * (1.0 - bent * bent) * (gelu_scale + (3 * 0.044715 * gelu_scale) * square)
            gp[rows, cols] = (rise + slope).astype(BF)

        rows_loop(tokens, 256, expand)
        advance(times["up"])

        def sum_down(i, rows, cols=cols):
            gdown[rows, cols] = dot_tn(cot_f[:, rows], u[:, cols]).astype(BF)

        rows_loop(model, TILE, sum_down)
        advance(times["down"])
    for src, dst in ((u, u_o), (gp, gp_o), (up_w, up_o), (gdown, gdown_o)):
        emit(src, dst)
    for i in range(len(chunks)):
        settle(i)
    emit(down_w, down_o)
    for c in range(len(chunks)):
        for s in range(count):
            copy_of(c, s).wait_send()
    for copy in vec_copies + pair_copies + part_copies:
        copy.wait_send()
    for copy in outs:
        copy.wait()


TIMES = {"gather": 115.0, "lead": 3.0, "mix": 1.5, "head": 2.0, "proj": 2.5, "norm": 2.5, "up": 3.0, "down": 1.5}


def forward_all(slopes, qkv, proj, up, down, small, x, cot, n, width=256, times=TIMES):
    count = n.bit_length() - 1
    two = (2,) * count
    chunks = []
    for c in (1, 0, 2):
        chunks += [("qkv", c, lo, width) for lo in range(0, qkv.shape[2], width)]
    for name, a in (("proj", proj), ("up", up), ("down", down)):
        chunks += [(name, None, lo, width) for lo in range(0, a.shape[1], width)]
    tokens, model = 2 * x.shape[0], x.shape[1]
    inner, hidden = qkv.shape[2], up.shape[1]
    heads = inner // HD
    weights = [((3, *two, *qkv.shape[1:]), BF), ((*two, *proj.shape), BF), ((*two, *up.shape), BF), ((*two, *down.shape), BF)]
    shapes = weights + [((16, model), F32), ((tokens, model), BF), ((tokens, model), BF)] + [((tokens, inner), BF)] * 4
    shapes += [((heads, tokens), F32), ((tokens, model), F32), ((tokens, model), BF), ((tokens, hidden), BF), ((tokens, hidden), BF), ((model, hidden), BF)]
    vm = lambda s, d: pltpu.VMEM(s, d)
    scratch = [vm(*w) for w in weights]
    scratch += [vm((count + 2, 16, model), F32), vm((count + 1, 16, model), F32), vm((tokens, model), BF), vm((tokens, model), BF), vm((tokens, model), BF)]
    scratch += [vm((tokens, inner), BF)] * 3 + [vm((inner, tokens), BF)] * 2 + [vm((tokens, inner), BF), vm((heads, tokens), F32)]
    scratch += [vm((tokens, model), BF)] * 2 + [vm((tokens, model), F32), vm((tokens, model), BF), vm((tokens, hidden), BF), vm((tokens, hidden), BF), vm((model, hidden), BF)]
    scratch += [vm((tokens, 128), F32)]
    sems = lambda k: pltpu.SemaphoreType.DMA((k,))
    k = len(chunks) * count
    scratch += [sems(k), sems(k), sems(count + 1), sems(count + 1), sems(4), sems(4), sems(8), sems(len(shapes))]

    def body(slopes_ref, *refs):
        forward_kernel(count, chunks, times, refs[:7], refs[7 : 7 + len(shapes)], refs[7 + len(shapes) :], slopes_ref)

    return pl.pallas_call(
        body, out_shape=tuple(jax.ShapeDtypeStruct(*s) for s in shapes),
        in_specs=[pl.BlockSpec(memory_space=pltpu.SMEM)] + [VM] * 7, out_specs=[ANY] * len(shapes), scratch_shapes=scratch,
        compiler_params=pltpu.CompilerParams(collective_id=0, has_side_effects=True, vmem_limit_bytes=62 * 2**20), name="forward_all",
    )(slopes, qkv, proj, up, down, small, x, cot)

SCATTER_MODES = (0, 1, 0, 1, 0, 1, 0, 2)


def backward_kernel(count, chunks, times, slopes, table, refs_in, refs_out, scratch):
    (x_h, cot_h, a1_h, q_h, k_h, v_h, o_h, lse_h, x2_h, a2_h, u_h, gp_h, gdown_h, qkv_h, proj_h, up_h, down_h) = refs_in
    (layer_o, grad_o, gqkv_o, gproj_o, gup_o, gdown_o, sums_o) = refs_out
    landing = scratch[:count]
    (sums, sland, x_f, cot, a1, lse, x2, gp, big, gdown, gproj, gqkv, wide, up_w, part, part_r, first_r, last_r,
     kt, dqt, acc_k, acc_v, pos, send, recv, vsend, vrecv, psend, precv, in_sem) = scratch[count:]
    me = lax.axis_index("dp")
    t = lax.axis_index("tensor")
    other = 1 - t
    mine = bits_of(me, count)
    orders = halving_orders(count)
    tokens, model = cot.shape
    width = q_h.shape[1]
    hidden = gp.shape[1]
    heads = width // HD
    local = tokens // 2
    q, k, v, o = (up_w.at[:, pl.ds(i * width, width)] for i in range(4))
    dq, dk, dv, do = q, k, v, o
    mesh_copy = functools.partial(pltpu.make_async_remote_copy, device_id_type=MESH)
    rows_of = lambda who, i, size: pl.ds(pl.multiple_of(who * local + i * size, size), size)

    enter(me, mine, count, other)
    loads = {}

    def load(name, src, dst):
        copy = pltpu.make_async_copy(src, dst, in_sem.at[len(loads)])
        copy.start()
        loads[name] = copy

    load("u", u_h, big)
    load("down", down_h, wide)
    load("gdown", gdown_h, gdown)
    load("cot", cot_h, cot)
    load("gp", gp_h, gp)
    load("x2", x2_h, x2)
    load("a2", a2_h, a1)
    load("up", up_h, up_w)
    load("lse", lse_h, lse)
    load("x", x_h, x_f)

    grads = {"qkv": gqkv, "proj": gproj, "up": big, "down": gdown}
    finals = {"qkv": gqkv_o, "proj": gproj_o, "up": gup_o, "down": gdown_o}
    size = chunks[0][3]

    def order_of(c):
        return orders[SCATTER_MODES[c % len(SCATTER_MODES)]]

    def held(c):
        name, lead, lo, _ = chunks[c]
        ref = grads[name]
        return ref if lead is None else ref.at[lead]

    def region(c, s, flip):
        order = order_of(c)
        at = []
        for b in reversed(range(count)):
            if b == order[s]:
                at.append(1 - mine[b] if flip else mine[b])
            else:
                at.append(mine[b] if b in order[:s] else slice(None))
        return tuple(at)

    def copy_of(c, s):
        name, lead, lo, _ = chunks[c]
        src = held(c)
        if name == "down" and s == 0:
            src = gdown_h
        at = (*region(c, s, True), slice(None), pl.ds(lo, size))
        return mesh_copy(src.at[at], landing[s].at[c], send.at[c * count + s], recv.at[c * count + s],
                         device_id={"dp": partner_of(me, mine, order_of(c)[s])})

    def run(item):
        at, c, s = item
        name, lead, lo, _ = chunks[c]
        copy_of(c, s - 1).wait_recv()
        got = landing[s - 1].at[c]
        keep = region(c, s - 1, False)
        cols = slice(lo, lo + size)
        ref = held(c)
        if s == count:
            total = ref[(*keep, slice(None), cols)].astype(F32) + got[...].astype(F32)
            out = finals[name]
            if lead is not None:
                out = out.at[lead]
            out[:, cols] = total
            return
        left = count - s

        def add(i, carry):
            sub = [lax.rem(i // (1 << (left - 1 - j)), 2) for j in range(left)]
            it = iter(sub)
            at = (*(next(it) if isinstance(b, slice) else b for b in keep), slice(None), cols)
            ref[at] = (ref[at].astype(F32) + got[tuple(sub)].astype(F32)).astype(BF)
            return carry

        lax.fori_loop(0, 1 << left, add, 0)
        copy_of(c, s).start()

    queue = []
    clock = [times["lead"]]
    slot = [0.0]
    each = times["scatter"] / len(chunks)

    def ready(names):
        for c, (name, lead, lo, _) in enumerate(chunks):
            if (name, lead, lo) in names:
                slot[0] = max(clock[0], slot[0] + each)
                copy_of(c, 0).start()
                queue.extend((slot[0] + s * times["step"], c, s) for s in range(1, count + 1))
        queue.sort()

    def due():
        batch = []
        while queue and queue[0][0] <= clock[0]:
            batch.append(queue.pop(0))
        return batch

    def advance(cost):
        clock[0] += cost
        for item in due():
            run(item)

    tiles = lambda name, total, lead=None, at=0: {(name, lead, lo) for lo in range(at, at + total, size)}
    ready(tiles("down", hidden))
    loads["gdown"].wait()
    sums[0] = jnp.zeros_like(sums[0])
    pos[...] = lax.broadcasted_iota(jnp.int32, pos.shape, 0).astype(F32)

    def whole(ref, h=None, cols=slice(None)):
        return ref[:, cols] if h is None else ref[h * (model // 2) : (h + 1) * (model // 2), cols]

    loads["u"].wait()
    loads["down"].wait()
    half = model // 2

    def lowered(who, h):
        return dot_nt(big[who].reshape(local, hidden), whole(wide, h))

    for h in range(2):
        part[0:local, h * half : (h + 1) * half] = lowered(other, h).astype(BF)
    first = mesh_copy(part.at[pl.ds(0, local)], first_r, psend.at[0], precv.at[0], device_id={"tensor": other})
    first.start()
    advance(times["half"])

    loads["cot"].wait()
    loads["gp"].wait()
    for j in range(hidden // TILE):
        cols = slice(j * TILE, (j + 1) * TILE)

        def grad_pre(i, rows, cols=cols):
            value = (dot_nn(cot[rows, :], whole(wide, cols=cols)) * gp[rows, cols].astype(F32)).astype(BF)
            gp[rows, cols] = value
            line = 8 + cols.start // model
            at = slice(cols.start % model, cols.start % model + TILE)
            sums[0, line : line + 1, at] += jnp.sum(value.astype(F32), axis=0, keepdims=True)

        rows_loop(tokens, 256, grad_pre)
        advance(times["quarter"])

    loads["x2"].wait()
    first.wait_recv()
    for h in range(2):
        cols = slice(h * half, (h + 1) * half)
        mid = x2[rows_of(t, 0, local), cols]
        layer_o[:, cols] = (mid + (lowered(t, h) + first_r[:, cols].astype(F32)) + table[5:6, cols]).astype(BF)
    advance(times["half"])
    load("qkv", qkv_h.at[0], wide.at[:, pl.ds(0, width)])
    load("qkv1", qkv_h.at[1], wide.at[:, pl.ds(width, width)])
    load("qkv2", qkv_h.at[2], wide.at[:, pl.ds(2 * width, width)])
    load("proj", proj_h, wide.at[:, pl.ds(3 * width, width)])

    loads["a2"].wait()
    loads["up"].wait()
    first.wait_send()
    part_copies = []
    for h in range(2):
        rows = pl.ds(h * local, local)
        for e in range(2):
            part[rows, e * half : (e + 1) * half] = dot_nt(gp[rows, :], whole(up_w, e)).astype(BF)
        copy = mesh_copy(part.at[rows], part_r.at[rows], psend.at[1 + h], precv.at[1 + h], device_id={"tensor": other})
        copy.start()
        part_copies.append(copy)
        advance(times["half"])
    for name, src, dst in (("q", q_h, q), ("k", k_h, k), ("v", v_h, v), ("o", o_h, o)):
        load(name, src, dst)
    for j in range(hidden // TILE):
        cols = slice(j * TILE, (j + 1) * TILE)
        for h in range(2):
            value = dot_tn(a1[:, h * half : (h + 1) * half], gp[:, cols]).astype(BF)
            big[(h, Ellipsis, cols)] = value.reshape(*big.shape[1:-1], TILE)
        ready(tiles("up", TILE, at=j * TILE))
        advance(times["quarter"])
    load("a1", a1_h, a1)

    def norm_parts(value):
        center = value - jnp.mean(value, axis=-1, keepdims=True)
        inverse = lax.rsqrt(jnp.mean(center * center, axis=-1, keepdims=True) + epsilon)
        return center * inverse, inverse

    def norm_back(grad, normed, inverse, gain):
        scaled = grad * gain
        return inverse * (scaled - jnp.mean(scaled, axis=-1, keepdims=True) - normed * jnp.mean(scaled * normed, axis=-1, keepdims=True))

    def add_sum(line, value):
        sums[0, line : line + 1, :] += jnp.sum(value, axis=0, keepdims=True)

    for copy in part_copies:
        copy.wait_recv()
    for who, count_it in ((t, True), (other, False)):

        def through(i, carry, who=who, count_it=count_it):
            rows = rows_of(who, i, 128)
            grad = part[rows, :].astype(F32) + part_r[rows, :].astype(F32)
            normed, inverse = norm_parts(x2[rows, :])
            outer = cot[rows, :].astype(F32)
            mid = outer + norm_back(grad, normed, inverse, table[1:2, :])
            x2[rows, :] = mid
            cot[rows, :] = mid.astype(BF)
            if count_it:
                add_sum(1, grad * normed)
                add_sum(3, mid)
                add_sum(4, grad)
                add_sum(5, outer)
            return carry

        lax.fori_loop(0, local // 128, through, 0)
        advance(times["norm"])
    gx2 = cot

    loads["proj"].wait()
    loads["o"].wait()
    proj_cols = slice(3 * width, 4 * width)
    for h in range(2):
        gproj[h] = dot_tn(gx2[:, h * half : (h + 1) * half], o[...]).astype(BF).reshape(gproj.shape[1:])
    ready(tiles("proj", width))
    advance(times["small"])

    def through_proj(i, rows):
        do[rows, :] = dot_nn(gx2[rows, :], whole(wide, cols=proj_cols)).astype(BF)

    rows_loop(tokens, TILE, through_proj)
    for name in ("q", "k", "v", "lse"):
        loads[name].wait()

    def turn_keys(i, rows):
        kt[:, rows] = k[rows, :].astype(F32).T.astype(BF)

    rows_loop(tokens, TILE, turn_keys)
    advance(times["small"])

    blocks = tokens // QB
    lane_half = lax.broadcasted_iota(jnp.int32, (QB, 2 * HD), 1) // HD
    batches = []
    for h in range(heads):
        batches.append(due())
        clock[0] += times["head"]

    def head_step(h, carry):
        for j in range(heads):
            if batches[j]:

                @pl.when(h == j)
                def _():
                    for item in batches[j]:
                        run(item)

        cols = span(h // 2, 2 * HD)
        head_rows = span(h, HD)
        side = lax.rem(h, 2)
        slope = slopes[h]

        @pl.when(side == 0)
        def _():
            acc_k[...] = jnp.zeros_like(acc_k)
            acc_v[...] = jnp.zeros_like(acc_v)

        for b in range(blocks):
            end = (b + 1) * QB
            rows = slice(b * QB, end)
            zero = jnp.zeros((QB, 2 * HD), BF)
            query = jnp.where(lane_half == side, q[rows, cols], zero)
            outer = jnp.where(lane_half == side, do[rows, cols], zero)
            bias = pos[0:end, :] * slope
            bias = jnp.concatenate([bias] * (QB // bias.shape[1]), axis=1)
            scores = dot_nt(k[0:end, cols], query) + bias - lse[pl.ds(h, 1), rows]
            keep = lax.broadcasted_iota(jnp.int32, (QB, QB), 0) <= lax.broadcasted_iota(jnp.int32, (QB, QB), 1)
            diag = jnp.where(keep, scores[b * QB : end, :], -1e30)
            scores = diag if b == 0 else jnp.concatenate([scores[0 : b * QB, :], diag], axis=0)
            probs = jnp.exp(scores)
            acc_v[0:end, :] += dot_nn(probs.astype(BF), outer)
            grad = dot_nt(v[0:end, cols], outer)
            inner = jnp.sum(probs * grad, axis=0, keepdims=True)
            low = (probs * (grad - inner)).astype(BF)
            acc_k[0:end, :] += dot_nn(low, query)
            dqt[head_rows, rows] = (dot_nn(kt[head_rows, 0:end], low) * HD ** (-0.5)).astype(BF)

        @pl.when(side == 1)
        def _():
            dk[:, cols] = acc_k[...].astype(BF)
            dv[:, cols] = acc_v[...].astype(BF)

        return carry

    lax.fori_loop(0, heads, head_step, 0)

    def turn(i, rows):
        dq[rows, :] = dqt[:, rows].astype(F32).T.astype(BF)

    rows_loop(tokens, TILE, turn)
    loads["a1"].wait()
    for c, ref in ((1, dk), (2, dv), (0, dq)):
        for h in range(2):
            gqkv[c, h] = dot_tn(a1[:, h * half : (h + 1) * half], ref[...]).astype(BF).reshape(gqkv.shape[2:])
        ready(tiles("qkv", width, lead=c))
        advance(times["small"])
    for at, ref in ((0, dq), (width, dv)):
        sums[0, 10:11, at : at + width] = jnp.sum(ref[...].astype(F32), axis=0, keepdims=True)

    for name in ("qkv", "qkv1", "qkv2"):
        loads[name].wait()

    def back_one(rows):
        total = dot_nt(dq[rows, :], whole(wide, cols=slice(0, width)))
        total += dot_nt(dk[rows, :], whole(wide, cols=slice(width, 2 * width)))
        return total + dot_nt(dv[rows, :], whole(wide, cols=slice(2 * width, 3 * width)))

    for copy in part_copies:
        copy.wait_send()

    def partner_rows(i, carry):
        part[span(i, 256), :] = back_one(rows_of(other, i, 256)).astype(BF)
        return carry

    lax.fori_loop(0, local // 256, partner_rows, 0)
    last = mesh_copy(part.at[pl.ds(0, local)], last_r, psend.at[3], precv.at[3], device_id={"tensor": other})
    last.start()
    advance(times["half"])
    loads["x"].wait()
    last.wait_recv()

    def own_rows(i, carry):
        rows = rows_of(t, i, 256)
        here = span(i, 256)
        grad = back_one(rows) + last_r[here, :].astype(F32)
        normed, inverse = norm_parts(x_f[here, :].astype(F32))
        grad_o[here, :] = x2[rows, :] + norm_back(grad, normed, inverse, table[0:1, :])
        add_sum(0, grad * normed)
        add_sum(2, grad)
        return carry

    lax.fori_loop(0, local // 256, own_rows, 0)
    advance(times["half"])

    def sum_step(s):
        to = {"dp": partner_of(me, mine, s)} if s < count else {"tensor": other}
        return mesh_copy(sums.at[s], sland.at[s], vsend.at[s], vrecv.at[s], device_id=to)

    sum_copies = [sum_step(s) for s in range(count + 1)]
    sum_copies[0].start()
    for s in range(count):
        advance(times["hop"])
        sum_copies[s].wait_recv()
        sums[s + 1] = sums[s] + sland[s]
        sum_copies[s + 1].start()
    while queue:
        run(queue.pop(0))
    sum_copies[count].wait_recv()
    sums_o[0:8, :] = sums[count, 0:8] + sland[count, 0:8]
    sums_o[8:16, :] = sums[count, 8:16]
    for c in range(len(chunks)):
        for s in range(count):
            copy_of(c, s).wait_send()
    for copy in sum_copies + [last]:
        copy.wait_send()


BACK_TIMES = {"scatter": 110.0, "step": 13.0, "lead": 3.0, "half": 3.0, "quarter": 1.7, "norm": 2.5, "small": 2.0, "head": 4.0, "hop": 2.5}


def backward_all(slopes, table, x, cot, a1, q, k, v, o, lse, x2, a2, u, gp, gdown, qkv_w, proj_w, up_w, down_w, n, width=256, times=BACK_TIMES):
    count = n.bit_length() - 1
    two = (2,) * count
    tokens, model = cot.shape
    inner, hidden = q.shape[1], gp.shape[1]
    heads = inner // HD
    r = model // n
    chunks = [("down", None, lo, width) for lo in range(0, hidden, width)]
    chunks += [("up", None, lo, width) for lo in range(0, hidden, width)]
    chunks += [("proj", None, lo, width) for lo in range(0, inner, width)]
    for c in (1, 2, 0):
        chunks += [("qkv", c, lo, width) for lo in range(0, inner, width)]
    f = lambda *s: jax.ShapeDtypeStruct(s, F32)
    outs = (jax.ShapeDtypeStruct(x.shape, BF), f(*x.shape), f(3, r, inner), f(r, inner), f(r, hidden), f(r, hidden), f(16, model))
    vm = lambda *s, d=BF: pltpu.VMEM(s, d)
    scratch = [vm(len(chunks), *two[: count - 1 - s], r, width) for s in range(count)]
    scratch += [vm(count + 1, 16, model, d=F32), vm(count + 1, 16, model, d=F32), vm(*x.shape), vm(tokens, model), vm(tokens, model)]
    scratch += [vm(heads, tokens, d=F32), vm(tokens, model, d=F32), vm(tokens, hidden)]
    scratch += [vm(*two, r, hidden), vm(*two, r, hidden), vm(*two, r, inner), vm(3, *two, r, inner), vm(model, hidden), vm(model, hidden)]
    scratch += [vm(tokens, model), vm(tokens, model), vm(*x.shape), vm(*x.shape), vm(inner, tokens), vm(inner, tokens)]
    scratch += [vm(tokens, 2 * HD, d=F32)] * 2 + [vm(tokens, 128, d=F32)]
    sems = lambda m: pltpu.SemaphoreType.DMA((m,))
    m = len(chunks) * count
    scratch += [sems(m), sems(m), sems(count + 1), sems(count + 1), sems(4), sems(4), sems(20)]
    flat = lambda a: a.reshape(*a.shape[: a.ndim - count - 2], model, a.shape[-1])
    by_block = lambda a: a.reshape(*two, r, a.shape[-1])

    def body(slopes_ref, table_ref, *refs):
        backward_kernel(count, chunks, times, slopes_ref, table_ref, refs[:17], refs[17 : 17 + len(outs)], refs[17 + len(outs) :])

    return pl.pallas_call(
        body, out_shape=outs, in_specs=[pl.BlockSpec(memory_space=pltpu.SMEM), VM] + [ANY] * 17, out_specs=[VM] * len(outs), scratch_shapes=scratch,
        compiler_params=pltpu.CompilerParams(collective_id=1, has_side_effects=True, vmem_limit_bytes=67043328), name="backward_all",
    )(slopes, table, x, cot, a1, q, k, v, o, lse, x2, a2, by_block(u), gp, by_block(gdown), flat(qkv_w), flat(proj_w), flat(up_w), flat(down_w))

def on_device(layer_in, w_qkv, b_qv, w_proj, w_ff1, b_ff1, w_ff2, norm_gains, add_biases, cotangent):
    n = lax.axis_size("dp")
    i = lax.axis_index("dp")
    t = lax.axis_index("tensor")
    width = w_qkv.shape[2]
    model = layer_in.shape[1]
    hidden = w_ff1.shape[1]
    heads = b_qv.shape[1]
    part = norm_gains.shape[1]
    zero = jnp.int32(0)
    put = lambda shape, a, at: lax.dynamic_update_slice(jnp.zeros(shape, F32), a.astype(F32), at)
    up_grid = (b_ff1.shape[0], n * b_ff1.shape[1])
    qv_grid = (*b_qv.shape[:2], n * b_qv.shape[2])
    small = jnp.concatenate([
        put((8, model), jnp.concatenate([norm_gains, add_biases]), (zero, (2 * i + t) * part)),
        put(up_grid, b_ff1, (zero, i * b_ff1.shape[1])).reshape(-1, model),
        put(qv_grid, b_qv, (zero, zero, i * b_qv.shape[2])).reshape(-1, model),
        jnp.zeros((8 - (hidden + 2 * width) // model, model), F32)])
    slopes = 2.0 ** (-8.0 * (t * heads + jnp.arange(heads, dtype=jnp.int32) + 1).astype(F32) / H)
    (qkv_w, proj_w, up_w, down_w, vectors, cot, a1, q, k, v, o, lse, x2, a2, u, rise, grad_down) = forward_all(
        slopes, w_qkv, w_proj.T, w_ff1, w_ff2.T, small, layer_in, cotangent, n)
    layer_out, grad_in, out_qkv, out_proj, out_up, out_down, sums = backward_all(
        slopes, vectors, layer_in, cot, a1, q, k, v, o, lse, x2, a2, u, rise, grad_down, qkv_w, proj_w, up_w, down_w, n)
    own = lax.dynamic_slice(sums, (zero, (2 * i + t) * part), (6, part))
    up_sums = lax.dynamic_slice_in_dim(sums[8 : 8 + hidden // model].reshape(up_grid), i * b_ff1.shape[1], b_ff1.shape[1], 1)
    qv_sums = lax.dynamic_slice_in_dim(sums[10].reshape(qv_grid), i * b_qv.shape[2], b_qv.shape[2], 2)
    return (layer_out, grad_in, out_qkv, qv_sums, out_proj.T, out_up, up_sums, out_down.T, own[:2], own[2:])


def solution(mesh):
    rows, cols = P(("dp", "tensor"), None), P(None, ("dp", "tensor"))
    return jax.shard_map(
        on_device,
        mesh=mesh,
        in_specs=(rows, P(None, "dp", "tensor"), P(None, "tensor", "dp"), P("tensor", "dp"), P("dp", "tensor"),
                  P("tensor", "dp"), P("tensor", "dp"), cols, cols, rows),
        out_specs=(rows, rows, P(None, "dp", "tensor"), P(None, "tensor", "dp"), P("tensor", "dp"), P("dp", "tensor"),
                   P("tensor", "dp"), P("tensor", "dp"), cols, cols),
        check_vma=False,
    )
```

```python
import functools
import math
import jax
import jax.numpy as jnp
from jax import lax
from jax.experimental import pallas as pl
from jax.experimental.pallas import tpu as pltpu
from jax.sharding import PartitionSpec as P

MESH = pl.DeviceIdType.MESH
ANY = pl.BlockSpec(memory_space=pl.ANY)
VM = pl.BlockSpec(memory_space=pltpu.VMEM)


def bits_of(index, count):
    return [lax.rem(index // (1 << b), 2) for b in range(count)]


def partner_of(index, mine, b):
    return index + (1 - 2 * mine[b]) * (1 << b)


def halving_orders(count):
    return [[(start + i) % count for i in range(count)] for start in range(3)]


def enter(index, mine, count, other):
    barrier = pltpu.get_barrier_semaphore()
    for b in range(count):
        pl.semaphore_signal(barrier, inc=1, device_id={"dp": partner_of(index, mine, b)}, device_id_type=MESH)
    pl.semaphore_signal(barrier, inc=1, device_id={"tensor": other}, device_id_type=MESH)
    pl.semaphore_wait(barrier, count + 1)


def block_index(mine, held, count):
    return tuple(slice(None) if b in held else mine[b] for b in reversed(range(count)))

SEQ_LEN = 1024
HD = 64
H = 16
epsilon = 1e-05
gelu_scale = 0.7978845608028654
F32 = jnp.float32
BF = jnp.bfloat16
TILE = 512
QB = 256
LOOK = 4


def bit_orders(count, modes, total, flip):
    if modes and count == 4:
        return [[mode // 10**i % 10 for i in (3, 2, 1, 0)] for mode in modes]
    cyclic = [[(start + i) % count for i in range(count)] for start in (0, 1, 0, 1, 0, 1, 0, 2)]
    return [(order[::-1] if flip else order) for order in (cyclic[c % len(cyclic)] for c in range(total))]


def dot_nn(a, b):
    return lax.dot_general(a, b, (((1,), (0,)), ((), ())), preferred_element_type=F32)


def dot_nt(a, b):
    return lax.dot_general(a, b, (((1,), (1,)), ((), ())), preferred_element_type=F32)


def dot_tn(a, b):
    return lax.dot_general(a, b, (((0,), (0,)), ((), ())), preferred_element_type=F32)


def span(i, size):
    return pl.ds(pl.multiple_of(i * size, size), size)


def paced_loop(steps, body, batches, run):
    def step(i, carry):
        for j in range(steps):
            if batches[j]:

                @pl.when(i == j)
                def _():
                    for item in batches[j]:
                        run(item)

        body(i)
        return carry

    lax.fori_loop(0, steps, step, 0)


def rows_loop(total, size, body):
    def step(i, carry):
        body(i, span(i, size))
        return carry

    lax.fori_loop(0, total // size, step, 0)


def forward_kernel(count, chunks, modes, order, plan, refs_in, refs_out, scratch, slopes):
    (qkv, proj, up, down, small, x, cot) = refs_in
    (qkv_o, proj_o, up_o, down_o, vec_o, cot_o, a1_o, q_o, k_o, v_o, o_o, lse_o, x2_o, a2_o, u_o, gp_o, gdown_o) = refs_out
    (qkv_w, proj_w, up_w, down_w, vec, vland, x_f, cot_f, a1, q, k, v, vt, ot, o, lse, part, part_r, x2, a2, u, gp, gdown, pos,
     send, recv, vsend, vrecv, psend, precv, own_sem, out_sem) = scratch
    me = lax.axis_index("dp")
    t = lax.axis_index("tensor")
    other = 1 - t
    mine = bits_of(me, count)
    orders = bit_orders(count, modes, len(chunks), True)
    full = block_index(mine, (), count)
    tokens, model = x_f.shape
    width = q.shape[1]
    hidden = u.shape[1]
    heads = width // HD
    local_rows = x.shape[0]
    mesh_copy = functools.partial(pltpu.make_async_remote_copy, device_id_type=MESH)

    enter(me, mine, count, other)
    waits = []

    def vec_step(s):
        to = {"dp": partner_of(me, mine, s)} if s < count else {"tensor": other}
        return mesh_copy(small if s == 0 else vec.at[s], vland.at[s], vsend.at[s], vrecv.at[s], device_id=to)

    vec[0] = small[...]
    vec_copies = [vec_step(s) for s in range(count + 1)]
    vec_copies[0].start()

    mine_rows = pl.ds(t * local_rows, local_rows)
    pair_copies = [mesh_copy(src, dst.at[mine_rows], psend.at[i], precv.at[i], device_id={"tensor": other})
                   for i, (src, dst) in enumerate(((x, x_f), (cot, cot_f)))]
    for copy in pair_copies:
        copy.start()

    names = {"qkv": (qkv, qkv_w), "proj": (proj, proj_w), "up": (up, up_w), "down": (down, down_w)}

    def views(c):
        name, lead, lo, size = chunks[c]
        src, dst = names[name]
        if lead is not None:
            src, dst = src.at[lead], dst.at[lead]
        return src.at[:, pl.ds(lo, size)], dst, (slice(None), pl.ds(lo, size))

    def copy_of(c, s):
        order = orders[c]
        src, dst, tail = views(c)
        at = (*block_index(mine, order[:s], count), *tail)
        return mesh_copy(src if s == 0 else dst.at[at], dst.at[at], send.at[c * count + s], recv.at[c * count + s],
                         device_id={"dp": partner_of(me, mine, order[s])})

    owns = [pltpu.make_async_copy(src, dst.at[full], own_sem.at[i]) for i, (src, dst) in enumerate(
        [(qkv.at[c], qkv_w.at[c]) for c in range(3)] + [(proj, proj_w), (up, up_w), (down, down_w)])]
    owns += [pltpu.make_async_copy(src, dst.at[mine_rows], own_sem.at[6 + i]) for i, (src, dst) in enumerate(((x, x_f), (cot, cot_f)))]
    for copy in owns:
        copy.start()
    for copy in owns:
        copy.wait()

    queue = [divmod(code, count) for code in order] if order and count == 4 else sorted(
        ((c, s) for c in range(len(chunks)) for s in range(count)), key=lambda cs: (cs[0] + LOOK * cs[1], cs[0]))
    share = list(plan) if plan and count == 4 else []
    done = set()

    def run(item):
        c, s = item
        if s > 0:
            copy_of(c, s - 1).wait_recv()
        copy_of(c, s).start()

    def settle(c):
        if c not in done:
            while any(item[0] == c for item in queue):
                run(queue.pop(0))
            copy_of(c, count - 1).wait_recv()
            done.add(c)

    def due():
        size = share.pop(0) if share else 2
        batch, queue[:] = queue[:size], queue[size:]
        return batch

    def advance():
        for item in due():
            run(item)

    def paced(steps, body):
        paced_loop(steps, body, [due() for _ in range(steps)], run)

    outs = []

    def emit(src, dst):
        copy = pltpu.make_async_copy(src, dst, out_sem.at[len(outs)])
        copy.start()
        outs.append(copy)

    advance()
    for s in range(count):
        vec_copies[s].wait_recv()
        vec[s + 1] = vec[s] + vland[s]
        vec_copies[s + 1].start()
        advance()
    for copy in pair_copies:
        copy.wait_recv()
    emit(cot_f, cot_o)
    vec_copies[count].wait_recv()
    vec[count + 1, 0:8] = vec[count, 0:8] + vland[count, 0:8]
    vec[count + 1, 8:16] = vec[count, 8:16]
    emit(vec.at[count + 1], vec_o)
    table = vec.at[count + 1]

    def normed(rows_value, gain, shift):
        center = rows_value - jnp.mean(rows_value, axis=-1, keepdims=True)
        spread = jnp.mean(center * center, axis=-1, keepdims=True)
        return (center * lax.rsqrt(spread + epsilon)) * gain + shift

    def norm_one(i, rows):
        a1[rows, :] = normed(x_f[rows, :].astype(F32), table[0:1, :], table[2:3, :]).astype(BF)

    pos[...] = lax.broadcasted_iota(jnp.int32, pos.shape, 0).astype(F32)
    paced(4, lambda i: norm_one(i, span(i, tokens // 4)))
    emit(a1, a1_o)

    for c, dst in ((1, k), (0, q), (2, v)):
        for i, chunk in enumerate(chunks):
            if chunk[0] == "qkv" and chunk[1] == c:
                settle(i)

        def mix(i, rows, c=c, dst=dst):
            value = dot_nn(a1[rows, :], qkv_w[c].reshape(model, width))
            if c == 0:
                value = (value + table[10:11, 0:width]).astype(BF).astype(F32) * HD ** (-0.5)
            if c == 2:
                value = value + table[10:11, width : 2 * width]
            dst[rows, :] = value.astype(BF)
            if c == 2:
                vt[:, rows] = value.T.astype(BF)

        paced(2, lambda i: mix(i, span(i, tokens // 2)))
    for src, dst in ((q, q_o), (k, k_o), (v, v_o), (qkv_w, qkv_o)):
        emit(src, dst)

    blocks = tokens // QB
    lane_half = lax.broadcasted_iota(jnp.int32, (QB, 2 * HD), 1) // HD

    def head_step(h):
        cols = span(h // 2, 2 * HD)
        slope = slopes[h]
        head_rows = span(h, HD)
        for b in range(blocks):
            end = (b + 1) * QB
            query = jnp.where(lane_half == lax.rem(h, 2), q[b * QB : end, cols], jnp.zeros((QB, 2 * HD), BF))
            bias = pos[0:end, :] * slope
            bias = jnp.concatenate([bias] * (QB // bias.shape[1]), axis=1)
            scores = dot_nt(k[0:end, cols], query) + bias
            diag = scores[b * QB : end, :]
            keep = lax.broadcasted_iota(jnp.int32, (QB, QB), 0) <= lax.broadcasted_iota(jnp.int32, (QB, QB), 1)
            diag = jnp.where(keep, diag, -1e30)
            scores = diag if b == 0 else jnp.concatenate([scores[0 : b * QB, :], diag], axis=0)
            peak = jnp.max(scores, axis=0, keepdims=True)
            weights = jnp.exp(scores - peak)
            total = jnp.sum(weights, axis=0, keepdims=True)
            out = dot_nn(vt[head_rows, 0:end], weights.astype(BF))
            ot[head_rows, b * QB : end] = (out / total).astype(BF)
            lse[pl.ds(h, 1), b * QB : end] = peak + jnp.log(total)

    paced(heads, head_step)
    for i, chunk in enumerate(chunks):
        if chunk[0] == "proj":
            settle(i)

    def turn(i, rows):
        o[rows, :] = ot[:, rows].astype(F32).T.astype(BF)

    rows_loop(tokens, TILE, turn)
    emit(o, o_o)
    emit(lse, lse_o)
    emit(proj_w, proj_o)

    def project(i, rows):
        part[rows, :] = dot_nt(o[rows, :], proj_w[...].reshape(model, width)).astype(BF)

    half = tokens // 2
    part_copies = []
    for j in range(2):
        project(j, pl.ds(j * half, half))
        copy = mesh_copy(part.at[pl.ds(j * half, half)], part_r.at[pl.ds(j * half, half)], psend.at[2 + j], precv.at[2 + j],
                         device_id={"tensor": other})
        copy.start()
        part_copies.append(copy)
        advance()
    for j in range(2):
        part_copies[j].wait_recv()

        def norm_two(i, j=j):
            rows = pl.ds(pl.multiple_of(j * half + i * 256, 256), 256)
            middle = x_f[rows, :].astype(F32) + (part[rows, :].astype(F32) + part_r[rows, :].astype(F32)) + table[3:4, :]
            x2[rows, :] = middle
            a2[rows, :] = normed(middle, table[1:2, :], table[4:5, :]).astype(BF)

        paced(half // 256, norm_two)
    emit(x2, x2_o)
    emit(a2, a2_o)

    for j in range(hidden // TILE):
        cols = pl.ds(j * TILE, TILE)
        for i, chunk in enumerate(chunks):
            if chunk[0] == "up" and j * TILE <= chunk[2] < (j + 1) * TILE:
                settle(i)

        row = 8 + j * TILE // model
        bias_at = j * TILE % model

        def expand(i, rows, cols=cols, row=row, bias_at=bias_at):
            pre = dot_nn(a2[rows, :], up_w[..., cols].reshape(model, TILE)) + table[row : row + 1, bias_at : bias_at + TILE]
            square = pre * pre
            bent = jnp.tanh(pre * (gelu_scale + (gelu_scale * 0.044715) * square))
            rise = 0.5 + 0.5 * bent
            u[rows, cols] = (pre * rise).astype(BF)
            slope = 0.5 * pre * (1.0 - bent * bent) * (gelu_scale + (3 * 0.044715 * gelu_scale) * square)
            gp[rows, cols] = (rise + slope).astype(BF)

        paced(tokens // 256, lambda i: expand(i, span(i, 256)))

        def sum_down(i, rows, cols=cols):
            gdown[rows, cols] = dot_tn(cot_f[:, rows], u[:, cols]).astype(BF)

        paced(model // TILE, lambda i: sum_down(i, span(i, TILE)))
        for src, dst in ((u, u_o), (gp, gp_o), (gdown, gdown_o)):
            emit(src.at[:, cols], dst.at[:, cols])
        emit(up_w.at[(Ellipsis, cols)], up_o.at[(Ellipsis, cols)])
    for i, (name, lead, lo, size) in enumerate(chunks):
        settle(i)
        if name == "down":
            emit(down_w.at[(Ellipsis, pl.ds(lo, size))], down_o.at[(Ellipsis, pl.ds(lo, size))])
    for c in range(len(chunks)):
        for s in range(count):
            copy_of(c, s).wait_send()
    for copy in vec_copies + pair_copies + part_copies:
        copy.wait_send()
    for copy in outs:
        copy.wait()


GATHER_MODES = (
    3201, 1320, 3210, 2130, 2301, 3201, 3021, 1320, 3021, 3201, 3021, 1230, 2310, 3012, 3201, 1230, 3120, 2031, 1032, 2031, 321, 1230,
    3210, 213,
)
GATHER_ORDER = (
    16, 8, 20, 68, 17, 12, 9, 69, 40, 4, 21, 13, 0, 5, 70, 10, 18, 48, 36, 41, 14, 22, 84, 1, 28, 11, 19, 24, 6, 85, 42, 29, 49, 23,
    32, 71, 44, 2, 37, 52, 64, 60, 7, 3, 86, 15, 25, 43, 30, 56, 76, 45, 88, 61, 38, 50, 92, 33, 53, 72, 65, 26, 31, 80, 39, 77, 93,
    46, 87, 34, 57, 54, 62, 89, 51, 73, 27, 66, 94, 81, 78, 47, 35, 58, 55, 63, 90, 67, 74, 82, 95, 79, 59, 91, 75, 83,
)
GATHER_PLAN = (
    41, 2, 3, 2, 2, 7, 0, 1, 0, 4, 0, 0, 1, 2, 2, 0, 4, 3, 3, 2, 1, 2, 1, 5, 0, 3, 1, 0, 0, 0, 0, 0, 1, 0, 1, 0, 0, 0, 1, 0, 0, 1, 0,
    0, 0, 0, 0, 0, 0, 0, 0, 0, 0,
)


def forward_all(slopes, qkv, proj, up, down, small, x, cot, n, width=256):
    count = n.bit_length() - 1
    two = (2,) * count
    chunks = []
    for c in (1, 0, 2):
        chunks += [("qkv", c, lo, width) for lo in range(0, qkv.shape[2], width)]
    for name, a in (("proj", proj), ("up", up), ("down", down)):
        chunks += [(name, None, lo, width) for lo in range(0, a.shape[1], width)]
    tokens, model = 2 * x.shape[0], x.shape[1]
    inner, hidden = qkv.shape[2], up.shape[1]
    heads = inner // HD
    weights = [((3, *two, *qkv.shape[1:]), BF), ((*two, *proj.shape), BF), ((*two, *up.shape), BF), ((*two, *down.shape), BF)]
    shapes = weights + [((16, model), F32), ((tokens, model), BF), ((tokens, model), BF)] + [((tokens, inner), BF)] * 4
    shapes += [((heads, tokens), F32), ((tokens, model), F32), ((tokens, model), BF), ((tokens, hidden), BF), ((tokens, hidden), BF), ((model, hidden), BF)]
    vm = lambda s, d: pltpu.VMEM(s, d)
    scratch = [vm(*w) for w in weights]
    scratch += [vm((count + 2, 16, model), F32), vm((count + 1, 16, model), F32), vm((tokens, model), BF), vm((tokens, model), BF), vm((tokens, model), BF)]
    scratch += [vm((tokens, inner), BF)] * 3 + [vm((inner, tokens), BF)] * 2 + [vm((tokens, inner), BF), vm((heads, tokens), F32)]
    scratch += [vm((tokens, model), BF)] * 2 + [vm((tokens, model), F32), vm((tokens, model), BF), vm((tokens, hidden), BF), vm((tokens, hidden), BF), vm((model, hidden), BF)]
    scratch += [vm((tokens, 128), F32)]
    sems = lambda k: pltpu.SemaphoreType.DMA((k,))
    k = len(chunks) * count
    scratch += [sems(k), sems(k), sems(count + 1), sems(count + 1), sems(4), sems(4), sems(8), sems(64)]

    def body(slopes_ref, *refs):
        forward_kernel(count, chunks, GATHER_MODES, GATHER_ORDER, GATHER_PLAN, refs[:7], refs[7 : 7 + len(shapes)], refs[7 + len(shapes) :], slopes_ref)

    return pl.pallas_call(
        body, out_shape=tuple(jax.ShapeDtypeStruct(*s) for s in shapes),
        in_specs=[pl.BlockSpec(memory_space=pltpu.SMEM)] + [VM] * 7, out_specs=[ANY] * len(shapes), scratch_shapes=scratch,
        compiler_params=pltpu.CompilerParams(collective_id=0, has_side_effects=True, vmem_limit_bytes=62 * 2**20), name="forward_all",
    )(slopes, qkv, proj, up, down, small, x, cot)

SCATTER_MODES = (
    123, 3012, 321, 213, 2310, 1203, 321, 1230, 2031, 1023, 132, 1032, 321, 1302, 1230, 231, 3102, 1023, 1032, 2013, 1032, 123, 1023,
    213,
)
SCATTER_ORDER = (
    1, 26, 11, 36, 2, 21, 27, 12, 37, 3, 46, 28, 6, 22, 41, 51, 56, 13, 31, 61, 16, 38, 4, 76, 7, 29, 71, 17, 47, 42, 23, 86, 57, 32,
    39, 87, 77, 72, 52, 14, 62, 24, 33, 106, 48, 81, 91, 43, 8, 58, 96, 101, 66, 18, 116, 34, 111, 92, 73, 53, 78, 88, 97, 63, 102,
    107, 9, 82, 112, 44, 59, 98, 74, 49, 79, 117, 64, 67, 93, 108, 103, 89, 19, 54, 113, 118, 68, 99, 104, 94, 83, 114, 109, 119, 84,
    69,
)
SCATTER_PLAN = (
    0, 0, 0, 0, 0, 0, 0, 0, 0, 0, 0, 0, 0, 0, 0, 1, 0, 0, 1, 0, 1, 1, 0, 1, 2, 1, 0, 0, 0, 1, 0, 0, 0, 1, 0, 0, 0, 0, 0, 3, 3, 3, 2,
    2, 3, 2, 6, 1, 5, 0, 1, 1, 1, 7, 3, 0, 2, 8, 5,
)


def backward_kernel(count, chunks, modes, order, plan, slopes, table, refs_in, refs_out, scratch):
    (x_h, cot_h, a1_h, q_h, k_h, v_h, o_h, lse_h, x2_h, a2_h, u_h, gp_h, gdown_h, qkv_h, proj_h, up_h, down_h) = refs_in
    (layer_o, grad_o, gqkv_o, gproj_o, gup_o, gdown_o, sums_o) = refs_out
    landing = scratch[:count]
    (sums, sland, x_f, cot, a1, lse, x2, gp, big, gdown, gproj, gqkv, wide, up_w, part, part_r, first_r, last_r,
     kt, dqt, acc_k, acc_v, pos, send, recv, vsend, vrecv, psend, precv, in_sem) = scratch[count:]
    me = lax.axis_index("dp")
    t = lax.axis_index("tensor")
    other = 1 - t
    mine = bits_of(me, count)
    orders = bit_orders(count, modes, len(chunks), False)
    tokens, model = cot.shape
    width = q_h.shape[1]
    hidden = gp.shape[1]
    heads = width // HD
    local = tokens // 2
    q, k, v, o = (up_w.at[:, pl.ds(i * width, width)] for i in range(4))
    dq, dk, dv, do = q, k, v, o
    mesh_copy = functools.partial(pltpu.make_async_remote_copy, device_id_type=MESH)
    rows_of = lambda who, i, size: pl.ds(pl.multiple_of(who * local + i * size, size), size)

    enter(me, mine, count, other)
    loads = {}

    def load(name, src, dst):
        copy = pltpu.make_async_copy(src, dst, in_sem.at[len(loads)])
        copy.start()
        loads[name] = copy

    load("u", u_h, big)
    load("down", down_h, wide)
    load("gdown", gdown_h, gdown)
    load("cot", cot_h, cot)
    load("gp", gp_h, gp)
    load("x2", x2_h, x2)
    load("a2", a2_h, a1)
    load("up", up_h, up_w)
    load("lse", lse_h, lse)
    load("x", x_h, x_f)

    grads = {"qkv": gqkv, "proj": gproj, "up": big, "down": gdown}
    finals = {"qkv": gqkv_o, "proj": gproj_o, "up": gup_o, "down": gdown_o}
    size = chunks[0][3]

    def order_of(c):
        return orders[c]

    def held(c):
        name, lead, lo, _ = chunks[c]
        ref = grads[name]
        return ref if lead is None else ref.at[lead]

    def region(c, s, flip):
        order = order_of(c)
        at = []
        for b in reversed(range(count)):
            if b == order[s]:
                at.append(1 - mine[b] if flip else mine[b])
            else:
                at.append(mine[b] if b in order[:s] else slice(None))
        return tuple(at)

    def copy_of(c, s):
        name, lead, lo, _ = chunks[c]
        src = held(c)
        if name == "down" and s == 0:
            src = gdown_h
        at = (*region(c, s, True), slice(None), pl.ds(lo, size))
        return mesh_copy(src.at[at], landing[s].at[c], send.at[c * count + s], recv.at[c * count + s],
                         device_id={"dp": partner_of(me, mine, order_of(c)[s])})

    def run(item):
        c, s = item
        name, lead, lo, _ = chunks[c]
        copy_of(c, s - 1).wait_recv()
        got = landing[s - 1].at[c]
        keep = region(c, s - 1, False)
        cols = slice(lo, lo + size)
        ref = held(c)
        if s == count:
            total = ref[(*keep, slice(None), cols)].astype(F32) + got[...].astype(F32)
            out = finals[name]
            if lead is not None:
                out = out.at[lead]
            out[:, cols] = total
            return
        left = count - s

        def add(i, carry):
            sub = [lax.rem(i // (1 << (left - 1 - j)), 2) for j in range(left)]
            it = iter(sub)
            at = (*(next(it) if isinstance(b, slice) else b for b in keep), slice(None), cols)
            ref[at] = (ref[at].astype(F32) + got[tuple(sub)].astype(F32)).astype(BF)
            return carry

        lax.fori_loop(0, 1 << left, add, 0)
        copy_of(c, s).start()

    queue = [(code // (count + 1), code % (count + 1)) for code in order] if order and count == 4 else sorted(
        ((c, s) for c in range(len(chunks)) for s in range(1, count + 1)), key=lambda cs: (cs[0] + LOOK * cs[1], cs[0]))
    share = list(plan) if plan and count == 4 else []
    open_chunks = set()

    def ready(names):
        for c, (name, lead, lo, _) in enumerate(chunks):
            if (name, lead, lo) in names:
                copy_of(c, 0).start()
                open_chunks.add(c)

    def due():
        batch = []
        for _ in range(share.pop(0) if share else 2):
            if queue and queue[0][0] in open_chunks:
                batch.append(queue.pop(0))
        return batch

    def advance():
        for item in due():
            run(item)

    def paced(steps, body):
        paced_loop(steps, body, [due() for _ in range(steps)], run)

    tiles = lambda name, total, lead=None, at=0: {(name, lead, lo) for lo in range(at, at + total, size)}
    ready(tiles("down", hidden))
    loads["gdown"].wait()
    sums[0] = jnp.zeros_like(sums[0])
    pos[...] = lax.broadcasted_iota(jnp.int32, pos.shape, 0).astype(F32)

    def whole(ref, h=None, cols=slice(None)):
        return ref[:, cols] if h is None else ref[span(h, model // 2), cols]

    loads["u"].wait()
    loads["down"].wait()
    half = model // 2

    def lowered(who, h):
        return dot_nt(big[who].reshape(local, hidden), whole(wide, h))

    def partner_lowered(h):
        part[0:local, span(h, half)] = lowered(other, h).astype(BF)

    paced(2, partner_lowered)
    first = mesh_copy(part.at[pl.ds(0, local)], first_r, psend.at[0], precv.at[0], device_id={"tensor": other})
    first.start()

    loads["cot"].wait()
    loads["gp"].wait()
    for j in range(hidden // TILE):
        cols = slice(j * TILE, (j + 1) * TILE)

        def grad_pre(i, rows, cols=cols):
            value = (dot_nn(cot[rows, :], whole(wide, cols=cols)) * gp[rows, cols].astype(F32)).astype(BF)
            gp[rows, cols] = value
            line = 8 + cols.start // model
            at = slice(cols.start % model, cols.start % model + TILE)
            sums[0, line : line + 1, at] += jnp.sum(value.astype(F32), axis=0, keepdims=True)

        paced(tokens // 256, lambda i: grad_pre(i, span(i, 256)))

    loads["x2"].wait()
    first.wait_recv()

    def own_lowered(h):
        cols = span(h, half)
        mid = x2[rows_of(t, 0, local), cols]
        layer_o[:, cols] = (mid + (lowered(t, h) + first_r[:, cols].astype(F32)) + table[5:6, cols]).astype(BF)

    paced(2, own_lowered)
    load("qkv", qkv_h.at[0], wide.at[:, pl.ds(0, width)])
    load("qkv1", qkv_h.at[1], wide.at[:, pl.ds(width, width)])
    load("qkv2", qkv_h.at[2], wide.at[:, pl.ds(2 * width, width)])
    load("proj", proj_h, wide.at[:, pl.ds(3 * width, width)])

    loads["a2"].wait()
    loads["up"].wait()
    first.wait_send()
    part_copies = []
    for h in range(2):
        rows = pl.ds(h * local, local)

        def back_up(e, rows=rows):
            part[rows, span(e, half)] = dot_nt(gp[rows, :], whole(up_w, e)).astype(BF)

        paced(2, back_up)
        copy = mesh_copy(part.at[rows], part_r.at[rows], psend.at[1 + h], precv.at[1 + h], device_id={"tensor": other})
        copy.start()
        part_copies.append(copy)
    for name, src, dst in (("q", q_h, q), ("k", k_h, k), ("v", v_h, v), ("o", o_h, o)):
        load(name, src, dst)
    for j in range(hidden // TILE):
        cols = slice(j * TILE, (j + 1) * TILE)

        def sum_up(h, carry, cols=cols):
            value = dot_tn(a1[:, span(h, half)], gp[:, cols]).astype(BF)
            big[(h, Ellipsis, cols)] = value.reshape(*big.shape[1:-1], TILE)
            return carry

        lax.fori_loop(0, 2, sum_up, 0)
        ready(tiles("up", TILE, at=j * TILE))
        advance()
    load("a1", a1_h, a1)

    def norm_parts(value):
        center = value - jnp.mean(value, axis=-1, keepdims=True)
        inverse = lax.rsqrt(jnp.mean(center * center, axis=-1, keepdims=True) + epsilon)
        return center * inverse, inverse

    def norm_back(grad, normed, inverse, gain):
        scaled = grad * gain
        return inverse * (scaled - jnp.mean(scaled, axis=-1, keepdims=True) - normed * jnp.mean(scaled * normed, axis=-1, keepdims=True))

    def add_sum(line, value):
        sums[0, line : line + 1, :] += jnp.sum(value, axis=0, keepdims=True)

    for copy in part_copies:
        copy.wait_recv()
    for who, count_it in ((t, True), (other, False)):

        def through(i, who=who, count_it=count_it):
            rows = rows_of(who, i, 128)
            grad = part[rows, :].astype(F32) + part_r[rows, :].astype(F32)
            normed, inverse = norm_parts(x2[rows, :])
            outer = cot[rows, :].astype(F32)
            mid = outer + norm_back(grad, normed, inverse, table[1:2, :])
            x2[rows, :] = mid
            cot[rows, :] = mid.astype(BF)
            if count_it:
                add_sum(1, grad * normed)
                add_sum(3, mid)
                add_sum(4, grad)
                add_sum(5, outer)

        paced(local // 128, through)
    gx2 = cot

    loads["proj"].wait()
    loads["o"].wait()
    proj_cols = slice(3 * width, 4 * width)

    def sum_proj(h, carry):
        gproj[h] = dot_tn(gx2[:, span(h, half)], o[...]).astype(BF).reshape(gproj.shape[1:])
        return carry

    lax.fori_loop(0, 2, sum_proj, 0)
    ready(tiles("proj", width))
    advance()

    def through_proj(i, rows):
        do[rows, :] = dot_nn(gx2[rows, :], whole(wide, cols=proj_cols)).astype(BF)

    paced(tokens // TILE, lambda i: through_proj(i, span(i, TILE)))
    for name in ("q", "k", "v", "lse"):
        loads[name].wait()

    def turn_keys(i, rows):
        kt[:, rows] = k[rows, :].astype(F32).T.astype(BF)

    rows_loop(tokens, TILE, turn_keys)

    blocks = tokens // QB
    lane_half = lax.broadcasted_iota(jnp.int32, (QB, 2 * HD), 1) // HD

    def head_step(h):
        cols = span(h // 2, 2 * HD)
        head_rows = span(h, HD)
        side = lax.rem(h, 2)
        slope = slopes[h]

        @pl.when(side == 0)
        def _():
            acc_k[...] = jnp.zeros_like(acc_k)
            acc_v[...] = jnp.zeros_like(acc_v)

        for b in range(blocks):
            end = (b + 1) * QB
            rows = slice(b * QB, end)
            zero = jnp.zeros((QB, 2 * HD), BF)
            query = jnp.where(lane_half == side, q[rows, cols], zero)
            outer = jnp.where(lane_half == side, do[rows, cols], zero)
            bias = pos[0:end, :] * slope
            bias = jnp.concatenate([bias] * (QB // bias.shape[1]), axis=1)
            scores = dot_nt(k[0:end, cols], query) + bias - lse[pl.ds(h, 1), rows]
            keep = lax.broadcasted_iota(jnp.int32, (QB, QB), 0) <= lax.broadcasted_iota(jnp.int32, (QB, QB), 1)
            diag = jnp.where(keep, scores[b * QB : end, :], -1e30)
            scores = diag if b == 0 else jnp.concatenate([scores[0 : b * QB, :], diag], axis=0)
            probs = jnp.exp(scores)
            acc_v[0:end, :] += dot_nn(probs.astype(BF), outer)
            grad = dot_nt(v[0:end, cols], outer)
            inner = jnp.sum(probs * grad, axis=0, keepdims=True)
            low = (probs * (grad - inner)).astype(BF)
            acc_k[0:end, :] += dot_nn(low, query)
            dqt[head_rows, rows] = (dot_nn(kt[head_rows, 0:end], low) * HD ** (-0.5)).astype(BF)

        @pl.when(side == 1)
        def _():
            dk[:, cols] = acc_k[...].astype(BF)
            dv[:, cols] = acc_v[...].astype(BF)

    paced(heads, head_step)

    def turn(i, rows):
        dq[rows, :] = dqt[:, rows].astype(F32).T.astype(BF)

    rows_loop(tokens, TILE, turn)
    loads["a1"].wait()
    for c, ref in ((1, dk), (2, dv), (0, dq)):

        def sum_qkv(h, carry, c=c, ref=ref):
            gqkv[c, h] = dot_tn(a1[:, span(h, half)], ref[...]).astype(BF).reshape(gqkv.shape[2:])
            return carry

        lax.fori_loop(0, 2, sum_qkv, 0)
        ready(tiles("qkv", width, lead=c))
        advance()
    for at, ref in ((0, dq), (width, dv)):
        sums[0, 10:11, at : at + width] = jnp.sum(ref[...].astype(F32), axis=0, keepdims=True)

    for name in ("qkv", "qkv1", "qkv2"):
        loads[name].wait()

    def back_one(rows):
        total = dot_nt(dq[rows, :], whole(wide, cols=slice(0, width)))
        total += dot_nt(dk[rows, :], whole(wide, cols=slice(width, 2 * width)))
        return total + dot_nt(dv[rows, :], whole(wide, cols=slice(2 * width, 3 * width)))

    for copy in part_copies:
        copy.wait_send()

    def partner_rows(i):
        part[span(i, 256), :] = back_one(rows_of(other, i, 256)).astype(BF)

    paced(local // 256, partner_rows)
    last = mesh_copy(part.at[pl.ds(0, local)], last_r, psend.at[3], precv.at[3], device_id={"tensor": other})
    last.start()
    advance()
    loads["x"].wait()
    last.wait_recv()

    def own_rows(i):
        rows = rows_of(t, i, 256)
        here = span(i, 256)
        grad = back_one(rows) + last_r[here, :].astype(F32)
        normed, inverse = norm_parts(x_f[here, :].astype(F32))
        grad_o[here, :] = x2[rows, :] + norm_back(grad, normed, inverse, table[0:1, :])
        add_sum(0, grad * normed)
        add_sum(2, grad)

    paced(local // 256, own_rows)

    def sum_step(s):
        to = {"dp": partner_of(me, mine, s)} if s < count else {"tensor": other}
        return mesh_copy(sums.at[s], sland.at[s], vsend.at[s], vrecv.at[s], device_id=to)

    sum_copies = [sum_step(s) for s in range(count + 1)]
    sum_copies[0].start()
    for s in range(count):
        advance()
        sum_copies[s].wait_recv()
        sums[s + 1] = sums[s] + sland[s]
        sum_copies[s + 1].start()
    while queue:
        run(queue.pop(0))
    sum_copies[count].wait_recv()
    sums_o[0:8, :] = sums[count, 0:8] + sland[count, 0:8]
    sums_o[8:16, :] = sums[count, 8:16]
    for c in range(len(chunks)):
        for s in range(count):
            copy_of(c, s).wait_send()
    for copy in sum_copies + [last]:
        copy.wait_send()


def backward_all(slopes, table, x, cot, a1, q, k, v, o, lse, x2, a2, u, gp, gdown, qkv_w, proj_w, up_w, down_w, n, width=256):
    count = n.bit_length() - 1
    two = (2,) * count
    tokens, model = cot.shape
    inner, hidden = q.shape[1], gp.shape[1]
    heads = inner // HD
    r = model // n
    chunks = [("down", None, lo, width) for lo in range(0, hidden, width)]
    chunks += [("up", None, lo, width) for lo in range(0, hidden, width)]
    chunks += [("proj", None, lo, width) for lo in range(0, inner, width)]
    for c in (1, 2, 0):
        chunks += [("qkv", c, lo, width) for lo in range(0, inner, width)]
    f = lambda *s: jax.ShapeDtypeStruct(s, F32)
    outs = (jax.ShapeDtypeStruct(x.shape, BF), f(*x.shape), f(3, r, inner), f(r, inner), f(r, hidden), f(r, hidden), f(16, model))
    vm = lambda *s, d=BF: pltpu.VMEM(s, d)
    scratch = [vm(len(chunks), *two[: count - 1 - s], r, width) for s in range(count)]
    scratch += [vm(count + 1, 16, model, d=F32), vm(count + 1, 16, model, d=F32), vm(*x.shape), vm(tokens, model), vm(tokens, model)]
    scratch += [vm(heads, tokens, d=F32), vm(tokens, model, d=F32), vm(tokens, hidden)]
    scratch += [vm(*two, r, hidden), vm(*two, r, hidden), vm(*two, r, inner), vm(3, *two, r, inner), vm(model, hidden), vm(model, hidden)]
    scratch += [vm(tokens, model), vm(tokens, model), vm(*x.shape), vm(*x.shape), vm(inner, tokens), vm(inner, tokens)]
    scratch += [vm(tokens, 2 * HD, d=F32)] * 2 + [vm(tokens, 128, d=F32)]
    sems = lambda m: pltpu.SemaphoreType.DMA((m,))
    m = len(chunks) * count
    scratch += [sems(m), sems(m), sems(count + 1), sems(count + 1), sems(4), sems(4), sems(20)]
    flat = lambda a: a.reshape(*a.shape[: a.ndim - count - 2], model, a.shape[-1])
    by_block = lambda a: a.reshape(*two, r, a.shape[-1])

    def body(slopes_ref, table_ref, *refs):
        backward_kernel(count, chunks, SCATTER_MODES, SCATTER_ORDER, SCATTER_PLAN, slopes_ref, table_ref, refs[:17], refs[17 : 17 + len(outs)], refs[17 + len(outs) :])

    return pl.pallas_call(
        body, out_shape=outs, in_specs=[pl.BlockSpec(memory_space=pltpu.SMEM), VM] + [ANY] * 17, out_specs=[VM] * len(outs), scratch_shapes=scratch,
        compiler_params=pltpu.CompilerParams(collective_id=1, has_side_effects=True, vmem_limit_bytes=67043328), name="backward_all",
    )(slopes, table, x, cot, a1, q, k, v, o, lse, x2, a2, by_block(u), gp, by_block(gdown), flat(qkv_w), flat(proj_w), flat(up_w), flat(down_w))

def finish_kernel(count, *refs):
    ins, outs, bufs = refs[:count], refs[count : 2 * count], refs[2 * count : 3 * count]
    in_sem, out_sem = refs[3 * count :]
    reads = [pltpu.make_async_copy(a, b, in_sem.at[i]) for i, (a, b) in enumerate(zip(ins, bufs))]
    writes = [pltpu.make_async_copy(b, c, out_sem.at[i]) for i, (b, c) in enumerate(zip(bufs, outs))]
    for copy in reads:
        copy.start()
    for read, write in zip(reads, writes):
        read.wait()
        write.start()
    for copy in writes:
        copy.wait()


def finish(arrays):
    count = len(arrays)
    return pl.pallas_call(
        functools.partial(finish_kernel, count), out_shape=tuple(jax.ShapeDtypeStruct(a.shape, a.dtype) for a in arrays),
        in_specs=[ANY] * count, out_specs=[ANY] * count,
        scratch_shapes=[pltpu.VMEM(a.shape, a.dtype) for a in arrays] + [pltpu.SemaphoreType.DMA((count,))] * 2, name="finish")(*arrays)


def on_device(layer_in, w_qkv, b_qv, w_proj, w_ff1, b_ff1, w_ff2, norm_gains, add_biases, cotangent):
    n = lax.axis_size("dp")
    i = lax.axis_index("dp")
    t = lax.axis_index("tensor")
    width = w_qkv.shape[2]
    model = layer_in.shape[1]
    hidden = w_ff1.shape[1]
    heads = b_qv.shape[1]
    part = norm_gains.shape[1]
    zero = jnp.int32(0)
    put = lambda shape, a, at: lax.dynamic_update_slice(jnp.zeros(shape, F32), a.astype(F32), at)
    up_grid = (b_ff1.shape[0], n * b_ff1.shape[1])
    qv_grid = (*b_qv.shape[:2], n * b_qv.shape[2])
    small = jnp.concatenate([
        put((8, model), jnp.concatenate([norm_gains, add_biases]), (zero, (2 * i + t) * part)),
        put(up_grid, b_ff1, (zero, i * b_ff1.shape[1])).reshape(-1, model),
        put(qv_grid, b_qv, (zero, zero, i * b_qv.shape[2])).reshape(-1, model),
        jnp.zeros((8 - (hidden + 2 * width) // model, model), F32)])
    slopes = 2.0 ** (-8.0 * (t * heads + jnp.arange(heads, dtype=jnp.int32) + 1).astype(F32) / H)
    (qkv_w, proj_w, up_w, down_w, vectors, cot, a1, q, k, v, o, lse, x2, a2, u, rise, grad_down) = forward_all(
        slopes, w_qkv, w_proj.T, w_ff1, w_ff2.T, small, layer_in, cotangent, n)
    layer_out, grad_in, out_qkv, out_proj, out_up, out_down, sums = backward_all(
        slopes, vectors, layer_in, cot, a1, q, k, v, o, lse, x2, a2, u, rise, grad_down, qkv_w, proj_w, up_w, down_w, n)
    layer_out, grad_in, out_qkv, out_proj, out_up, out_down, sums = finish(
        (layer_out, grad_in, out_qkv, out_proj, out_up, out_down, sums))
    own = lax.dynamic_slice(sums, (zero, (2 * i + t) * part), (6, part))
    up_sums = lax.dynamic_slice_in_dim(sums[8 : 8 + hidden // model].reshape(up_grid), i * b_ff1.shape[1], b_ff1.shape[1], 1)
    qv_sums = lax.dynamic_slice_in_dim(sums[10].reshape(qv_grid), i * b_qv.shape[2], b_qv.shape[2], 2)
    return (layer_out, grad_in, out_qkv, qv_sums, out_proj.T, out_up, up_sums, out_down.T, own[:2], own[2:])


def solution(mesh):
    rows, cols = P(("dp", "tensor"), None), P(None, ("dp", "tensor"))
    return jax.shard_map(
        on_device,
        mesh=mesh,
        in_specs=(rows, P(None, "dp", "tensor"), P(None, "tensor", "dp"), P("tensor", "dp"), P("dp", "tensor"),
                  P("tensor", "dp"), P("tensor", "dp"), cols, cols, rows),
        out_specs=(rows, rows, P(None, "dp", "tensor"), P(None, "tensor", "dp"), P("tensor", "dp"), P("dp", "tensor"),
                   P("tensor", "dp"), P("tensor", "dp"), cols, cols),
        check_vma=False,
    )
```

```python
import functools
import math
import jax
import jax.numpy as jnp
from jax import lax
from jax.experimental import pallas as pl
from jax.experimental.pallas import tpu as pltpu
from jax.sharding import PartitionSpec as P

MESH = pl.DeviceIdType.MESH
ANY = pl.BlockSpec(memory_space=pl.ANY)
VM = pl.BlockSpec(memory_space=pltpu.VMEM)


def bits_of(index, count):
    return [lax.rem(index // (1 << b), 2) for b in range(count)]


def partner_of(index, mine, b):
    return index + (1 - 2 * mine[b]) * (1 << b)


def halving_orders(count):
    return [[(start + i) % count for i in range(count)] for start in range(3)]


def enter(index, mine, count, other):
    barrier = pltpu.get_barrier_semaphore()
    for b in range(count):
        pl.semaphore_signal(barrier, inc=1, device_id={"dp": partner_of(index, mine, b)}, device_id_type=MESH)
    pl.semaphore_signal(barrier, inc=1, device_id={"tensor": other}, device_id_type=MESH)
    pl.semaphore_wait(barrier, count + 1)


def block_index(mine, held, count):
    return tuple(slice(None) if b in held else mine[b] for b in reversed(range(count)))

SEQ_LEN = 1024
HD = 64
H = 16
epsilon = 1e-05
gelu_scale = 0.7978845608028654
F32 = jnp.float32
BF = jnp.bfloat16
TILE = 512
QB = 256
LOOK = 4


def bit_orders(count, modes, total, flip):
    if modes and count == 4:
        return [[mode // 10**i % 10 for i in (3, 2, 1, 0)] for mode in modes]
    cyclic = [[(start + i) % count for i in range(count)] for start in (0, 1, 0, 1, 0, 1, 0, 2)]
    return [(order[::-1] if flip else order) for order in (cyclic[c % len(cyclic)] for c in range(total))]


def dot_nn(a, b):
    return lax.dot_general(a, b, (((1,), (0,)), ((), ())), preferred_element_type=F32)


def dot_nt(a, b):
    return lax.dot_general(a, b, (((1,), (1,)), ((), ())), preferred_element_type=F32)


def dot_tn(a, b):
    return lax.dot_general(a, b, (((0,), (0,)), ((), ())), preferred_element_type=F32)


def span(i, size):
    return pl.ds(pl.multiple_of(i * size, size), size)


def paced_loop(steps, body, batches, run):
    def step(i, carry):
        for j in range(steps):
            if batches[j]:

                @pl.when(i == j)
                def _():
                    for item in batches[j]:
                        run(item)

        body(i)
        return carry

    lax.fori_loop(0, steps, step, 0)


def rows_loop(total, size, body):
    def step(i, carry):
        body(i, span(i, size))
        return carry

    lax.fori_loop(0, total // size, step, 0)


def forward_kernel(count, chunks, modes, order, plan, refs_in, refs_out, scratch, slopes):
    (qkv, proj, up, down, small, x, cot) = refs_in
    (qkv_o, proj_o, up_o, down_o, vec_o, cot_o, a1_o, q_o, k_o, v_o, o_o, lse_o, x2_o, a2_o, u_o, gp_o, gdown_o) = refs_out
    (qkv_w, proj_w, up_w, down_w, vec, vland, x_f, cot_f, a1, q, k, v, vt, ot, o, lse, part, part_r, x2, a2, u, gp, gdown, pos,
     send, recv, vsend, vrecv, psend, precv, own_sem, out_sem) = scratch
    me = lax.axis_index("dp")
    t = lax.axis_index("tensor")
    other = 1 - t
    mine = bits_of(me, count)
    orders = bit_orders(count, modes, len(chunks), True)
    full = block_index(mine, (), count)
    tokens, model = x_f.shape
    width = q.shape[1]
    hidden = u.shape[1]
    heads = width // HD
    local_rows = x.shape[0]
    mesh_copy = functools.partial(pltpu.make_async_remote_copy, device_id_type=MESH)

    enter(me, mine, count, other)
    waits = []

    def vec_step(s):
        to = {"dp": partner_of(me, mine, s)} if s < count else {"tensor": other}
        return mesh_copy(small if s == 0 else vec.at[s], vland.at[s], vsend.at[s], vrecv.at[s], device_id=to)

    vec[0] = small[...]
    vec_copies = [vec_step(s) for s in range(count + 1)]
    vec_copies[0].start()

    mine_rows = pl.ds(t * local_rows, local_rows)
    pair_copies = [mesh_copy(src, dst.at[mine_rows], psend.at[i], precv.at[i], device_id={"tensor": other})
                   for i, (src, dst) in enumerate(((x, x_f), (cot, cot_f)))]
    for copy in pair_copies:
        copy.start()

    names = {"qkv": (qkv, qkv_w), "proj": (proj, proj_w), "up": (up, up_w), "down": (down, down_w)}

    def views(c):
        name, lead, lo, size = chunks[c]
        src, dst = names[name]
        if lead is not None:
            src, dst = src.at[lead], dst.at[lead]
        return src.at[:, pl.ds(lo, size)], dst, (slice(None), pl.ds(lo, size))

    def copy_of(c, s):
        order = orders[c]
        src, dst, tail = views(c)
        at = (*block_index(mine, order[:s], count), *tail)
        return mesh_copy(src if s == 0 else dst.at[at], dst.at[at], send.at[c * count + s], recv.at[c * count + s],
                         device_id={"dp": partner_of(me, mine, order[s])})

    owns = [pltpu.make_async_copy(src, dst.at[full], own_sem.at[i]) for i, (src, dst) in enumerate(
        [(qkv.at[c], qkv_w.at[c]) for c in range(3)] + [(proj, proj_w), (up, up_w), (down, down_w)])]
    owns += [pltpu.make_async_copy(src, dst.at[mine_rows], own_sem.at[6 + i]) for i, (src, dst) in enumerate(((x, x_f), (cot, cot_f)))]
    for copy in owns:
        copy.start()
    for copy in owns:
        copy.wait()

    queue = [divmod(code, count) for code in order] if order and count == 4 else sorted(
        ((c, s) for c in range(len(chunks)) for s in range(count)), key=lambda cs: (cs[0] + LOOK * cs[1], cs[0]))
    share = list(plan) if plan and count == 4 else []
    done = set()

    def run(item):
        c, s = item
        if s > 0:
            copy_of(c, s - 1).wait_recv()
        copy_of(c, s).start()

    def settle(c):
        if c not in done:
            while any(item[0] == c for item in queue):
                run(queue.pop(0))
            copy_of(c, count - 1).wait_recv()
            done.add(c)

    def due():
        size = share.pop(0) if share else 2
        batch, queue[:] = queue[:size], queue[size:]
        return batch

    def advance():
        for item in due():
            run(item)

    def paced(steps, body):
        paced_loop(steps, body, [due() for _ in range(steps)], run)

    outs = []

    def emit(src, dst):
        copy = pltpu.make_async_copy(src, dst, out_sem.at[len(outs)])
        copy.start()
        outs.append(copy)

    advance()
    for s in range(count):
        vec_copies[s].wait_recv()
        vec[s + 1] = vec[s] + vland[s]
        vec_copies[s + 1].start()
        advance()
    for copy in pair_copies:
        copy.wait_recv()
    emit(cot_f, cot_o)
    vec_copies[count].wait_recv()
    vec[count + 1, 0:8] = vec[count, 0:8] + vland[count, 0:8]
    vec[count + 1, 8:16] = vec[count, 8:16]
    emit(vec.at[count + 1], vec_o)
    table = vec.at[count + 1]

    def normed(rows_value, gain, shift):
        center = rows_value - jnp.mean(rows_value, axis=-1, keepdims=True)
        spread = jnp.mean(center * center, axis=-1, keepdims=True)
        return (center * lax.rsqrt(spread + epsilon)) * gain + shift

    def norm_one(i, rows):
        a1[rows, :] = normed(x_f[rows, :].astype(F32), table[0:1, :], table[2:3, :]).astype(BF)

    pos[...] = lax.broadcasted_iota(jnp.int32, pos.shape, 0).astype(F32)
    paced(4, lambda i: norm_one(i, span(i, tokens // 4)))
    emit(a1, a1_o)

    for c, dst in ((1, k), (0, q), (2, v)):
        for i, chunk in enumerate(chunks):
            if chunk[0] == "qkv" and chunk[1] == c:
                settle(i)

        def mix(i, rows, c=c, dst=dst):
            value = dot_nn(a1[rows, :], qkv_w[c].reshape(model, width))
            if c == 0:
                value = (value + table[10:11, 0:width]).astype(BF).astype(F32) * HD ** (-0.5)
            if c == 2:
                value = value + table[10:11, width : 2 * width]
            dst[rows, :] = value.astype(BF)
            if c == 2:
                vt[:, rows] = value.T.astype(BF)

        paced(2, lambda i: mix(i, span(i, tokens // 2)))
    for src, dst in ((q, q_o), (k, k_o), (v, v_o), (qkv_w, qkv_o)):
        emit(src, dst)

    blocks = tokens // QB
    lane_half = lax.broadcasted_iota(jnp.int32, (QB, 2 * HD), 1) // HD

    def head_step(h):
        cols = span(h // 2, 2 * HD)
        slope = slopes[h]
        head_rows = span(h, HD)
        for b in range(blocks):
            end = (b + 1) * QB
            query = jnp.where(lane_half == lax.rem(h, 2), q[b * QB : end, cols], jnp.zeros((QB, 2 * HD), BF))
            bias = pos[0:end, :] * slope
            bias = jnp.concatenate([bias] * (QB // bias.shape[1]), axis=1)
            scores = dot_nt(k[0:end, cols], query) + bias
            diag = scores[b * QB : end, :]
            keep = lax.broadcasted_iota(jnp.int32, (QB, QB), 0) <= lax.broadcasted_iota(jnp.int32, (QB, QB), 1)
            diag = jnp.where(keep, diag, -1e30)
            scores = diag if b == 0 else jnp.concatenate([scores[0 : b * QB, :], diag], axis=0)
            peak = jnp.max(scores, axis=0, keepdims=True)
            weights = jnp.exp(scores - peak)
            total = jnp.sum(weights, axis=0, keepdims=True)
            out = dot_nn(vt[head_rows, 0:end], weights.astype(BF))
            ot[head_rows, b * QB : end] = (out / total).astype(BF)
            lse[pl.ds(h, 1), b * QB : end] = peak + jnp.log(total)

    paced(heads, head_step)
    for i, chunk in enumerate(chunks):
        if chunk[0] == "proj":
            settle(i)

    def turn(i, rows):
        o[rows, :] = ot[:, rows].astype(F32).T.astype(BF)

    rows_loop(tokens, TILE, turn)
    emit(o, o_o)
    emit(lse, lse_o)
    emit(proj_w, proj_o)

    def project(i, rows):
        part[rows, :] = dot_nt(o[rows, :], proj_w[...].reshape(model, width)).astype(BF)

    half = tokens // 2
    part_copies = []
    for j in range(2):
        project(j, pl.ds(j * half, half))
        copy = mesh_copy(part.at[pl.ds(j * half, half)], part_r.at[pl.ds(j * half, half)], psend.at[2 + j], precv.at[2 + j],
                         device_id={"tensor": other})
        copy.start()
        part_copies.append(copy)
        advance()
    for j in range(2):
        part_copies[j].wait_recv()

        def norm_two(i, j=j):
            rows = pl.ds(pl.multiple_of(j * half + i * 256, 256), 256)
            middle = x_f[rows, :].astype(F32) + (part[rows, :].astype(F32) + part_r[rows, :].astype(F32)) + table[3:4, :]
            x2[rows, :] = middle
            a2[rows, :] = normed(middle, table[1:2, :], table[4:5, :]).astype(BF)

        paced(half // 256, norm_two)
    emit(x2, x2_o)
    emit(a2, a2_o)

    for j in range(hidden // TILE):
        cols = pl.ds(j * TILE, TILE)
        for i, chunk in enumerate(chunks):
            if chunk[0] == "up" and j * TILE <= chunk[2] < (j + 1) * TILE:
                settle(i)

        row = 8 + j * TILE // model
        bias_at = j * TILE % model

        def expand(i, rows, cols=cols, row=row, bias_at=bias_at):
            pre = dot_nn(a2[rows, :], up_w[..., cols].reshape(model, TILE)) + table[row : row + 1, bias_at : bias_at + TILE]
            square = pre * pre
            bent = jnp.tanh(pre * (gelu_scale + (gelu_scale * 0.044715) * square))
            rise = 0.5 + 0.5 * bent
            u[rows, cols] = (pre * rise).astype(BF)
            slope = 0.5 * pre * (1.0 - bent * bent) * (gelu_scale + (3 * 0.044715 * gelu_scale) * square)
            gp[rows, cols] = (rise + slope).astype(BF)

        paced(tokens // 256, lambda i: expand(i, span(i, 256)))

        def sum_down(i, rows, cols=cols):
            gdown[rows, cols] = dot_tn(cot_f[:, rows], u[:, cols]).astype(BF)

        paced(model // TILE, lambda i: sum_down(i, span(i, TILE)))
        for src, dst in ((u, u_o), (gp, gp_o), (gdown, gdown_o)):
            emit(src.at[:, cols], dst.at[:, cols])
        emit(up_w.at[(Ellipsis, cols)], up_o.at[(Ellipsis, cols)])
    for i, (name, lead, lo, size) in enumerate(chunks):
        settle(i)
        if name == "down":
            emit(down_w.at[(Ellipsis, pl.ds(lo, size))], down_o.at[(Ellipsis, pl.ds(lo, size))])
    for c in range(len(chunks)):
        for s in range(count):
            copy_of(c, s).wait_send()
    for copy in vec_copies + pair_copies + part_copies:
        copy.wait_send()
    for copy in outs:
        copy.wait()


GATHER_MODES = (
    3201, 1320, 3210, 2130, 2301, 3201, 3021, 1320, 3021, 3201, 3021, 1230, 2310, 3012, 3201, 1230, 3120, 2031, 1032, 2031, 321, 1230,
    3210, 213,
)
GATHER_ORDER = (
    16, 8, 20, 68, 17, 12, 9, 69, 40, 4, 21, 13, 0, 5, 70, 10, 18, 48, 36, 41, 14, 22, 84, 1, 28, 11, 19, 24, 6, 85, 42, 29, 49, 23,
    32, 71, 44, 2, 37, 52, 64, 60, 7, 3, 86, 15, 25, 43, 30, 56, 76, 45, 88, 61, 38, 50, 92, 33, 53, 72, 65, 26, 31, 80, 39, 77, 93,
    46, 87, 34, 57, 54, 62, 89, 51, 73, 27, 66, 94, 81, 78, 47, 35, 58, 55, 63, 90, 67, 74, 82, 95, 79, 59, 91, 75, 83,
)
GATHER_PLAN = (
    41, 2, 3, 2, 2, 7, 0, 1, 0, 4, 0, 0, 1, 2, 2, 0, 4, 3, 3, 2, 1, 2, 1, 5, 0, 3, 1, 0, 0, 0, 0, 0, 1, 0, 1, 0, 0, 0, 1, 0, 0, 1, 0,
    0, 0, 0, 0, 0, 0, 0, 0, 0, 0,
)


def forward_all(slopes, qkv, proj, up, down, small, x, cot, n, width=256):
    count = n.bit_length() - 1
    two = (2,) * count
    chunks = []
    for c in (1, 0, 2):
        chunks += [("qkv", c, lo, width) for lo in range(0, qkv.shape[2], width)]
    for name, a in (("proj", proj), ("up", up), ("down", down)):
        chunks += [(name, None, lo, width) for lo in range(0, a.shape[1], width)]
    tokens, model = 2 * x.shape[0], x.shape[1]
    inner, hidden = qkv.shape[2], up.shape[1]
    heads = inner // HD
    weights = [((3, *two, *qkv.shape[1:]), BF), ((*two, *proj.shape), BF), ((*two, *up.shape), BF), ((*two, *down.shape), BF)]
    shapes = weights + [((16, model), F32), ((tokens, model), BF), ((tokens, model), BF)] + [((tokens, inner), BF)] * 4
    shapes += [((heads, tokens), F32), ((tokens, model), F32), ((tokens, model), BF), ((tokens, hidden), BF), ((tokens, hidden), BF), ((model, hidden), BF)]
    vm = lambda s, d: pltpu.VMEM(s, d)
    scratch = [vm(*w) for w in weights]
    scratch += [vm((count + 2, 16, model), F32), vm((count + 1, 16, model), F32), vm((tokens, model), BF), vm((tokens, model), BF), vm((tokens, model), BF)]
    scratch += [vm((tokens, inner), BF)] * 3 + [vm((inner, tokens), BF)] * 2 + [vm((tokens, inner), BF), vm((heads, tokens), F32)]
    scratch += [vm((tokens, model), BF)] * 2 + [vm((tokens, model), F32), vm((tokens, model), BF), vm((tokens, hidden), BF), vm((tokens, hidden), BF), vm((model, hidden), BF)]
    scratch += [vm((tokens, 128), F32)]
    sems = lambda k: pltpu.SemaphoreType.DMA((k,))
    k = len(chunks) * count
    scratch += [sems(k), sems(k), sems(count + 1), sems(count + 1), sems(4), sems(4), sems(8), sems(64)]

    def body(slopes_ref, *refs):
        forward_kernel(count, chunks, GATHER_MODES, GATHER_ORDER, GATHER_PLAN, refs[:7], refs[7 : 7 + len(shapes)], refs[7 + len(shapes) :], slopes_ref)

    return pl.pallas_call(
        body, out_shape=tuple(jax.ShapeDtypeStruct(*s) for s in shapes),
        in_specs=[pl.BlockSpec(memory_space=pltpu.SMEM)] + [VM] * 7, out_specs=[ANY] * len(shapes), scratch_shapes=scratch,
        compiler_params=pltpu.CompilerParams(collective_id=0, has_side_effects=True, vmem_limit_bytes=62 * 2**20), name="forward_all",
    )(slopes, qkv, proj, up, down, small, x, cot)

SCATTER_MODES = (
    1023, 2013, 231, 1320, 1023, 3021, 213, 3012, 1320, 213, 213, 3021, 1203, 1023, 1302, 1023, 132, 213, 132, 1032, 3120, 213, 1023,
    2013,
)
SCATTER_ORDER = (
    1, 11, 26, 31, 16, 21, 2, 27, 22, 12, 32, 46, 3, 61, 17, 28, 23, 81, 41, 56, 51, 66, 36, 47, 62, 86, 13, 18, 71, 76, 4, 24, 29,
    57, 67, 33, 96, 52, 82, 91, 37, 63, 6, 87, 42, 101, 106, 77, 19, 48, 68, 111, 14, 116, 97, 53, 92, 83, 7, 58, 38, 88, 34, 72, 112,
    107, 64, 102, 117, 43, 8, 59, 78, 49, 73, 108, 98, 118, 69, 84, 93, 44, 54, 89, 113, 103, 39, 99, 109, 119, 94, 74, 79, 104, 114,
    9,
)
SCATTER_PLAN = (
    0, 0, 0, 0, 0, 0, 0, 0, 0, 0, 0, 0, 0, 0, 0, 0, 0, 0, 0, 2, 0, 1, 2, 1, 1, 1, 1, 0, 0, 1, 0, 0, 0, 0, 0, 0, 1, 0, 0, 1, 3, 2, 4,
    1, 4, 5, 5, 5, 0, 1, 4, 4, 3, 3, 4, 7, 6,
)


def backward_kernel(count, chunks, modes, order, plan, slopes, table, refs_in, refs_out, scratch):
    (x_h, cot_h, a1_h, q_h, k_h, v_h, o_h, lse_h, x2_h, a2_h, u_h, gp_h, gdown_h, qkv_h, proj_h, up_h, down_h) = refs_in
    (layer_o, grad_o, gqkv_o, gproj_o, gup_o, gdown_o, sums_o) = refs_out
    landing = scratch[:count]
    (sums, sland, x_f, cot, a1, lse, x2, gp, big, gdown, gproj, gqkv, wide, up_w, part, part_r, first_r, last_r,
     kt, dqt, acc_k, acc_v, pos, send, recv, vsend, vrecv, psend, precv, in_sem) = scratch[count:]
    me = lax.axis_index("dp")
    t = lax.axis_index("tensor")
    other = 1 - t
    mine = bits_of(me, count)
    orders = bit_orders(count, modes, len(chunks), False)
    tokens, model = cot.shape
    width = q_h.shape[1]
    hidden = gp.shape[1]
    heads = width // HD
    local = tokens // 2
    q, k, v, o = (up_w.at[:, pl.ds(i * width, width)] for i in range(4))
    dq, dk, dv, do = q, k, v, o
    mesh_copy = functools.partial(pltpu.make_async_remote_copy, device_id_type=MESH)
    rows_of = lambda who, i, size: pl.ds(pl.multiple_of(who * local + i * size, size), size)

    enter(me, mine, count, other)
    loads = {}

    def load(name, src, dst):
        copy = pltpu.make_async_copy(src, dst, in_sem.at[len(loads)])
        copy.start()
        loads[name] = copy

    load("u", u_h, big)
    load("down", down_h, wide)
    load("gdown", gdown_h, gdown)
    load("cot", cot_h, cot)
    load("gp", gp_h, gp)
    load("x2", x2_h, x2)
    load("a2", a2_h, a1)
    load("up", up_h, up_w)
    load("lse", lse_h, lse)
    load("x", x_h, x_f)

    grads = {"qkv": gqkv, "proj": gproj, "up": big, "down": gdown}
    finals = {"qkv": gqkv_o, "proj": gproj_o, "up": gup_o, "down": gdown_o}
    size = chunks[0][3]

    def order_of(c):
        return orders[c]

    def held(c):
        name, lead, lo, _ = chunks[c]
        ref = grads[name]
        return ref if lead is None else ref.at[lead]

    def region(c, s, flip):
        order = order_of(c)
        at = []
        for b in reversed(range(count)):
            if b == order[s]:
                at.append(1 - mine[b] if flip else mine[b])
            else:
                at.append(mine[b] if b in order[:s] else slice(None))
        return tuple(at)

    def copy_of(c, s):
        name, lead, lo, _ = chunks[c]
        src = held(c)
        if name == "down" and s == 0:
            src = gdown_h
        at = (*region(c, s, True), slice(None), pl.ds(lo, size))
        return mesh_copy(src.at[at], landing[s].at[c], send.at[c * count + s], recv.at[c * count + s],
                         device_id={"dp": partner_of(me, mine, order_of(c)[s])})

    def run(item):
        c, s = item
        name, lead, lo, _ = chunks[c]
        copy_of(c, s - 1).wait_recv()
        got = landing[s - 1].at[c]
        keep = region(c, s - 1, False)
        cols = slice(lo, lo + size)
        ref = held(c)
        if s == count:
            total = ref[(*keep, slice(None), cols)].astype(F32) + got[...].astype(F32)
            out = finals[name]
            if lead is not None:
                out = out.at[lead]
            out[:, cols] = total
            return
        left = count - s

        def add(i, carry):
            sub = [lax.rem(i // (1 << (left - 1 - j)), 2) for j in range(left)]
            it = iter(sub)
            at = (*(next(it) if isinstance(b, slice) else b for b in keep), slice(None), cols)
            ref[at] = (ref[at].astype(F32) + got[tuple(sub)].astype(F32)).astype(BF)
            return carry

        lax.fori_loop(0, 1 << left, add, 0)
        copy_of(c, s).start()

    queue = [(code // (count + 1), code % (count + 1)) for code in order] if order and count == 4 else sorted(
        ((c, s) for c in range(len(chunks)) for s in range(1, count + 1)), key=lambda cs: (cs[0] + LOOK * cs[1], cs[0]))
    share = list(plan) if plan and count == 4 else []
    open_chunks = set()

    def ready(names, mark=True, start=True):
        for c, (name, lead, lo, _) in enumerate(chunks):
            if (name, lead, lo) in names:
                if start:
                    copy_of(c, 0).start()
                if mark:
                    open_chunks.add(c)

    def due():
        batch = []
        for _ in range(share.pop(0) if share else 2):
            if queue and queue[0][0] in open_chunks:
                batch.append(queue.pop(0))
        return batch

    def advance():
        for item in due():
            run(item)

    def paced(steps, body):
        paced_loop(steps, body, [due() for _ in range(steps)], run)

    tiles = lambda name, total, lead=None, at=0: {(name, lead, lo) for lo in range(at, at + total, size)}
    ready(tiles("down", hidden))
    loads["gdown"].wait()
    sums[0] = jnp.zeros_like(sums[0])
    pos[...] = lax.broadcasted_iota(jnp.int32, pos.shape, 0).astype(F32)

    def whole(ref, h=None, cols=slice(None)):
        return ref[:, cols] if h is None else ref[span(h, model // 2), cols]

    loads["u"].wait()
    loads["down"].wait()
    half = model // 2

    def lowered(who, h):
        return dot_nt(big[who].reshape(local, hidden), whole(wide, h))

    def partner_lowered(h):
        part[0:local, span(h, half)] = lowered(other, h).astype(BF)

    paced(2, partner_lowered)
    first = mesh_copy(part.at[pl.ds(0, local)], first_r, psend.at[0], precv.at[0], device_id={"tensor": other})
    first.start()

    loads["cot"].wait()
    loads["gp"].wait()
    for j in range(hidden // TILE):
        cols = slice(j * TILE, (j + 1) * TILE)

        def grad_pre(i, rows, cols=cols):
            value = (dot_nn(cot[rows, :], whole(wide, cols=cols)) * gp[rows, cols].astype(F32)).astype(BF)
            gp[rows, cols] = value
            line = 8 + cols.start // model
            at = slice(cols.start % model, cols.start % model + TILE)
            sums[0, line : line + 1, at] += jnp.sum(value.astype(F32), axis=0, keepdims=True)

        paced(tokens // 256, lambda i: grad_pre(i, span(i, 256)))

    loads["x2"].wait()
    first.wait_recv()

    def own_lowered(h):
        cols = span(h, half)
        mid = x2[rows_of(t, 0, local), cols]
        layer_o[:, cols] = (mid + (lowered(t, h) + first_r[:, cols].astype(F32)) + table[5:6, cols]).astype(BF)

    paced(2, own_lowered)
    load("qkv", qkv_h.at[0], wide.at[:, pl.ds(0, width)])
    load("qkv1", qkv_h.at[1], wide.at[:, pl.ds(width, width)])
    load("qkv2", qkv_h.at[2], wide.at[:, pl.ds(2 * width, width)])
    load("proj", proj_h, wide.at[:, pl.ds(3 * width, width)])

    loads["a2"].wait()
    loads["up"].wait()
    first.wait_send()
    part_copies = []
    for h in range(2):
        rows = pl.ds(h * local, local)

        def back_up(e, rows=rows):
            part[rows, span(e, half)] = dot_nt(gp[rows, :], whole(up_w, e)).astype(BF)

        paced(2, back_up)
        copy = mesh_copy(part.at[rows], part_r.at[rows], psend.at[1 + h], precv.at[1 + h], device_id={"tensor": other})
        copy.start()
        part_copies.append(copy)
    for name, src, dst in (("q", q_h, q), ("k", k_h, k), ("v", v_h, v), ("o", o_h, o)):
        load(name, src, dst)
    for j in range(hidden // TILE):
        cols = slice(j * TILE, (j + 1) * TILE)

        def sum_up(h, carry, cols=cols):
            value = dot_tn(a1[:, span(h, half)], gp[:, cols]).astype(BF)
            big[(h, Ellipsis, cols)] = value.reshape(*big.shape[1:-1], TILE)
            return carry

        lax.fori_loop(0, 2, sum_up, 0)
        ready(tiles("up", TILE, at=j * TILE))
        advance()
    load("a1", a1_h, a1)

    def norm_parts(value):
        center = value - jnp.mean(value, axis=-1, keepdims=True)
        inverse = lax.rsqrt(jnp.mean(center * center, axis=-1, keepdims=True) + epsilon)
        return center * inverse, inverse

    def norm_back(grad, normed, inverse, gain):
        scaled = grad * gain
        return inverse * (scaled - jnp.mean(scaled, axis=-1, keepdims=True) - normed * jnp.mean(scaled * normed, axis=-1, keepdims=True))

    def add_sum(line, value):
        sums[0, line : line + 1, :] += jnp.sum(value, axis=0, keepdims=True)

    for copy in part_copies:
        copy.wait_recv()
    for who, count_it in ((t, True), (other, False)):

        def through(i, who=who, count_it=count_it):
            rows = rows_of(who, i, 128)
            grad = part[rows, :].astype(F32) + part_r[rows, :].astype(F32)
            normed, inverse = norm_parts(x2[rows, :])
            outer = cot[rows, :].astype(F32)
            mid = outer + norm_back(grad, normed, inverse, table[1:2, :])
            x2[rows, :] = mid
            cot[rows, :] = mid.astype(BF)
            if count_it:
                add_sum(1, grad * normed)
                add_sum(3, mid)
                add_sum(4, grad)
                add_sum(5, outer)

        paced(local // 128, through)
    gx2 = cot

    loads["proj"].wait()
    loads["o"].wait()
    proj_cols = slice(3 * width, 4 * width)

    def sum_proj(h, carry):
        gproj[h] = dot_tn(gx2[:, span(h, half)], o[...]).astype(BF).reshape(gproj.shape[1:])
        return carry

    lax.fori_loop(0, 2, sum_proj, 0)
    ready(tiles("proj", width))
    advance()

    def through_proj(i, rows):
        do[rows, :] = dot_nn(gx2[rows, :], whole(wide, cols=proj_cols)).astype(BF)

    paced(tokens // TILE, lambda i: through_proj(i, span(i, TILE)))
    for name in ("q", "k", "v", "lse"):
        loads[name].wait()

    def turn_keys(i, rows):
        kt[:, rows] = k[rows, :].astype(F32).T.astype(BF)

    rows_loop(tokens, TILE, turn_keys)

    blocks = tokens // QB
    lane_half = lax.broadcasted_iota(jnp.int32, (QB, 2 * HD), 1) // HD

    group = width // 2

    def group_names(g):
        return {("qkv", c, lo) for c in range(3) for lo in range(g * group, (g + 1) * group, size)}

    def group_grads(g):
        cols = slice(g * group, (g + 1) * group)

        def turn(i, rows):
            dq[rows, cols] = dqt[cols, rows].astype(F32).T.astype(BF)

        rows_loop(tokens, TILE, turn)
        for c, ref in ((1, dk), (2, dv), (0, dq)):

            def sum_qkv(h, carry, c=c, ref=ref):
                gqkv[(c, h, Ellipsis, cols)] = dot_tn(a1[:, span(h, half)], ref[:, cols]).astype(BF).reshape(*gqkv.shape[2:-1], group)
                return carry

            lax.fori_loop(0, 2, sum_qkv, 0)

    def head_step(h):
        @pl.when(h == heads // 2)
        def _():
            group_grads(0)
            ready(group_names(0), mark=False)

        cols = span(h // 2, 2 * HD)
        head_rows = span(h, HD)
        side = lax.rem(h, 2)
        slope = slopes[h]

        @pl.when(side == 0)
        def _():
            acc_k[...] = jnp.zeros_like(acc_k)
            acc_v[...] = jnp.zeros_like(acc_v)

        for b in range(blocks):
            end = (b + 1) * QB
            rows = slice(b * QB, end)
            zero = jnp.zeros((QB, 2 * HD), BF)
            query = jnp.where(lane_half == side, q[rows, cols], zero)
            outer = jnp.where(lane_half == side, do[rows, cols], zero)
            bias = pos[0:end, :] * slope
            bias = jnp.concatenate([bias] * (QB // bias.shape[1]), axis=1)
            scores = dot_nt(k[0:end, cols], query) + bias - lse[pl.ds(h, 1), rows]
            keep = lax.broadcasted_iota(jnp.int32, (QB, QB), 0) <= lax.broadcasted_iota(jnp.int32, (QB, QB), 1)
            diag = jnp.where(keep, scores[b * QB : end, :], -1e30)
            scores = diag if b == 0 else jnp.concatenate([scores[0 : b * QB, :], diag], axis=0)
            probs = jnp.exp(scores)
            acc_v[0:end, :] += dot_nn(probs.astype(BF), outer)
            grad = dot_nt(v[0:end, cols], outer)
            inner = jnp.sum(probs * grad, axis=0, keepdims=True)
            low = (probs * (grad - inner)).astype(BF)
            acc_k[0:end, :] += dot_nn(low, query)
            dqt[head_rows, rows] = (dot_nn(kt[head_rows, 0:end], low) * HD ** (-0.5)).astype(BF)

        @pl.when(side == 1)
        def _():
            dk[:, cols] = acc_k[...].astype(BF)
            dv[:, cols] = acc_v[...].astype(BF)

    loads["a1"].wait()
    batches = [due() for _ in range(heads // 2 + 1)]
    ready(group_names(0), start=False)
    paced_loop(heads, head_step, batches + [due() for _ in range(heads // 2 - 1)], run)
    group_grads(1)
    ready(group_names(1))
    advance()
    for at, ref in ((0, dq), (width, dv)):
        sums[0, 10:11, at : at + width] = jnp.sum(ref[...].astype(F32), axis=0, keepdims=True)

    for name in ("qkv", "qkv1", "qkv2"):
        loads[name].wait()

    def back_one(rows):
        total = dot_nt(dq[rows, :], whole(wide, cols=slice(0, width)))
        total += dot_nt(dk[rows, :], whole(wide, cols=slice(width, 2 * width)))
        return total + dot_nt(dv[rows, :], whole(wide, cols=slice(2 * width, 3 * width)))

    for copy in part_copies:
        copy.wait_send()

    def partner_rows(i):
        part[span(i, 256), :] = back_one(rows_of(other, i, 256)).astype(BF)

    paced(local // 256, partner_rows)
    last = mesh_copy(part.at[pl.ds(0, local)], last_r, psend.at[3], precv.at[3], device_id={"tensor": other})
    last.start()
    advance()
    loads["x"].wait()
    last.wait_recv()

    def own_rows(i):
        rows = rows_of(t, i, 256)
        here = span(i, 256)
        grad = back_one(rows) + last_r[here, :].astype(F32)
        normed, inverse = norm_parts(x_f[here, :].astype(F32))
        grad_o[here, :] = x2[rows, :] + norm_back(grad, normed, inverse, table[0:1, :])
        add_sum(0, grad * normed)
        add_sum(2, grad)

    paced(local // 256, own_rows)

    def sum_step(s):
        to = {"dp": partner_of(me, mine, s)} if s < count else {"tensor": other}
        return mesh_copy(sums.at[s], sland.at[s], vsend.at[s], vrecv.at[s], device_id=to)

    sum_copies = [sum_step(s) for s in range(count + 1)]
    sum_copies[0].start()
    for s in range(count):
        advance()
        sum_copies[s].wait_recv()
        sums[s + 1] = sums[s] + sland[s]
        sum_copies[s + 1].start()
    while queue:
        run(queue.pop(0))
    sum_copies[count].wait_recv()
    sums_o[0:8, :] = sums[count, 0:8] + sland[count, 0:8]
    sums_o[8:16, :] = sums[count, 8:16]
    for c in range(len(chunks)):
        for s in range(count):
            copy_of(c, s).wait_send()
    for copy in sum_copies + [last]:
        copy.wait_send()


def backward_all(slopes, table, x, cot, a1, q, k, v, o, lse, x2, a2, u, gp, gdown, qkv_w, proj_w, up_w, down_w, n, width=256):
    count = n.bit_length() - 1
    two = (2,) * count
    tokens, model = cot.shape
    inner, hidden = q.shape[1], gp.shape[1]
    heads = inner // HD
    r = model // n
    chunks = [("down", None, lo, width) for lo in range(0, hidden, width)]
    chunks += [("up", None, lo, width) for lo in range(0, hidden, width)]
    chunks += [("proj", None, lo, width) for lo in range(0, inner, width)]
    chunks += [("qkv", c, lo, width) for lo in range(0, inner, width) for c in (1, 2, 0)]
    f = lambda *s: jax.ShapeDtypeStruct(s, F32)
    outs = (jax.ShapeDtypeStruct(x.shape, BF), f(*x.shape), f(3, r, inner), f(r, inner), f(r, hidden), f(r, hidden), f(16, model))
    vm = lambda *s, d=BF: pltpu.VMEM(s, d)
    scratch = [vm(len(chunks), *two[: count - 1 - s], r, width) for s in range(count)]
    scratch += [vm(count + 1, 16, model, d=F32), vm(count + 1, 16, model, d=F32), vm(*x.shape), vm(tokens, model), vm(tokens, model)]
    scratch += [vm(heads, tokens, d=F32), vm(tokens, model, d=F32), vm(tokens, hidden)]
    scratch += [vm(*two, r, hidden), vm(*two, r, hidden), vm(*two, r, inner), vm(3, *two, r, inner), vm(model, hidden), vm(model, hidden)]
    scratch += [vm(tokens, model), vm(tokens, model), vm(*x.shape), vm(*x.shape), vm(inner, tokens), vm(inner, tokens)]
    scratch += [vm(tokens, 2 * HD, d=F32)] * 2 + [vm(tokens, 128, d=F32)]
    sems = lambda m: pltpu.SemaphoreType.DMA((m,))
    m = len(chunks) * count
    scratch += [sems(m), sems(m), sems(count + 1), sems(count + 1), sems(4), sems(4), sems(20)]
    flat = lambda a: a.reshape(*a.shape[: a.ndim - count - 2], model, a.shape[-1])
    by_block = lambda a: a.reshape(*two, r, a.shape[-1])

    def body(slopes_ref, table_ref, *refs):
        backward_kernel(count, chunks, SCATTER_MODES, SCATTER_ORDER, SCATTER_PLAN, slopes_ref, table_ref, refs[:17], refs[17 : 17 + len(outs)], refs[17 + len(outs) :])

    return pl.pallas_call(
        body, out_shape=outs, in_specs=[pl.BlockSpec(memory_space=pltpu.SMEM), VM] + [ANY] * 17, out_specs=[VM] * len(outs), scratch_shapes=scratch,
        compiler_params=pltpu.CompilerParams(collective_id=1, has_side_effects=True, vmem_limit_bytes=67043328), name="backward_all",
    )(slopes, table, x, cot, a1, q, k, v, o, lse, x2, a2, by_block(u), gp, by_block(gdown), flat(qkv_w), flat(proj_w), flat(up_w), flat(down_w))

def finish_kernel(count, *refs):
    ins, outs, bufs = refs[:count], refs[count : 2 * count], refs[2 * count : 3 * count]
    in_sem, out_sem = refs[3 * count :]
    reads = [pltpu.make_async_copy(a, b, in_sem.at[i]) for i, (a, b) in enumerate(zip(ins, bufs))]
    writes = [pltpu.make_async_copy(b, c, out_sem.at[i]) for i, (b, c) in enumerate(zip(bufs, outs))]
    for copy in reads:
        copy.start()
    for read, write in zip(reads, writes):
        read.wait()
        write.start()
    for copy in writes:
        copy.wait()


def finish(arrays):
    count = len(arrays)
    return pl.pallas_call(
        functools.partial(finish_kernel, count), out_shape=tuple(jax.ShapeDtypeStruct(a.shape, a.dtype) for a in arrays),
        in_specs=[ANY] * count, out_specs=[ANY] * count,
        scratch_shapes=[pltpu.VMEM(a.shape, a.dtype) for a in arrays] + [pltpu.SemaphoreType.DMA((count,))] * 2, name="finish")(*arrays)


def on_device(layer_in, w_qkv, b_qv, w_proj, w_ff1, b_ff1, w_ff2, norm_gains, add_biases, cotangent):
    n = lax.axis_size("dp")
    i = lax.axis_index("dp")
    t = lax.axis_index("tensor")
    width = w_qkv.shape[2]
    model = layer_in.shape[1]
    hidden = w_ff1.shape[1]
    heads = b_qv.shape[1]
    part = norm_gains.shape[1]
    zero = jnp.int32(0)
    put = lambda shape, a, at: lax.dynamic_update_slice(jnp.zeros(shape, F32), a.astype(F32), at)
    up_grid = (b_ff1.shape[0], n * b_ff1.shape[1])
    qv_grid = (*b_qv.shape[:2], n * b_qv.shape[2])
    small = jnp.concatenate([
        put((8, model), jnp.concatenate([norm_gains, add_biases]), (zero, (2 * i + t) * part)),
        put(up_grid, b_ff1, (zero, i * b_ff1.shape[1])).reshape(-1, model),
        put(qv_grid, b_qv, (zero, zero, i * b_qv.shape[2])).reshape(-1, model),
        jnp.zeros((8 - (hidden + 2 * width) // model, model), F32)])
    slopes = 2.0 ** (-8.0 * (t * heads + jnp.arange(heads, dtype=jnp.int32) + 1).astype(F32) / H)
    (qkv_w, proj_w, up_w, down_w, vectors, cot, a1, q, k, v, o, lse, x2, a2, u, rise, grad_down) = forward_all(
        slopes, w_qkv, w_proj.T, w_ff1, w_ff2.T, small, layer_in, cotangent, n)
    layer_out, grad_in, out_qkv, out_proj, out_up, out_down, sums = backward_all(
        slopes, vectors, layer_in, cot, a1, q, k, v, o, lse, x2, a2, u, rise, grad_down, qkv_w, proj_w, up_w, down_w, n)
    layer_out, grad_in, out_qkv, out_proj, out_up, out_down, sums = finish(
        (layer_out, grad_in, out_qkv, out_proj, out_up, out_down, sums))
    own = lax.dynamic_slice(sums, (zero, (2 * i + t) * part), (6, part))
    up_sums = lax.dynamic_slice_in_dim(sums[8 : 8 + hidden // model].reshape(up_grid), i * b_ff1.shape[1], b_ff1.shape[1], 1)
    qv_sums = lax.dynamic_slice_in_dim(sums[10].reshape(qv_grid), i * b_qv.shape[2], b_qv.shape[2], 2)
    return (layer_out, grad_in, out_qkv, qv_sums, out_proj.T, out_up, up_sums, out_down.T, own[:2], own[2:])


def solution(mesh):
    rows, cols = P(("dp", "tensor"), None), P(None, ("dp", "tensor"))
    return jax.shard_map(
        on_device,
        mesh=mesh,
        in_specs=(rows, P(None, "dp", "tensor"), P(None, "tensor", "dp"), P("tensor", "dp"), P("dp", "tensor"),
                  P("tensor", "dp"), P("tensor", "dp"), cols, cols, rows),
        out_specs=(rows, rows, P(None, "dp", "tensor"), P(None, "tensor", "dp"), P("tensor", "dp"), P("dp", "tensor"),
                   P("tensor", "dp"), P("tensor", "dp"), cols, cols),
        check_vma=False,
    )
```

```python
import functools
import math
import jax
import jax.numpy as jnp
from jax import lax
from jax.experimental import pallas as pl
from jax.experimental.pallas import tpu as pltpu
from jax.sharding import PartitionSpec as P

MESH = pl.DeviceIdType.MESH
ANY = pl.BlockSpec(memory_space=pl.ANY)
VM = pl.BlockSpec(memory_space=pltpu.VMEM)


def bits_of(index, count):
    return [lax.rem(index // (1 << b), 2) for b in range(count)]


def partner_of(index, mine, b):
    return index + (1 - 2 * mine[b]) * (1 << b)


def halving_orders(count):
    return [[(start + i) % count for i in range(count)] for start in range(3)]


def enter(index, mine, count, other):
    barrier = pltpu.get_barrier_semaphore()
    for b in range(count):
        pl.semaphore_signal(barrier, inc=1, device_id={"dp": partner_of(index, mine, b)}, device_id_type=MESH)
    pl.semaphore_signal(barrier, inc=1, device_id={"tensor": other}, device_id_type=MESH)
    pl.semaphore_wait(barrier, count + 1)


def block_index(mine, held, count):
    return tuple(slice(None) if b in held else mine[b] for b in reversed(range(count)))

SEQ_LEN = 1024
HD = 64
H = 16
epsilon = 1e-05
gelu_scale = 0.7978845608028654
F32 = jnp.float32
BF = jnp.bfloat16
TILE = 512
QB = 256
LOOK = 4


def bit_orders(count, modes, total, flip):
    if modes and count == 4:
        return [[mode // 10**i % 10 for i in (3, 2, 1, 0)] for mode in modes]
    cyclic = [[(start + i) % count for i in range(count)] for start in (0, 1, 0, 1, 0, 1, 0, 2)]
    return [(order[::-1] if flip else order) for order in (cyclic[c % len(cyclic)] for c in range(total))]


def dot_nn(a, b):
    return lax.dot_general(a, b, (((1,), (0,)), ((), ())), preferred_element_type=F32)


def dot_nt(a, b):
    return lax.dot_general(a, b, (((1,), (1,)), ((), ())), preferred_element_type=F32)


def dot_tn(a, b):
    return lax.dot_general(a, b, (((0,), (0,)), ((), ())), preferred_element_type=F32)


def span(i, size):
    return pl.ds(pl.multiple_of(i * size, size), size)


def paced_loop(steps, body, batches, run):
    def step(i, carry):
        for j in range(steps):
            if batches[j]:

                @pl.when(i == j)
                def _():
                    for item in batches[j]:
                        run(item)

        body(i)
        return carry

    lax.fori_loop(0, steps, step, 0)


def rows_loop(total, size, body):
    def step(i, carry):
        body(i, span(i, size))
        return carry

    lax.fori_loop(0, total // size, step, 0)


def forward_kernel(count, chunks, modes, order, plan, refs_in, refs_out, scratch, slopes):
    (qkv, proj, up, down, small, x, cot) = refs_in
    (qkv_o, proj_o, up_o, down_o, vec_o, cot_o, a1_o, q_o, k_o, v_o, o_o, lse_o, x2_o, a2_o, u_o, gp_o, gdown_o) = refs_out
    (qkv_w, proj_w, up_w, down_w, vec, vland, x_f, cot_f, a1, q, k, v, vt, ot, o, lse, part, part_r, x2, a2, u, gp, gdown, pos,
     send, recv, vsend, vrecv, psend, precv, own_sem, out_sem) = scratch
    me = lax.axis_index("dp")
    t = lax.axis_index("tensor")
    other = 1 - t
    mine = bits_of(me, count)
    orders = bit_orders(count, modes, len(chunks), True)
    full = block_index(mine, (), count)
    tokens, model = x_f.shape
    width = q.shape[1]
    hidden = u.shape[1]
    heads = width // HD
    local_rows = x.shape[0]
    mesh_copy = functools.partial(pltpu.make_async_remote_copy, device_id_type=MESH)

    enter(me, mine, count, other)
    waits = []

    def vec_step(s):
        to = {"dp": partner_of(me, mine, s)} if s < count else {"tensor": other}
        return mesh_copy(small if s == 0 else vec.at[s], vland.at[s], vsend.at[s], vrecv.at[s], device_id=to)

    vec[0] = small[...]
    vec_copies = [vec_step(s) for s in range(count + 1)]
    vec_copies[0].start()

    mine_rows = pl.ds(t * local_rows, local_rows)
    pair_copies = [mesh_copy(src, dst.at[mine_rows], psend.at[i], precv.at[i], device_id={"tensor": other})
                   for i, (src, dst) in enumerate(((x, x_f), (cot, cot_f)))]
    for copy in pair_copies:
        copy.start()

    names = {"qkv": (qkv, qkv_w), "proj": (proj, proj_w), "up": (up, up_w), "down": (down, down_w)}

    def views(c):
        name, lead, lo, size = chunks[c]
        src, dst = names[name]
        if lead is not None:
            src, dst = src.at[lead], dst.at[lead]
        return src.at[:, pl.ds(lo, size)], dst, (slice(None), pl.ds(lo, size))

    def copy_of(c, s):
        order = orders[c]
        src, dst, tail = views(c)
        at = (*block_index(mine, order[:s], count), *tail)
        return mesh_copy(src if s == 0 else dst.at[at], dst.at[at], send.at[c * count + s], recv.at[c * count + s],
                         device_id={"dp": partner_of(me, mine, order[s])})

    owns = [pltpu.make_async_copy(src, dst.at[full], own_sem.at[i]) for i, (src, dst) in enumerate(
        [(qkv.at[c], qkv_w.at[c]) for c in range(3)] + [(proj, proj_w), (up, up_w), (down, down_w)])]
    owns += [pltpu.make_async_copy(src, dst.at[mine_rows], own_sem.at[6 + i]) for i, (src, dst) in enumerate(((x, x_f), (cot, cot_f)))]
    for copy in owns:
        copy.start()
    for copy in owns:
        copy.wait()

    queue = [divmod(code, count) for code in order] if order and count == 4 else sorted(
        ((c, s) for c in range(len(chunks)) for s in range(count)), key=lambda cs: (cs[0] + LOOK * cs[1], cs[0]))
    share = list(plan) if plan and count == 4 else []
    done = set()

    def run(item):
        c, s = item
        if s > 0:
            copy_of(c, s - 1).wait_recv()
        copy_of(c, s).start()

    def settle(c):
        if c not in done:
            while any(item[0] == c for item in queue):
                run(queue.pop(0))
            copy_of(c, count - 1).wait_recv()
            done.add(c)

    def due():
        size = share.pop(0) if share else 2
        batch, queue[:] = queue[:size], queue[size:]
        return batch

    def advance():
        for item in due():
            run(item)

    def paced(steps, body):
        paced_loop(steps, body, [due() for _ in range(steps)], run)

    outs = []

    def emit(src, dst):
        copy = pltpu.make_async_copy(src, dst, out_sem.at[len(outs)])
        copy.start()
        outs.append(copy)

    advance()
    for s in range(count):
        vec_copies[s].wait_recv()
        vec[s + 1] = vec[s] + vland[s]
        vec_copies[s + 1].start()
        advance()
    for copy in pair_copies:
        copy.wait_recv()
    emit(cot_f, cot_o)
    vec_copies[count].wait_recv()
    vec[count + 1, 0:8] = vec[count, 0:8] + vland[count, 0:8]
    vec[count + 1, 8:16] = vec[count, 8:16]
    emit(vec.at[count + 1], vec_o)
    table = vec.at[count + 1]

    def normed(rows_value, gain, shift):
        center = rows_value - jnp.mean(rows_value, axis=-1, keepdims=True)
        spread = jnp.mean(center * center, axis=-1, keepdims=True)
        return (center * lax.rsqrt(spread + epsilon)) * gain + shift

    def norm_one(i, rows):
        a1[rows, :] = normed(x_f[rows, :].astype(F32), table[0:1, :], table[2:3, :]).astype(BF)

    pos[...] = lax.broadcasted_iota(jnp.int32, pos.shape, 0).astype(F32)
    paced(4, lambda i: norm_one(i, span(i, tokens // 4)))
    emit(a1, a1_o)

    for c, dst in ((1, k), (0, q), (2, v)):
        for i, chunk in enumerate(chunks):
            if chunk[0] == "qkv" and chunk[1] == c:
                settle(i)

        def mix(i, rows, c=c, dst=dst):
            value = dot_nn(a1[rows, :], qkv_w[c].reshape(model, width))
            if c == 0:
                value = (value + table[10:11, 0:width]).astype(BF).astype(F32) * HD ** (-0.5)
            if c == 2:
                value = value + table[10:11, width : 2 * width]
            dst[rows, :] = value.astype(BF)
            if c == 2:
                vt[:, rows] = value.T.astype(BF)

        paced(2, lambda i: mix(i, span(i, tokens // 2)))
    for src, dst in ((q, q_o), (k, k_o), (v, v_o), (qkv_w, qkv_o)):
        emit(src, dst)

    blocks = tokens // QB
    lane_half = lax.broadcasted_iota(jnp.int32, (QB, 2 * HD), 1) // HD

    def head_step(h):
        cols = span(h // 2, 2 * HD)
        slope = slopes[h]
        head_rows = span(h, HD)
        for b in range(blocks):
            end = (b + 1) * QB
            query = jnp.where(lane_half == lax.rem(h, 2), q[b * QB : end, cols], jnp.zeros((QB, 2 * HD), BF))
            bias = pos[0:end, :] * slope
            bias = jnp.concatenate([bias] * (QB // bias.shape[1]), axis=1)
            scores = dot_nt(k[0:end, cols], query) + bias
            diag = scores[b * QB : end, :]
            keep = lax.broadcasted_iota(jnp.int32, (QB, QB), 0) <= lax.broadcasted_iota(jnp.int32, (QB, QB), 1)
            diag = jnp.where(keep, diag, -1e30)
            scores = diag if b == 0 else jnp.concatenate([scores[0 : b * QB, :], diag], axis=0)
            peak = jnp.max(scores, axis=0, keepdims=True)
            weights = jnp.exp(scores - peak)
            total = jnp.sum(weights, axis=0, keepdims=True)
            out = dot_nn(vt[head_rows, 0:end], weights.astype(BF))
            ot[head_rows, b * QB : end] = (out / total).astype(BF)
            lse[pl.ds(h, 1), b * QB : end] = peak + jnp.log(total)

    paced(heads, head_step)
    for i, chunk in enumerate(chunks):
        if chunk[0] == "proj":
            settle(i)

    def turn(i, rows):
        o[rows, :] = ot[:, rows].astype(F32).T.astype(BF)

    rows_loop(tokens, TILE, turn)
    emit(o, o_o)
    emit(lse, lse_o)
    emit(proj_w, proj_o)

    def project(i, rows):
        part[rows, :] = dot_nt(o[rows, :], proj_w[...].reshape(model, width)).astype(BF)

    half = tokens // 2
    part_copies = []
    for j in range(2):
        project(j, pl.ds(j * half, half))
        copy = mesh_copy(part.at[pl.ds(j * half, half)], part_r.at[pl.ds(j * half, half)], psend.at[2 + j], precv.at[2 + j],
                         device_id={"tensor": other})
        copy.start()
        part_copies.append(copy)
        advance()
    for j in range(2):
        part_copies[j].wait_recv()

        def norm_two(i, j=j):
            rows = pl.ds(pl.multiple_of(j * half + i * 256, 256), 256)
            middle = x_f[rows, :].astype(F32) + (part[rows, :].astype(F32) + part_r[rows, :].astype(F32)) + table[3:4, :]
            x2[rows, :] = middle
            a2[rows, :] = normed(middle, table[1:2, :], table[4:5, :]).astype(BF)

        paced(half // 256, norm_two)
    emit(x2, x2_o)
    emit(a2, a2_o)

    for j in range(hidden // TILE):
        cols = pl.ds(j * TILE, TILE)
        for i, chunk in enumerate(chunks):
            if chunk[0] == "up" and j * TILE <= chunk[2] < (j + 1) * TILE:
                settle(i)

        row = 8 + j * TILE // model
        bias_at = j * TILE % model

        def expand(i, rows, cols=cols, row=row, bias_at=bias_at):
            pre = dot_nn(a2[rows, :], up_w[..., cols].reshape(model, TILE)) + table[row : row + 1, bias_at : bias_at + TILE]
            square = pre * pre
            bent = jnp.tanh(pre * (gelu_scale + (gelu_scale * 0.044715) * square))
            rise = 0.5 + 0.5 * bent
            u[rows, cols] = (pre * rise).astype(BF)
            slope = 0.5 * pre * (1.0 - bent * bent) * (gelu_scale + (3 * 0.044715 * gelu_scale) * square)
            gp[rows, cols] = (rise + slope).astype(BF)

        paced(tokens // 256, lambda i: expand(i, span(i, 256)))

        def sum_down(i, rows, cols=cols):
            gdown[rows, cols] = dot_tn(cot_f[:, rows], u[:, cols]).astype(BF)

        paced(model // TILE, lambda i: sum_down(i, span(i, TILE)))
        for src, dst in ((u, u_o), (gp, gp_o), (gdown, gdown_o)):
            emit(src.at[:, cols], dst.at[:, cols])
        emit(up_w.at[(Ellipsis, cols)], up_o.at[(Ellipsis, cols)])
    for i, (name, lead, lo, size) in enumerate(chunks):
        settle(i)
        if name == "down":
            emit(down_w.at[(Ellipsis, pl.ds(lo, size))], down_o.at[(Ellipsis, pl.ds(lo, size))])
    for c in range(len(chunks)):
        for s in range(count):
            copy_of(c, s).wait_send()
    for copy in vec_copies + pair_copies + part_copies:
        copy.wait_send()
    for copy in outs:
        copy.wait()


GATHER_MODES = (
    3201, 1320, 3210, 2130, 2301, 3201, 3021, 1320, 3021, 3201, 3021, 1230, 2310, 3012, 3201, 1230, 3120, 2031, 1032, 2031, 321, 1230,
    3210, 213,
)
GATHER_ORDER = (
    16, 8, 20, 68, 17, 12, 9, 69, 40, 4, 21, 13, 0, 5, 70, 10, 18, 48, 36, 41, 14, 22, 84, 1, 28, 11, 19, 24, 6, 85, 42, 29, 49, 23,
    32, 71, 44, 2, 37, 52, 64, 60, 7, 3, 86, 15, 25, 43, 30, 56, 76, 45, 88, 61, 38, 50, 92, 33, 53, 72, 65, 26, 31, 80, 39, 77, 93,
    46, 87, 34, 57, 54, 62, 89, 51, 73, 27, 66, 94, 81, 78, 47, 35, 58, 55, 63, 90, 67, 74, 82, 95, 79, 59, 91, 75, 83,
)
GATHER_PLAN = (
    41, 2, 3, 2, 2, 7, 0, 1, 0, 4, 0, 0, 1, 2, 2, 0, 4, 3, 3, 2, 1, 2, 1, 5, 0, 3, 1, 0, 0, 0, 0, 0, 1, 0, 1, 0, 0, 0, 1, 0, 0, 1, 0,
    0, 0, 0, 0, 0, 0, 0, 0, 0, 0,
)


def forward_all(slopes, qkv, proj, up, down, small, x, cot, n, width=256):
    count = n.bit_length() - 1
    two = (2,) * count
    chunks = []
    for c in (1, 0, 2):
        chunks += [("qkv", c, lo, width) for lo in range(0, qkv.shape[2], width)]
    for name, a in (("proj", proj), ("up", up), ("down", down)):
        chunks += [(name, None, lo, width) for lo in range(0, a.shape[1], width)]
    tokens, model = 2 * x.shape[0], x.shape[1]
    inner, hidden = qkv.shape[2], up.shape[1]
    heads = inner // HD
    weights = [((3, *two, *qkv.shape[1:]), BF), ((*two, *proj.shape), BF), ((*two, *up.shape), BF), ((*two, *down.shape), BF)]
    shapes = weights + [((16, model), F32), ((tokens, model), BF), ((tokens, model), BF)] + [((tokens, inner), BF)] * 4
    shapes += [((heads, tokens), F32), ((tokens, model), F32), ((tokens, model), BF), ((tokens, hidden), BF), ((tokens, hidden), BF), ((model, hidden), BF)]
    vm = lambda s, d: pltpu.VMEM(s, d)
    scratch = [vm(*w) for w in weights]
    scratch += [vm((count + 2, 16, model), F32), vm((count + 1, 16, model), F32), vm((tokens, model), BF), vm((tokens, model), BF), vm((tokens, model), BF)]
    scratch += [vm((tokens, inner), BF)] * 3 + [vm((inner, tokens), BF)] * 2 + [vm((tokens, inner), BF), vm((heads, tokens), F32)]
    scratch += [vm((tokens, model), BF)] * 2 + [vm((tokens, model), F32), vm((tokens, model), BF), vm((tokens, hidden), BF), vm((tokens, hidden), BF), vm((model, hidden), BF)]
    scratch += [vm((tokens, 128), F32)]
    sems = lambda k: pltpu.SemaphoreType.DMA((k,))
    k = len(chunks) * count
    scratch += [sems(k), sems(k), sems(count + 1), sems(count + 1), sems(4), sems(4), sems(8), sems(64)]

    def body(slopes_ref, *refs):
        forward_kernel(count, chunks, GATHER_MODES, GATHER_ORDER, GATHER_PLAN, refs[:7], refs[7 : 7 + len(shapes)], refs[7 + len(shapes) :], slopes_ref)

    return pl.pallas_call(
        body, out_shape=tuple(jax.ShapeDtypeStruct(*s) for s in shapes),
        in_specs=[pl.BlockSpec(memory_space=pltpu.SMEM)] + [VM] * 7, out_specs=[ANY] * len(shapes), scratch_shapes=scratch,
        compiler_params=pltpu.CompilerParams(collective_id=0, has_side_effects=True, vmem_limit_bytes=62 * 2**20), name="forward_all",
    )(slopes, qkv, proj, up, down, small, x, cot)

SCATTER_MODES = (
    1023, 2013, 231, 1320, 1023, 3021, 213, 3012, 1320, 213, 213, 3021, 1203, 1023, 1302, 1023, 132, 213, 132, 1032, 3120, 213, 1023,
    2013,
)
SCATTER_ORDER = (
    1, 11, 26, 31, 16, 21, 2, 27, 22, 12, 32, 46, 3, 61, 17, 28, 23, 81, 41, 56, 51, 66, 36, 47, 62, 86, 13, 18, 71, 76, 4, 24, 29,
    57, 67, 33, 96, 52, 82, 91, 37, 63, 6, 87, 42, 101, 106, 77, 19, 48, 68, 111, 14, 116, 97, 53, 92, 83, 7, 58, 38, 88, 34, 72, 112,
    107, 64, 102, 117, 43, 8, 59, 78, 49, 73, 108, 98, 118, 69, 84, 93, 44, 54, 89, 113, 103, 39, 99, 109, 119, 94, 74, 79, 104, 114,
    9,
)
SCATTER_PLAN = (
    0, 0, 0, 0, 0, 0, 0, 0, 0, 0, 0, 0, 0, 0, 0, 0, 0, 0, 0, 2, 0, 1, 2, 1, 1, 1, 1, 0, 0, 1, 0, 0, 0, 0, 0, 0, 1, 0, 0, 1, 3, 2, 4,
    1, 4, 5, 5, 5, 0, 1, 4, 4, 3, 3, 4, 7, 6,
)


def backward_kernel(count, chunks, modes, order, plan, slopes, table, refs_in, refs_out, scratch):
    (x_h, cot_h, a1_h, q_h, k_h, v_h, o_h, lse_h, x2_h, a2_h, u_h, gp_h, gdown_h, qkv_h, proj_h, up_h, down_h) = refs_in
    (layer_o, grad_o, gqkv_o, gproj_o, gup_o, gdown_o, sums_o) = refs_out
    landing = scratch[:count]
    (sums, sland, x_f, cot, a1, lse, x2, gp, big, gdown, gproj, gqkv, wide, up_w, part, part_r, first_r, last_r,
     kt, dqt, acc_k, acc_v, pos, send, recv, vsend, vrecv, psend, precv, in_sem) = scratch[count:]
    me = lax.axis_index("dp")
    t = lax.axis_index("tensor")
    other = 1 - t
    mine = bits_of(me, count)
    orders = bit_orders(count, modes, len(chunks), False)
    tokens, model = cot.shape
    width = q_h.shape[1]
    hidden = gp.shape[1]
    heads = width // HD
    local = tokens // 2
    q, k, v, o = (up_w.at[:, pl.ds(i * width, width)] for i in range(4))
    dq, dk, dv, do = q, k, v, o
    mesh_copy = functools.partial(pltpu.make_async_remote_copy, device_id_type=MESH)
    rows_of = lambda who, i, size: pl.ds(pl.multiple_of(who * local + i * size, size), size)

    enter(me, mine, count, other)
    loads = {}

    def load(name, src, dst):
        copy = pltpu.make_async_copy(src, dst, in_sem.at[len(loads)])
        copy.start()
        loads[name] = copy

    load("u", u_h, big)
    load("down", down_h, wide)
    load("gdown", gdown_h, gdown)
    load("cot", cot_h, cot)
    load("gp", gp_h, gp)
    load("x2", x2_h, x2)
    load("a2", a2_h, a1)
    load("up", up_h, up_w)
    load("lse", lse_h, lse)
    load("x", x_h, x_f)

    grads = {"qkv": gqkv, "proj": gproj, "up": big, "down": gdown}
    finals = {"qkv": gqkv_o, "proj": gproj_o, "up": gup_o, "down": gdown_o}
    size = chunks[0][3]

    def order_of(c):
        return orders[c]

    def held(c):
        name, lead, lo, _ = chunks[c]
        ref = grads[name]
        return ref if lead is None else ref.at[lead]

    def region(c, s, flip):
        order = order_of(c)
        at = []
        for b in reversed(range(count)):
            if b == order[s]:
                at.append(1 - mine[b] if flip else mine[b])
            else:
                at.append(mine[b] if b in order[:s] else slice(None))
        return tuple(at)

    def copy_of(c, s):
        name, lead, lo, _ = chunks[c]
        src = held(c)
        if name == "down" and s == 0:
            src = gdown_h
        at = (*region(c, s, True), slice(None), pl.ds(lo, size))
        return mesh_copy(src.at[at], landing[s].at[c], send.at[c * count + s], recv.at[c * count + s],
                         device_id={"dp": partner_of(me, mine, order_of(c)[s])})

    def run(item):
        c, s = item
        name, lead, lo, _ = chunks[c]
        copy_of(c, s - 1).wait_recv()
        got = landing[s - 1].at[c]
        keep = region(c, s - 1, False)
        cols = slice(lo, lo + size)
        ref = held(c)
        if s == count:
            total = ref[(*keep, slice(None), cols)].astype(F32) + got[...].astype(F32)
            out = finals[name]
            if lead is not None:
                out = out.at[lead]
            out[:, cols] = total
            return
        left = count - s

        def add(i, carry):
            sub = [lax.rem(i // (1 << (left - 1 - j)), 2) for j in range(left)]
            it = iter(sub)
            at = (*(next(it) if isinstance(b, slice) else b for b in keep), slice(None), cols)
            ref[at] = (ref[at].astype(F32) + got[tuple(sub)].astype(F32)).astype(BF)
            return carry

        lax.fori_loop(0, 1 << left, add, 0)
        copy_of(c, s).start()

    queue = [(code // (count + 1), code % (count + 1)) for code in order] if order and count == 4 else sorted(
        ((c, s) for c in range(len(chunks)) for s in range(1, count + 1)), key=lambda cs: (cs[0] + LOOK * cs[1], cs[0]))
    share = list(plan) if plan and count == 4 else []
    open_chunks = set()

    def ready(names, mark=True, start=True):
        for c, (name, lead, lo, _) in enumerate(chunks):
            if (name, lead, lo) in names:
                if start:
                    copy_of(c, 0).start()
                if mark:
                    open_chunks.add(c)

    def due():
        batch = []
        for _ in range(share.pop(0) if share else 2):
            if queue and queue[0][0] in open_chunks:
                batch.append(queue.pop(0))
        return batch

    def advance():
        for item in due():
            run(item)

    def paced(steps, body):
        paced_loop(steps, body, [due() for _ in range(steps)], run)

    tiles = lambda name, total, lead=None, at=0: {(name, lead, lo) for lo in range(at, at + total, size)}
    ready(tiles("down", hidden))
    loads["gdown"].wait()
    sums[0] = jnp.zeros_like(sums[0])
    pos[...] = lax.broadcasted_iota(jnp.int32, pos.shape, 0).astype(F32)

    def whole(ref, h=None, cols=slice(None)):
        return ref[:, cols] if h is None else ref[span(h, model // 2), cols]

    loads["u"].wait()
    loads["down"].wait()
    half = model // 2

    def lowered(who, h):
        return dot_nt(big[who].reshape(local, hidden), whole(wide, h))

    def partner_lowered(h):
        part[0:local, span(h, half)] = lowered(other, h).astype(BF)

    paced(2, partner_lowered)
    first = mesh_copy(part.at[pl.ds(0, local)], first_r, psend.at[0], precv.at[0], device_id={"tensor": other})
    first.start()

    loads["cot"].wait()
    loads["gp"].wait()
    for j in range(hidden // TILE):
        cols = slice(j * TILE, (j + 1) * TILE)

        def grad_pre(i, rows, cols=cols):
            value = (dot_nn(cot[rows, :], whole(wide, cols=cols)) * gp[rows, cols].astype(F32)).astype(BF)
            gp[rows, cols] = value
            line = 8 + cols.start // model
            at = slice(cols.start % model, cols.start % model + TILE)
            sums[0, line : line + 1, at] += jnp.sum(value.astype(F32), axis=0, keepdims=True)

        paced(tokens // 256, lambda i: grad_pre(i, span(i, 256)))

    loads["x2"].wait()
    first.wait_recv()

    def own_lowered(h):
        cols = span(h, half)
        mid = x2[rows_of(t, 0, local), cols]
        layer_o[:, cols] = (mid + (lowered(t, h) + first_r[:, cols].astype(F32)) + table[5:6, cols]).astype(BF)

    paced(2, own_lowered)
    load("qkv", qkv_h.at[0], wide.at[:, pl.ds(0, width)])
    load("qkv1", qkv_h.at[1], wide.at[:, pl.ds(width, width)])
    load("qkv2", qkv_h.at[2], wide.at[:, pl.ds(2 * width, width)])
    load("proj", proj_h, wide.at[:, pl.ds(3 * width, width)])

    loads["a2"].wait()
    loads["up"].wait()
    first.wait_send()
    part_copies = []
    for h in range(2):
        rows = pl.ds(h * local, local)

        def back_up(e, rows=rows):
            part[rows, span(e, half)] = dot_nt(gp[rows, :], whole(up_w, e)).astype(BF)

        paced(2, back_up)
        copy = mesh_copy(part.at[rows], part_r.at[rows], psend.at[1 + h], precv.at[1 + h], device_id={"tensor": other})
        copy.start()
        part_copies.append(copy)
    for name, src, dst in (("q", q_h, q), ("k", k_h, k), ("v", v_h, v), ("o", o_h, o)):
        load(name, src, dst)
    for j in range(hidden // TILE):
        cols = slice(j * TILE, (j + 1) * TILE)

        def sum_up(h, carry, cols=cols):
            value = dot_tn(a1[:, span(h, half)], gp[:, cols]).astype(BF)
            big[(h, Ellipsis, cols)] = value.reshape(*big.shape[1:-1], TILE)
            return carry

        lax.fori_loop(0, 2, sum_up, 0)
        ready(tiles("up", TILE, at=j * TILE))
        advance()
    load("a1", a1_h, a1)

    def norm_parts(value):
        center = value - jnp.mean(value, axis=-1, keepdims=True)
        inverse = lax.rsqrt(jnp.mean(center * center, axis=-1, keepdims=True) + epsilon)
        return center * inverse, inverse

    def norm_back(grad, normed, inverse, gain):
        scaled = grad * gain
        return inverse * (scaled - jnp.mean(scaled, axis=-1, keepdims=True) - normed * jnp.mean(scaled * normed, axis=-1, keepdims=True))

    def add_sum(line, value):
        sums[0, line : line + 1, :] += jnp.sum(value, axis=0, keepdims=True)

    for copy in part_copies:
        copy.wait_recv()
    for who, count_it in ((t, True), (other, False)):

        def through(i, who=who, count_it=count_it):
            rows = rows_of(who, i, 128)
            grad = part[rows, :].astype(F32) + part_r[rows, :].astype(F32)
            normed, inverse = norm_parts(x2[rows, :])
            outer = cot[rows, :].astype(F32)
            mid = outer + norm_back(grad, normed, inverse, table[1:2, :])
            x2[rows, :] = mid
            cot[rows, :] = mid.astype(BF)
            if count_it:
                add_sum(1, grad * normed)
                add_sum(3, mid)
                add_sum(4, grad)
                add_sum(5, outer)

        paced(local // 128, through)
    gx2 = cot

    loads["proj"].wait()
    loads["o"].wait()
    proj_cols = slice(3 * width, 4 * width)

    def sum_proj(h, carry):
        gproj[h] = dot_tn(gx2[:, span(h, half)], o[...]).astype(BF).reshape(gproj.shape[1:])
        return carry

    lax.fori_loop(0, 2, sum_proj, 0)
    ready(tiles("proj", width))
    advance()

    def through_proj(i, rows):
        do[rows, :] = dot_nn(gx2[rows, :], whole(wide, cols=proj_cols)).astype(BF)

    paced(tokens // TILE, lambda i: through_proj(i, span(i, TILE)))
    for name in ("q", "k", "v", "lse"):
        loads[name].wait()

    def turn_keys(i, rows):
        kt[:, rows] = k[rows, :].astype(F32).T.astype(BF)

    rows_loop(tokens, TILE, turn_keys)

    blocks = tokens // QB
    lane_half = lax.broadcasted_iota(jnp.int32, (QB, 2 * HD), 1) // HD

    group = width // 2

    def group_names(g):
        return {("qkv", c, lo) for c in range(3) for lo in range(g * group, (g + 1) * group, size)}

    def group_grads(g):
        cols = slice(g * group, (g + 1) * group)

        def turn(i, rows):
            dq[rows, cols] = dqt[cols, rows].astype(F32).T.astype(BF)

        rows_loop(tokens, TILE, turn)
        for c, ref in ((1, dk), (2, dv), (0, dq)):

            def sum_qkv(h, carry, c=c, ref=ref):
                gqkv[(c, h, Ellipsis, cols)] = dot_tn(a1[:, span(h, half)], ref[:, cols]).astype(BF).reshape(*gqkv.shape[2:-1], group)
                return carry

            lax.fori_loop(0, 2, sum_qkv, 0)

    def head_step(h):
        @pl.when(h == heads // 2)
        def _():
            group_grads(0)
            ready(group_names(0), mark=False)

        cols = span(h // 2, 2 * HD)
        head_rows = span(h, HD)
        side = lax.rem(h, 2)
        slope = slopes[h]

        @pl.when(side == 0)
        def _():
            acc_k[...] = jnp.zeros_like(acc_k)
            acc_v[...] = jnp.zeros_like(acc_v)

        for b in range(blocks):
            end = (b + 1) * QB
            rows = slice(b * QB, end)
            zero = jnp.zeros((QB, 2 * HD), BF)
            query = jnp.where(lane_half == side, q[rows, cols], zero)
            outer = jnp.where(lane_half == side, do[rows, cols], zero)
            bias = pos[0:end, :] * slope
            bias = jnp.concatenate([bias] * (QB // bias.shape[1]), axis=1)
            scores = dot_nt(k[0:end, cols], query) + bias - lse[pl.ds(h, 1), rows]
            keep = lax.broadcasted_iota(jnp.int32, (QB, QB), 0) <= lax.broadcasted_iota(jnp.int32, (QB, QB), 1)
            diag = jnp.where(keep, scores[b * QB : end, :], -1e30)
            scores = diag if b == 0 else jnp.concatenate([scores[0 : b * QB, :], diag], axis=0)
            probs = jnp.exp(scores)
            acc_v[0:end, :] += dot_nn(probs.astype(BF), outer)
            grad = dot_nt(v[0:end, cols], outer)
            inner = jnp.sum(probs * grad, axis=0, keepdims=True)
            low = (probs * (grad - inner)).astype(BF)
            acc_k[0:end, :] += dot_nn(low, query)
            dqt[head_rows, rows] = (dot_nn(kt[head_rows, 0:end], low) * HD ** (-0.5)).astype(BF)

        @pl.when(side == 1)
        def _():
            dk[:, cols] = acc_k[...].astype(BF)
            dv[:, cols] = acc_v[...].astype(BF)

    loads["a1"].wait()
    batches = [due() for _ in range(heads // 2 + 1)]
    ready(group_names(0), start=False)
    paced_loop(heads, head_step, batches + [due() for _ in range(heads // 2 - 1)], run)
    group_grads(1)
    ready(group_names(1))
    advance()
    for at, ref in ((0, dq), (width, dv)):
        sums[0, 10:11, at : at + width] = jnp.sum(ref[...].astype(F32), axis=0, keepdims=True)

    for name in ("qkv", "qkv1", "qkv2"):
        loads[name].wait()

    def back_one(rows):
        total = dot_nt(dq[rows, :], whole(wide, cols=slice(0, width)))
        total += dot_nt(dk[rows, :], whole(wide, cols=slice(width, 2 * width)))
        return total + dot_nt(dv[rows, :], whole(wide, cols=slice(2 * width, 3 * width)))

    for copy in part_copies:
        copy.wait_send()

    def partner_rows(i):
        part[span(i, 256), :] = back_one(rows_of(other, i, 256)).astype(BF)

    paced(local // 256, partner_rows)
    last = mesh_copy(part.at[pl.ds(0, local)], last_r, psend.at[3], precv.at[3], device_id={"tensor": other})
    last.start()
    advance()
    loads["x"].wait()
    last.wait_recv()

    def own_rows(i):
        rows = rows_of(t, i, 256)
        here = span(i, 256)
        grad = back_one(rows) + last_r[here, :].astype(F32)
        normed, inverse = norm_parts(x_f[here, :].astype(F32))
        grad_o[here, :] = x2[rows, :] + norm_back(grad, normed, inverse, table[0:1, :])
        add_sum(0, grad * normed)
        add_sum(2, grad)

    paced(local // 256, own_rows)

    def sum_step(s):
        to = {"dp": partner_of(me, mine, s)} if s < count else {"tensor": other}
        return mesh_copy(sums.at[s], sland.at[s], vsend.at[s], vrecv.at[s], device_id=to)

    sum_copies = [sum_step(s) for s in range(count + 1)]
    sum_copies[0].start()
    for s in range(count):
        advance()
        sum_copies[s].wait_recv()
        sums[s + 1] = sums[s] + sland[s]
        sum_copies[s + 1].start()
    while queue:
        run(queue.pop(0))
    sum_copies[count].wait_recv()
    sums_o[0:8, :] = sums[count, 0:8] + sland[count, 0:8]
    sums_o[8:16, :] = sums[count, 8:16]
    for c in range(len(chunks)):
        for s in range(count):
            copy_of(c, s).wait_send()
    for copy in sum_copies + [last]:
        copy.wait_send()


def backward_all(slopes, table, x, cot, a1, q, k, v, o, lse, x2, a2, u, gp, gdown, qkv_w, proj_w, up_w, down_w, n, width=256):
    count = n.bit_length() - 1
    two = (2,) * count
    tokens, model = cot.shape
    inner, hidden = q.shape[1], gp.shape[1]
    heads = inner // HD
    r = model // n
    chunks = [("down", None, lo, width) for lo in range(0, hidden, width)]
    chunks += [("up", None, lo, width) for lo in range(0, hidden, width)]
    chunks += [("proj", None, lo, width) for lo in range(0, inner, width)]
    chunks += [("qkv", c, lo, width) for lo in range(0, inner, width) for c in (1, 2, 0)]
    f = lambda *s: jax.ShapeDtypeStruct(s, F32)
    outs = (jax.ShapeDtypeStruct(x.shape, BF), f(*x.shape), f(3, r, inner), f(r, inner), f(r, hidden), f(r, hidden), f(16, model))
    vm = lambda *s, d=BF: pltpu.VMEM(s, d)
    scratch = [vm(len(chunks), *two[: count - 1 - s], r, width) for s in range(count)]
    scratch += [vm(count + 1, 16, model, d=F32), vm(count + 1, 16, model, d=F32), vm(*x.shape), vm(tokens, model), vm(tokens, model)]
    scratch += [vm(heads, tokens, d=F32), vm(tokens, model, d=F32), vm(tokens, hidden)]
    scratch += [vm(*two, r, hidden), vm(*two, r, hidden), vm(*two, r, inner), vm(3, *two, r, inner), vm(model, hidden), vm(model, hidden)]
    scratch += [vm(tokens, model), vm(tokens, model), vm(*x.shape), vm(*x.shape), vm(inner, tokens), vm(inner, tokens)]
    scratch += [vm(tokens, 2 * HD, d=F32)] * 2 + [vm(tokens, 128, d=F32)]
    sems = lambda m: pltpu.SemaphoreType.DMA((m,))
    m = len(chunks) * count
    scratch += [sems(m), sems(m), sems(count + 1), sems(count + 1), sems(4), sems(4), sems(20)]
    flat = lambda a: a.reshape(*a.shape[: a.ndim - count - 2], model, a.shape[-1])
    by_block = lambda a: a.reshape(*two, r, a.shape[-1])

    def body(slopes_ref, table_ref, *refs):
        backward_kernel(count, chunks, SCATTER_MODES, SCATTER_ORDER, SCATTER_PLAN, slopes_ref, table_ref, refs[:17], refs[17 : 17 + len(outs)], refs[17 + len(outs) :])

    return pl.pallas_call(
        body, out_shape=outs, in_specs=[pl.BlockSpec(memory_space=pltpu.SMEM), VM] + [ANY] * 17, out_specs=[VM] * len(outs), scratch_shapes=scratch,
        compiler_params=pltpu.CompilerParams(collective_id=1, has_side_effects=True, vmem_limit_bytes=67043328), name="backward_all",
    )(slopes, table, x, cot, a1, q, k, v, o, lse, x2, a2, by_block(u), gp, by_block(gdown), flat(qkv_w), flat(proj_w), flat(up_w), flat(down_w))

def finish_kernel(count, *refs):
    ins, outs, refs = refs[:count], refs[count : 2 * count], refs[2 * count :]
    gains_o, shifts_o, bufs, (in_sem, out_sem) = refs[0], refs[1], refs[2 : 2 + count], refs[2 + count :]
    reads = [pltpu.make_async_copy(a, b, in_sem.at[i]) for i, (a, b) in enumerate(zip(ins, bufs))]
    writes = [pltpu.make_async_copy(b, c, out_sem.at[i]) for i, (b, c) in enumerate(zip(bufs, outs))]
    for copy in reads:
        copy.start()
    for read, write in zip(reads, writes):
        read.wait()
        write.start()
    part = gains_o.shape[1]
    base = (2 * lax.axis_index("dp") + lax.axis_index("tensor")) * part
    block = bufs[-1][0:8, span(base // 128, 128)]
    turned = pltpu.roll(block, lax.rem(128 - lax.rem(base, 128), 128), 1)
    gains_o[...] = turned[0:2, 0:part]
    shifts_o[...] = turned[2:6, 0:part]
    for copy in writes:
        copy.wait()


def finish(arrays, part):
    count = len(arrays)
    vectors = (jax.ShapeDtypeStruct((2, part), F32), jax.ShapeDtypeStruct((4, part), F32))
    return pl.pallas_call(
        functools.partial(finish_kernel, count), out_shape=tuple(jax.ShapeDtypeStruct(a.shape, a.dtype) for a in arrays) + vectors,
        in_specs=[ANY] * count, out_specs=[ANY] * count + [VM] * 2,
        scratch_shapes=[pltpu.VMEM(a.shape, a.dtype) for a in arrays] + [pltpu.SemaphoreType.DMA((count,))] * 2, name="finish")(*arrays)


def on_device(layer_in, w_qkv, b_qv, w_proj, w_ff1, b_ff1, w_ff2, norm_gains, add_biases, cotangent):
    n = lax.axis_size("dp")
    i = lax.axis_index("dp")
    t = lax.axis_index("tensor")
    width = w_qkv.shape[2]
    model = layer_in.shape[1]
    hidden = w_ff1.shape[1]
    heads = b_qv.shape[1]
    part = norm_gains.shape[1]
    zero = jnp.int32(0)
    put = lambda shape, a, at: lax.dynamic_update_slice(jnp.zeros(shape, F32), a.astype(F32), at)
    up_grid = (b_ff1.shape[0], n * b_ff1.shape[1])
    qv_grid = (*b_qv.shape[:2], n * b_qv.shape[2])
    small = jnp.concatenate([
        put((8, model), jnp.concatenate([norm_gains, add_biases]), (zero, (2 * i + t) * part)),
        put(up_grid, b_ff1, (zero, i * b_ff1.shape[1])).reshape(-1, model),
        put(qv_grid, b_qv, (zero, zero, i * b_qv.shape[2])).reshape(-1, model),
        jnp.zeros((8 - (hidden + 2 * width) // model, model), F32)])
    slopes = 2.0 ** (-8.0 * (t * heads + jnp.arange(heads, dtype=jnp.int32) + 1).astype(F32) / H)
    (qkv_w, proj_w, up_w, down_w, vectors, cot, a1, q, k, v, o, lse, x2, a2, u, rise, grad_down) = forward_all(
        slopes, w_qkv, w_proj.T, w_ff1, w_ff2.T, small, layer_in, cotangent, n)
    layer_out, grad_in, out_qkv, out_proj, out_up, out_down, sums = backward_all(
        slopes, vectors, layer_in, cot, a1, q, k, v, o, lse, x2, a2, u, rise, grad_down, qkv_w, proj_w, up_w, down_w, n)
    layer_out, grad_in, out_qkv, out_proj, out_up, out_down, sums, out_gains, out_shifts = finish(
        (layer_out, grad_in, out_qkv, out_proj, out_up, out_down, sums), part)
    up_sums = lax.dynamic_slice_in_dim(sums[8 : 8 + hidden // model].reshape(up_grid), i * b_ff1.shape[1], b_ff1.shape[1], 1)
    qv_sums = lax.dynamic_slice_in_dim(sums[10].reshape(qv_grid), i * b_qv.shape[2], b_qv.shape[2], 2)
    return (layer_out, grad_in, out_qkv, qv_sums, out_proj.T, out_up, up_sums, out_down.T, out_gains, out_shifts)


def solution(mesh):
    rows, cols = P(("dp", "tensor"), None), P(None, ("dp", "tensor"))
    return jax.shard_map(
        on_device,
        mesh=mesh,
        in_specs=(rows, P(None, "dp", "tensor"), P(None, "tensor", "dp"), P("tensor", "dp"), P("dp", "tensor"),
                  P("tensor", "dp"), P("tensor", "dp"), cols, cols, rows),
        out_specs=(rows, rows, P(None, "dp", "tensor"), P(None, "tensor", "dp"), P("tensor", "dp"), P("dp", "tensor"),
                   P("tensor", "dp"), P("tensor", "dp"), cols, cols),
        check_vma=False,
    )
```

```python
import functools
import math
import jax
import jax.numpy as jnp
from jax import lax
from jax.experimental import pallas as pl
from jax.experimental.pallas import tpu as pltpu
from jax.sharding import PartitionSpec as P

MESH = pl.DeviceIdType.MESH
ANY = pl.BlockSpec(memory_space=pl.ANY)
VM = pl.BlockSpec(memory_space=pltpu.VMEM)


def bits_of(index, count):
    return [lax.rem(index // (1 << b), 2) for b in range(count)]


def partner_of(index, mine, b):
    return index + (1 - 2 * mine[b]) * (1 << b)


def halving_orders(count):
    return [[(start + i) % count for i in range(count)] for start in range(3)]


def enter(index, mine, count, other):
    barrier = pltpu.get_barrier_semaphore()
    for b in range(count):
        pl.semaphore_signal(barrier, inc=1, device_id={"dp": partner_of(index, mine, b)}, device_id_type=MESH)
    pl.semaphore_signal(barrier, inc=1, device_id={"tensor": other}, device_id_type=MESH)
    pl.semaphore_wait(barrier, count + 1)


def block_index(mine, held, count):
    return tuple(slice(None) if b in held else mine[b] for b in reversed(range(count)))

SEQ_LEN = 1024
HD = 64
H = 16
epsilon = 1e-05
gelu_scale = 0.7978845608028654
F32 = jnp.float32
BF = jnp.bfloat16
TILE = 512
QB = 256
LOOK = 4


def bit_orders(count, modes, total, flip):
    if modes and count == 4:
        return [[mode // 10**i % 10 for i in (3, 2, 1, 0)] for mode in modes]
    cyclic = [[(start + i) % count for i in range(count)] for start in (0, 1, 0, 1, 0, 1, 0, 2)]
    return [(order[::-1] if flip else order) for order in (cyclic[c % len(cyclic)] for c in range(total))]


def dot_nn(a, b):
    return lax.dot_general(a, b, (((1,), (0,)), ((), ())), preferred_element_type=F32)


def dot_nt(a, b):
    return lax.dot_general(a, b, (((1,), (1,)), ((), ())), preferred_element_type=F32)


def dot_tn(a, b):
    return lax.dot_general(a, b, (((0,), (0,)), ((), ())), preferred_element_type=F32)


def span(i, size):
    return pl.ds(pl.multiple_of(i * size, size), size)


def paced_loop(steps, body, batches, run):
    def step(i, carry):
        for j in range(steps):
            if batches[j]:

                @pl.when(i == j)
                def _():
                    for item in batches[j]:
                        run(item)

        body(i)
        return carry

    lax.fori_loop(0, steps, step, 0)


def rows_loop(total, size, body):
    def step(i, carry):
        body(i, span(i, size))
        return carry

    lax.fori_loop(0, total // size, step, 0)


def forward_kernel(count, chunks, modes, order, plan, refs_in, refs_out, scratch, slopes):
    (qkv, proj, up, down, small, x, cot) = refs_in
    (qkv_o, proj_o, up_o, down_o, vec_o, cot_o, a1_o, q_o, k_o, v_o, o_o, lse_o, x2_o, a2_o, u_o, gp_o, gdown_o) = refs_out
    (qkv_w, proj_w, up_w, down_w, vec, vland, x_f, cot_f, a1, q, k, v, vt, ot, o, lse, part, part_r, x2, a2, u, gp, gdown, pos,
     send, recv, vsend, vrecv, psend, precv, own_sem, out_sem) = scratch
    me = lax.axis_index("dp")
    t = lax.axis_index("tensor")
    other = 1 - t
    mine = bits_of(me, count)
    orders = bit_orders(count, modes, len(chunks), True)
    full = block_index(mine, (), count)
    tokens, model = x_f.shape
    width = q.shape[1]
    hidden = u.shape[1]
    heads = width // HD
    local_rows = x.shape[0]
    mesh_copy = functools.partial(pltpu.make_async_remote_copy, device_id_type=MESH)

    enter(me, mine, count, other)
    waits = []

    def vec_step(s):
        to = {"dp": partner_of(me, mine, s)} if s < count else {"tensor": other}
        return mesh_copy(small if s == 0 else vec.at[s], vland.at[s], vsend.at[s], vrecv.at[s], device_id=to)

    vec[0] = small[...]
    vec_copies = [vec_step(s) for s in range(count + 1)]
    vec_copies[0].start()

    mine_rows = pl.ds(t * local_rows, local_rows)
    pair_copies = [mesh_copy(src, dst.at[mine_rows], psend.at[i], precv.at[i], device_id={"tensor": other})
                   for i, (src, dst) in enumerate(((x, x_f), (cot, cot_f)))]
    for copy in pair_copies:
        copy.start()

    names = {"qkv": (qkv, qkv_w), "proj": (proj, proj_w), "up": (up, up_w), "down": (down, down_w)}

    def views(c):
        name, lead, lo, size = chunks[c]
        src, dst = names[name]
        if lead is not None:
            src, dst = src.at[lead], dst.at[lead]
        return src.at[:, pl.ds(lo, size)], dst, (slice(None), pl.ds(lo, size))

    def copy_of(c, s):
        order = orders[c]
        src, dst, tail = views(c)
        at = (*block_index(mine, order[:s], count), *tail)
        return mesh_copy(src if s == 0 else dst.at[at], dst.at[at], send.at[c * count + s], recv.at[c * count + s],
                         device_id={"dp": partner_of(me, mine, order[s])})

    owns = [pltpu.make_async_copy(src, dst.at[full], own_sem.at[i]) for i, (src, dst) in enumerate(
        [(qkv.at[c], qkv_w.at[c]) for c in range(3)] + [(proj, proj_w), (up, up_w), (down, down_w)])]
    owns += [pltpu.make_async_copy(src, dst.at[mine_rows], own_sem.at[6 + i]) for i, (src, dst) in enumerate(((x, x_f), (cot, cot_f)))]
    for copy in owns:
        copy.start()
    for copy in owns:
        copy.wait()

    queue = [divmod(code, count) for code in order] if order and count == 4 else sorted(
        ((c, s) for c in range(len(chunks)) for s in range(count)), key=lambda cs: (cs[0] + LOOK * cs[1], cs[0]))
    share = list(plan) if plan and count == 4 else []
    done = set()

    def run(item):
        c, s = item
        if s > 0:
            copy_of(c, s - 1).wait_recv()
        copy_of(c, s).start()

    def settle(c):
        if c not in done:
            while any(item[0] == c for item in queue):
                run(queue.pop(0))
            copy_of(c, count - 1).wait_recv()
            done.add(c)

    def due():
        size = share.pop(0) if share else 2
        batch, queue[:] = queue[:size], queue[size:]
        return batch

    def advance():
        for item in due():
            run(item)

    def paced(steps, body):
        paced_loop(steps, body, [due() for _ in range(steps)], run)

    outs = []

    def emit(src, dst):
        copy = pltpu.make_async_copy(src, dst, out_sem.at[len(outs)])
        copy.start()
        outs.append(copy)

    advance()
    for s in range(count):
        vec_copies[s].wait_recv()
        vec[s + 1] = vec[s] + vland[s]
        vec_copies[s + 1].start()
        advance()
    for copy in pair_copies:
        copy.wait_recv()
    emit(cot_f, cot_o)
    vec_copies[count].wait_recv()
    vec[count + 1, 0:8] = vec[count, 0:8] + vland[count, 0:8]
    vec[count + 1, 8:16] = vec[count, 8:16]
    emit(vec.at[count + 1], vec_o)
    table = vec.at[count + 1]

    def normed(rows_value, gain, shift):
        center = rows_value - jnp.mean(rows_value, axis=-1, keepdims=True)
        spread = jnp.mean(center * center, axis=-1, keepdims=True)
        return (center * lax.rsqrt(spread + epsilon)) * gain + shift

    def norm_one(i, rows):
        a1[rows, :] = normed(x_f[rows, :].astype(F32), table[0:1, :], table[2:3, :]).astype(BF)

    pos[...] = lax.broadcasted_iota(jnp.int32, pos.shape, 0).astype(F32)
    paced(4, lambda i: norm_one(i, span(i, tokens // 4)))
    emit(a1, a1_o)

    for c, dst in ((1, k), (0, q), (2, v)):
        for i, chunk in enumerate(chunks):
            if chunk[0] == "qkv" and chunk[1] == c:
                settle(i)

        def mix(i, rows, c=c, dst=dst):
            value = dot_nn(a1[rows, :], qkv_w[c].reshape(model, width))
            if c == 0:
                value = (value + table[10:11, 0:width]).astype(BF).astype(F32) * HD ** (-0.5)
            if c == 2:
                value = value + table[10:11, width : 2 * width]
            dst[rows, :] = value.astype(BF)
            if c == 2:
                vt[:, rows] = value.T.astype(BF)

        paced(2, lambda i: mix(i, span(i, tokens // 2)))
    for src, dst in ((q, q_o), (k, k_o), (v, v_o), (qkv_w, qkv_o)):
        emit(src, dst)

    blocks = tokens // QB
    lane_half = lax.broadcasted_iota(jnp.int32, (QB, 2 * HD), 1) // HD

    def head_step(h):
        cols = span(h // 2, 2 * HD)
        slope = slopes[h]
        head_rows = span(h, HD)
        for b in range(blocks):
            end = (b + 1) * QB
            query = jnp.where(lane_half == lax.rem(h, 2), q[b * QB : end, cols], jnp.zeros((QB, 2 * HD), BF))
            bias = pos[0:end, :] * slope
            bias = jnp.concatenate([bias] * (QB // bias.shape[1]), axis=1)
            scores = dot_nt(k[0:end, cols], query) + bias
            diag = scores[b * QB : end, :]
            keep = lax.broadcasted_iota(jnp.int32, (QB, QB), 0) <= lax.broadcasted_iota(jnp.int32, (QB, QB), 1)
            diag = jnp.where(keep, diag, -1e30)
            scores = diag if b == 0 else jnp.concatenate([scores[0 : b * QB, :], diag], axis=0)
            peak = jnp.max(scores, axis=0, keepdims=True)
            weights = jnp.exp(scores - peak)
            total = jnp.sum(weights, axis=0, keepdims=True)
            out = dot_nn(vt[head_rows, 0:end], weights.astype(BF))
            ot[head_rows, b * QB : end] = (out / total).astype(BF)
            lse[pl.ds(h, 1), b * QB : end] = peak + jnp.log(total)

    paced(heads, head_step)
    for i, chunk in enumerate(chunks):
        if chunk[0] == "proj":
            settle(i)

    def turn(i, rows):
        o[rows, :] = ot[:, rows].astype(F32).T.astype(BF)

    rows_loop(tokens, TILE, turn)
    emit(o, o_o)
    emit(lse, lse_o)
    emit(proj_w, proj_o)

    def project(i, rows):
        part[rows, :] = dot_nt(o[rows, :], proj_w[...].reshape(model, width)).astype(BF)

    half = tokens // 2
    part_copies = []
    for j in range(2):
        project(j, pl.ds(j * half, half))
        copy = mesh_copy(part.at[pl.ds(j * half, half)], part_r.at[pl.ds(j * half, half)], psend.at[2 + j], precv.at[2 + j],
                         device_id={"tensor": other})
        copy.start()
        part_copies.append(copy)
        advance()
    for j in range(2):
        part_copies[j].wait_recv()

        def norm_two(i, j=j):
            rows = pl.ds(pl.multiple_of(j * half + i * 256, 256), 256)
            middle = x_f[rows, :].astype(F32) + (part[rows, :].astype(F32) + part_r[rows, :].astype(F32)) + table[3:4, :]
            x2[rows, :] = middle
            a2[rows, :] = normed(middle, table[1:2, :], table[4:5, :]).astype(BF)

        paced(half // 256, norm_two)
    emit(x2, x2_o)
    emit(a2, a2_o)

    for j in range(hidden // TILE):
        cols = pl.ds(j * TILE, TILE)
        for i, chunk in enumerate(chunks):
            if chunk[0] == "up" and j * TILE <= chunk[2] < (j + 1) * TILE:
                settle(i)

        row = 8 + j * TILE // model
        bias_at = j * TILE % model

        def expand(i, rows, cols=cols, row=row, bias_at=bias_at):
            pre = dot_nn(a2[rows, :], up_w[..., cols].reshape(model, TILE)) + table[row : row + 1, bias_at : bias_at + TILE]
            square = pre * pre
            bent = jnp.tanh(pre * (gelu_scale + (gelu_scale * 0.044715) * square))
            rise = 0.5 + 0.5 * bent
            u[rows, cols] = (pre * rise).astype(BF)
            slope = 0.5 * pre * (1.0 - bent * bent) * (gelu_scale + (3 * 0.044715 * gelu_scale) * square)
            gp[rows, cols] = (rise + slope).astype(BF)

        paced(tokens // 256, lambda i: expand(i, span(i, 256)))

        def sum_down(i, rows, cols=cols):
            gdown[rows, cols] = dot_tn(cot_f[:, rows], u[:, cols]).astype(BF)

        paced(model // TILE, lambda i: sum_down(i, span(i, TILE)))
        for src, dst in ((u, u_o), (gp, gp_o), (gdown, gdown_o)):
            emit(src.at[:, cols], dst.at[:, cols])
        emit(up_w.at[(Ellipsis, cols)], up_o.at[(Ellipsis, cols)])
    for i, (name, lead, lo, size) in enumerate(chunks):
        settle(i)
        if name == "down":
            emit(down_w.at[(Ellipsis, pl.ds(lo, size))], down_o.at[(Ellipsis, pl.ds(lo, size))])
    for c in range(len(chunks)):
        for s in range(count):
            copy_of(c, s).wait_send()
    for copy in vec_copies + pair_copies + part_copies:
        copy.wait_send()
    for copy in outs:
        copy.wait()


GATHER_MODES = (
    3021, 2130, 2031, 3210, 3120, 2301, 3210, 1320, 3201, 3210, 2301, 3210, 1320, 1203, 1302, 3012, 312, 1320, 231, 3201, 2310, 2031,
    2031, 321,
)
GATHER_ORDER = (
    20, 36, 12, 4, 0, 21, 37, 8, 5, 13, 92, 32, 1, 16, 6, 38, 93, 9, 28, 22, 2, 14, 84, 33, 10, 17, 39, 24, 29, 44, 40, 23, 15, 7, 18,
    3, 85, 94, 34, 60, 52, 76, 11, 48, 41, 25, 56, 53, 19, 30, 45, 72, 95, 86, 61, 64, 77, 80, 35, 49, 57, 26, 42, 68, 54, 88, 31, 73,
    46, 62, 65, 87, 78, 43, 81, 50, 55, 27, 89, 58, 69, 74, 47, 66, 82, 63, 51, 79, 90, 70, 59, 67, 75, 83, 71, 91,
)
GATHER_PLAN = (
    39, 3, 2, 3, 3, 4, 2, 2, 0, 2, 3, 1, 1, 2, 1, 1, 2, 2, 2, 2, 4, 1, 3, 3, 1, 2, 0, 0, 0, 1, 0, 0, 0, 2, 0, 0, 0, 0, 0, 0, 0, 2, 0,
    0, 0, 0, 0, 0, 0, 0, 0, 0, 0,
)


def forward_all(slopes, qkv, proj, up, down, small, x, cot, n, width=256):
    count = n.bit_length() - 1
    two = (2,) * count
    chunks = []
    for c in (1, 0, 2):
        chunks += [("qkv", c, lo, width) for lo in range(0, qkv.shape[2], width)]
    for name, a in (("proj", proj), ("up", up), ("down", down)):
        chunks += [(name, None, lo, width) for lo in range(0, a.shape[1], width)]
    tokens, model = 2 * x.shape[0], x.shape[1]
    inner, hidden = qkv.shape[2], up.shape[1]
    heads = inner // HD
    weights = [((3, *two, *qkv.shape[1:]), BF), ((*two, *proj.shape), BF), ((*two, *up.shape), BF), ((*two, *down.shape), BF)]
    shapes = weights + [((16, model), F32), ((tokens, model), BF), ((tokens, model), BF)] + [((tokens, inner), BF)] * 4
    shapes += [((heads, tokens), F32), ((tokens, model), F32), ((tokens, model), BF), ((tokens, hidden), BF), ((tokens, hidden), BF), ((model, hidden), BF)]
    vm = lambda s, d: pltpu.VMEM(s, d)
    scratch = [vm(*w) for w in weights]
    scratch += [vm((count + 2, 16, model), F32), vm((count + 1, 16, model), F32), vm((tokens, model), BF), vm((tokens, model), BF), vm((tokens, model), BF)]
    scratch += [vm((tokens, inner), BF)] * 3 + [vm((inner, tokens), BF)] * 2 + [vm((tokens, inner), BF), vm((heads, tokens), F32)]
    scratch += [vm((tokens, model), BF)] * 2 + [vm((tokens, model), F32), vm((tokens, model), BF), vm((tokens, hidden), BF), vm((tokens, hidden), BF), vm((model, hidden), BF)]
    scratch += [vm((tokens, 128), F32)]
    sems = lambda k: pltpu.SemaphoreType.DMA((k,))
    k = len(chunks) * count
    scratch += [sems(k), sems(k), sems(count + 1), sems(count + 1), sems(4), sems(4), sems(8), sems(64)]

    def body(slopes_ref, *refs):
        forward_kernel(count, chunks, GATHER_MODES, GATHER_ORDER, GATHER_PLAN, refs[:7], refs[7 : 7 + len(shapes)], refs[7 + len(shapes) :], slopes_ref)

    return pl.pallas_call(
        body, out_shape=tuple(jax.ShapeDtypeStruct(*s) for s in shapes),
        in_specs=[pl.BlockSpec(memory_space=pltpu.SMEM)] + [VM] * 7, out_specs=[ANY] * len(shapes), scratch_shapes=scratch,
        compiler_params=pltpu.CompilerParams(collective_id=0, has_side_effects=True, vmem_limit_bytes=62 * 2**20), name="forward_all",
    )(slopes, qkv, proj, up, down, small, x, cot)

SCATTER_MODES = (
    1023, 2013, 231, 1320, 1023, 3021, 213, 3012, 1320, 213, 213, 3021, 1203, 1023, 1302, 1023, 132, 213, 132, 1032, 3120, 213, 1023,
    2013,
)
SCATTER_ORDER = (
    1, 11, 26, 31, 16, 21, 2, 27, 22, 12, 32, 46, 3, 61, 17, 28, 23, 81, 41, 56, 51, 66, 36, 47, 62, 86, 13, 18, 71, 76, 4, 24, 29,
    57, 67, 33, 96, 52, 82, 91, 37, 63, 6, 87, 42, 101, 106, 77, 19, 48, 68, 111, 14, 116, 97, 53, 92, 83, 7, 58, 38, 88, 34, 72, 112,
    107, 64, 102, 117, 43, 8, 59, 78, 49, 73, 108, 98, 118, 69, 84, 93, 44, 54, 89, 113, 103, 39, 99, 109, 119, 94, 74, 79, 104, 114,
    9,
)
SCATTER_PLAN = (
    0, 0, 0, 0, 0, 0, 0, 0, 0, 0, 0, 0, 0, 0, 0, 0, 0, 0, 0, 2, 0, 1, 2, 1, 1, 1, 1, 0, 0, 1, 0, 0, 0, 0, 0, 0, 1, 0, 0, 1, 3, 2, 4,
    1, 4, 5, 5, 5, 0, 1, 4, 4, 3, 3, 4, 7, 6,
)


def backward_kernel(count, chunks, modes, order, plan, slopes, table, refs_in, refs_out, scratch):
    (x_h, cot_h, a1_h, q_h, k_h, v_h, o_h, lse_h, x2_h, a2_h, u_h, gp_h, gdown_h, qkv_h, proj_h, up_h, down_h) = refs_in
    (layer_o, grad_o, gqkv_o, gproj_o, gup_o, gdown_o, sums_o) = refs_out
    landing = scratch[:count]
    (sums, sland, x_f, cot, a1, lse, x2, gp, big, gdown, gproj, gqkv, wide, up_w, part, part_r, first_r, last_r,
     kt, dqt, acc_k, acc_v, pos, send, recv, vsend, vrecv, psend, precv, in_sem) = scratch[count:]
    me = lax.axis_index("dp")
    t = lax.axis_index("tensor")
    other = 1 - t
    mine = bits_of(me, count)
    orders = bit_orders(count, modes, len(chunks), False)
    tokens, model = cot.shape
    width = q_h.shape[1]
    hidden = gp.shape[1]
    heads = width // HD
    local = tokens // 2
    q, k, v, o = (up_w.at[:, pl.ds(i * width, width)] for i in range(4))
    dq, dk, dv, do = q, k, v, o
    mesh_copy = functools.partial(pltpu.make_async_remote_copy, device_id_type=MESH)
    rows_of = lambda who, i, size: pl.ds(pl.multiple_of(who * local + i * size, size), size)

    enter(me, mine, count, other)
    loads = {}

    def load(name, src, dst):
        copy = pltpu.make_async_copy(src, dst, in_sem.at[len(loads)])
        copy.start()
        loads[name] = copy

    load("u", u_h, big)
    load("down", down_h, wide)
    load("gdown", gdown_h, gdown)
    load("cot", cot_h, cot)
    load("gp", gp_h, gp)
    load("x2", x2_h, x2)
    load("a2", a2_h, a1)
    load("up", up_h, up_w)
    load("lse", lse_h, lse)
    load("x", x_h, x_f)

    grads = {"qkv": gqkv, "proj": gproj, "up": big, "down": gdown}
    finals = {"qkv": gqkv_o, "proj": gproj_o, "up": gup_o, "down": gdown_o}
    size = chunks[0][3]

    def order_of(c):
        return orders[c]

    def held(c):
        name, lead, lo, _ = chunks[c]
        ref = grads[name]
        return ref if lead is None else ref.at[lead]

    def region(c, s, flip):
        order = order_of(c)
        at = []
        for b in reversed(range(count)):
            if b == order[s]:
                at.append(1 - mine[b] if flip else mine[b])
            else:
                at.append(mine[b] if b in order[:s] else slice(None))
        return tuple(at)

    def copy_of(c, s):
        name, lead, lo, _ = chunks[c]
        src = held(c)
        if name == "down" and s == 0:
            src = gdown_h
        at = (*region(c, s, True), slice(None), pl.ds(lo, size))
        return mesh_copy(src.at[at], landing[s].at[c], send.at[c * count + s], recv.at[c * count + s],
                         device_id={"dp": partner_of(me, mine, order_of(c)[s])})

    def run(item):
        c, s = item
        name, lead, lo, _ = chunks[c]
        copy_of(c, s - 1).wait_recv()
        got = landing[s - 1].at[c]
        keep = region(c, s - 1, False)
        cols = slice(lo, lo + size)
        ref = held(c)
        if s == count:
            total = ref[(*keep, slice(None), cols)].astype(F32) + got[...].astype(F32)
            out = finals[name]
            if lead is not None:
                out = out.at[lead]
            out[:, cols] = total
            return
        left = count - s

        def add(i, carry):
            sub = [lax.rem(i // (1 << (left - 1 - j)), 2) for j in range(left)]
            it = iter(sub)
            at = (*(next(it) if isinstance(b, slice) else b for b in keep), slice(None), cols)
            ref[at] = (ref[at].astype(F32) + got[tuple(sub)].astype(F32)).astype(BF)
            return carry

        lax.fori_loop(0, 1 << left, add, 0)
        copy_of(c, s).start()

    queue = [(code // (count + 1), code % (count + 1)) for code in order] if order and count == 4 else sorted(
        ((c, s) for c in range(len(chunks)) for s in range(1, count + 1)), key=lambda cs: (cs[0] + LOOK * cs[1], cs[0]))
    share = list(plan) if plan and count == 4 else []
    open_chunks = set()

    def ready(names, mark=True, start=True):
        for c, (name, lead, lo, _) in enumerate(chunks):
            if (name, lead, lo) in names:
                if start:
                    copy_of(c, 0).start()
                if mark:
                    open_chunks.add(c)

    def due():
        batch = []
        for _ in range(share.pop(0) if share else 2):
            if queue and queue[0][0] in open_chunks:
                batch.append(queue.pop(0))
        return batch

    def advance():
        for item in due():
            run(item)

    def paced(steps, body):
        paced_loop(steps, body, [due() for _ in range(steps)], run)

    tiles = lambda name, total, lead=None, at=0: {(name, lead, lo) for lo in range(at, at + total, size)}
    ready(tiles("down", hidden))
    loads["gdown"].wait()
    sums[0] = jnp.zeros_like(sums[0])
    pos[...] = lax.broadcasted_iota(jnp.int32, pos.shape, 0).astype(F32)

    def whole(ref, h=None, cols=slice(None)):
        return ref[:, cols] if h is None else ref[span(h, model // 2), cols]

    loads["u"].wait()
    loads["down"].wait()
    half = model // 2

    def lowered(who, h):
        return dot_nt(big[who].reshape(local, hidden), whole(wide, h))

    def partner_lowered(h):
        part[0:local, span(h, half)] = lowered(other, h).astype(BF)

    paced(2, partner_lowered)
    first = mesh_copy(part.at[pl.ds(0, local)], first_r, psend.at[0], precv.at[0], device_id={"tensor": other})
    first.start()

    loads["cot"].wait()
    loads["gp"].wait()
    for j in range(hidden // TILE):
        cols = slice(j * TILE, (j + 1) * TILE)

        def grad_pre(i, rows, cols=cols):
            value = (dot_nn(cot[rows, :], whole(wide, cols=cols)) * gp[rows, cols].astype(F32)).astype(BF)
            gp[rows, cols] = value
            line = 8 + cols.start // model
            at = slice(cols.start % model, cols.start % model + TILE)
            sums[0, line : line + 1, at] += jnp.sum(value.astype(F32), axis=0, keepdims=True)

        paced(tokens // 256, lambda i: grad_pre(i, span(i, 256)))

    loads["x2"].wait()
    first.wait_recv()

    def own_lowered(h):
        cols = span(h, half)
        mid = x2[rows_of(t, 0, local), cols]
        layer_o[:, cols] = (mid + (lowered(t, h) + first_r[:, cols].astype(F32)) + table[5:6, cols]).astype(BF)

    paced(2, own_lowered)
    load("qkv", qkv_h.at[0], wide.at[:, pl.ds(0, width)])
    load("qkv1", qkv_h.at[1], wide.at[:, pl.ds(width, width)])
    load("qkv2", qkv_h.at[2], wide.at[:, pl.ds(2 * width, width)])
    load("proj", proj_h, wide.at[:, pl.ds(3 * width, width)])

    loads["a2"].wait()
    loads["up"].wait()
    first.wait_send()
    part_copies = []
    for h in range(2):
        rows = pl.ds(h * local, local)

        def back_up(e, rows=rows):
            part[rows, span(e, half)] = dot_nt(gp[rows, :], whole(up_w, e)).astype(BF)

        paced(2, back_up)
        copy = mesh_copy(part.at[rows], part_r.at[rows], psend.at[1 + h], precv.at[1 + h], device_id={"tensor": other})
        copy.start()
        part_copies.append(copy)
    for name, src, dst in (("q", q_h, q), ("k", k_h, k), ("v", v_h, v), ("o", o_h, o)):
        load(name, src, dst)
    for j in range(hidden // TILE):
        cols = slice(j * TILE, (j + 1) * TILE)

        def sum_up(h, carry, cols=cols):
            value = dot_tn(a1[:, span(h, half)], gp[:, cols]).astype(BF)
            big[(h, Ellipsis, cols)] = value.reshape(*big.shape[1:-1], TILE)
            return carry

        lax.fori_loop(0, 2, sum_up, 0)
        ready(tiles("up", TILE, at=j * TILE))
        advance()
    load("a1", a1_h, a1)

    def norm_parts(value):
        center = value - jnp.mean(value, axis=-1, keepdims=True)
        inverse = lax.rsqrt(jnp.mean(center * center, axis=-1, keepdims=True) + epsilon)
        return center * inverse, inverse

    def norm_back(grad, normed, inverse, gain):
        scaled = grad * gain
        return inverse * (scaled - jnp.mean(scaled, axis=-1, keepdims=True) - normed * jnp.mean(scaled * normed, axis=-1, keepdims=True))

    def add_sum(line, value):
        sums[0, line : line + 1, :] += jnp.sum(value, axis=0, keepdims=True)

    for copy in part_copies:
        copy.wait_recv()
    for who, count_it in ((t, True), (other, False)):

        def through(i, who=who, count_it=count_it):
            rows = rows_of(who, i, 128)
            grad = part[rows, :].astype(F32) + part_r[rows, :].astype(F32)
            normed, inverse = norm_parts(x2[rows, :])
            outer = cot[rows, :].astype(F32)
            mid = outer + norm_back(grad, normed, inverse, table[1:2, :])
            x2[rows, :] = mid
            cot[rows, :] = mid.astype(BF)
            if count_it:
                add_sum(1, grad * normed)
                add_sum(3, mid)
                add_sum(4, grad)
                add_sum(5, outer)

        paced(local // 128, through)
    gx2 = cot

    loads["proj"].wait()
    loads["o"].wait()
    proj_cols = slice(3 * width, 4 * width)

    def sum_proj(h, carry):
        gproj[h] = dot_tn(gx2[:, span(h, half)], o[...]).astype(BF).reshape(gproj.shape[1:])
        return carry

    lax.fori_loop(0, 2, sum_proj, 0)
    ready(tiles("proj", width))
    advance()

    def through_proj(i, rows):
        do[rows, :] = dot_nn(gx2[rows, :], whole(wide, cols=proj_cols)).astype(BF)

    paced(tokens // TILE, lambda i: through_proj(i, span(i, TILE)))
    for name in ("q", "k", "v", "lse"):
        loads[name].wait()

    def turn_keys(i, rows):
        kt[:, rows] = k[rows, :].astype(F32).T.astype(BF)

    rows_loop(tokens, TILE, turn_keys)

    blocks = tokens // QB
    lane_half = lax.broadcasted_iota(jnp.int32, (QB, 2 * HD), 1) // HD

    group = width // 2

    def group_names(g):
        return {("qkv", c, lo) for c in range(3) for lo in range(g * group, (g + 1) * group, size)}

    def group_grads(g):
        cols = slice(g * group, (g + 1) * group)

        def turn(i, rows):
            dq[rows, cols] = dqt[cols, rows].astype(F32).T.astype(BF)

        rows_loop(tokens, TILE, turn)
        for c, ref in ((1, dk), (2, dv), (0, dq)):

            def sum_qkv(h, carry, c=c, ref=ref):
                gqkv[(c, h, Ellipsis, cols)] = dot_tn(a1[:, span(h, half)], ref[:, cols]).astype(BF).reshape(*gqkv.shape[2:-1], group)
                return carry

            lax.fori_loop(0, 2, sum_qkv, 0)

    def head_step(h):
        @pl.when(h == heads // 2)
        def _():
            group_grads(0)
            ready(group_names(0), mark=False)

        cols = span(h // 2, 2 * HD)
        head_rows = span(h, HD)
        side = lax.rem(h, 2)
        slope = slopes[h]

        @pl.when(side == 0)
        def _():
            acc_k[...] = jnp.zeros_like(acc_k)
            acc_v[...] = jnp.zeros_like(acc_v)

        for b in range(blocks):
            end = (b + 1) * QB
            rows = slice(b * QB, end)
            zero = jnp.zeros((QB, 2 * HD), BF)
            query = jnp.where(lane_half == side, q[rows, cols], zero)
            outer = jnp.where(lane_half == side, do[rows, cols], zero)
            bias = pos[0:end, :] * slope
            bias = jnp.concatenate([bias] * (QB // bias.shape[1]), axis=1)
            scores = dot_nt(k[0:end, cols], query) + bias - lse[pl.ds(h, 1), rows]
            keep = lax.broadcasted_iota(jnp.int32, (QB, QB), 0) <= lax.broadcasted_iota(jnp.int32, (QB, QB), 1)
            diag = jnp.where(keep, scores[b * QB : end, :], -1e30)
            scores = diag if b == 0 else jnp.concatenate([scores[0 : b * QB, :], diag], axis=0)
            probs = jnp.exp(scores)
            acc_v[0:end, :] += dot_nn(probs.astype(BF), outer)
            grad = dot_nt(v[0:end, cols], outer)
            inner = jnp.sum(probs * grad, axis=0, keepdims=True)
            low = (probs * (grad - inner)).astype(BF)
            acc_k[0:end, :] += dot_nn(low, query)
            dqt[head_rows, rows] = (dot_nn(kt[head_rows, 0:end], low) * HD ** (-0.5)).astype(BF)

        @pl.when(side == 1)
        def _():
            dk[:, cols] = acc_k[...].astype(BF)
            dv[:, cols] = acc_v[...].astype(BF)

    loads["a1"].wait()
    batches = [due() for _ in range(heads // 2 + 1)]
    ready(group_names(0), start=False)
    paced_loop(heads, head_step, batches + [due() for _ in range(heads // 2 - 1)], run)
    group_grads(1)
    ready(group_names(1))
    advance()
    for at, ref in ((0, dq), (width, dv)):
        sums[0, 10:11, at : at + width] = jnp.sum(ref[...].astype(F32), axis=0, keepdims=True)

    for name in ("qkv", "qkv1", "qkv2"):
        loads[name].wait()

    def back_one(rows):
        total = dot_nt(dq[rows, :], whole(wide, cols=slice(0, width)))
        total += dot_nt(dk[rows, :], whole(wide, cols=slice(width, 2 * width)))
        return total + dot_nt(dv[rows, :], whole(wide, cols=slice(2 * width, 3 * width)))

    for copy in part_copies:
        copy.wait_send()

    def partner_rows(i):
        part[span(i, 256), :] = back_one(rows_of(other, i, 256)).astype(BF)

    paced(local // 256, partner_rows)
    last = mesh_copy(part.at[pl.ds(0, local)], last_r, psend.at[3], precv.at[3], device_id={"tensor": other})
    last.start()
    advance()
    loads["x"].wait()
    last.wait_recv()

    def own_rows(i):
        rows = rows_of(t, i, 256)
        here = span(i, 256)
        grad = back_one(rows) + last_r[here, :].astype(F32)
        normed, inverse = norm_parts(x_f[here, :].astype(F32))
        grad_o[here, :] = x2[rows, :] + norm_back(grad, normed, inverse, table[0:1, :])
        add_sum(0, grad * normed)
        add_sum(2, grad)

    paced(local // 256, own_rows)

    def sum_step(s):
        to = {"dp": partner_of(me, mine, s)} if s < count else {"tensor": other}
        return mesh_copy(sums.at[s], sland.at[s], vsend.at[s], vrecv.at[s], device_id=to)

    sum_copies = [sum_step(s) for s in range(count + 1)]
    sum_copies[0].start()
    for s in range(count):
        advance()
        sum_copies[s].wait_recv()
        sums[s + 1] = sums[s] + sland[s]
        sum_copies[s + 1].start()
    while queue:
        run(queue.pop(0))
    sum_copies[count].wait_recv()
    sums_o[0:8, :] = sums[count, 0:8] + sland[count, 0:8]
    sums_o[8:16, :] = sums[count, 8:16]
    for c in range(len(chunks)):
        for s in range(count):
            copy_of(c, s).wait_send()
    for copy in sum_copies + [last]:
        copy.wait_send()


def backward_all(slopes, table, x, cot, a1, q, k, v, o, lse, x2, a2, u, gp, gdown, qkv_w, proj_w, up_w, down_w, n, width=256):
    count = n.bit_length() - 1
    two = (2,) * count
    tokens, model = cot.shape
    inner, hidden = q.shape[1], gp.shape[1]
    heads = inner // HD
    r = model // n
    chunks = [("down", None, lo, width) for lo in range(0, hidden, width)]
    chunks += [("up", None, lo, width) for lo in range(0, hidden, width)]
    chunks += [("proj", None, lo, width) for lo in range(0, inner, width)]
    chunks += [("qkv", c, lo, width) for lo in range(0, inner, width) for c in (1, 2, 0)]
    f = lambda *s: jax.ShapeDtypeStruct(s, F32)
    outs = (jax.ShapeDtypeStruct(x.shape, BF), f(*x.shape), f(3, r, inner), f(r, inner), f(r, hidden), f(r, hidden), f(16, model))
    vm = lambda *s, d=BF: pltpu.VMEM(s, d)
    scratch = [vm(len(chunks), *two[: count - 1 - s], r, width) for s in range(count)]
    scratch += [vm(count + 1, 16, model, d=F32), vm(count + 1, 16, model, d=F32), vm(*x.shape), vm(tokens, model), vm(tokens, model)]
    scratch += [vm(heads, tokens, d=F32), vm(tokens, model, d=F32), vm(tokens, hidden)]
    scratch += [vm(*two, r, hidden), vm(*two, r, hidden), vm(*two, r, inner), vm(3, *two, r, inner), vm(model, hidden), vm(model, hidden)]
    scratch += [vm(tokens, model), vm(tokens, model), vm(*x.shape), vm(*x.shape), vm(inner, tokens), vm(inner, tokens)]
    scratch += [vm(tokens, 2 * HD, d=F32)] * 2 + [vm(tokens, 128, d=F32)]
    sems = lambda m: pltpu.SemaphoreType.DMA((m,))
    m = len(chunks) * count
    scratch += [sems(m), sems(m), sems(count + 1), sems(count + 1), sems(4), sems(4), sems(20)]
    flat = lambda a: a.reshape(*a.shape[: a.ndim - count - 2], model, a.shape[-1])
    by_block = lambda a: a.reshape(*two, r, a.shape[-1])

    def body(slopes_ref, table_ref, *refs):
        backward_kernel(count, chunks, SCATTER_MODES, SCATTER_ORDER, SCATTER_PLAN, slopes_ref, table_ref, refs[:17], refs[17 : 17 + len(outs)], refs[17 + len(outs) :])

    return pl.pallas_call(
        body, out_shape=outs, in_specs=[pl.BlockSpec(memory_space=pltpu.SMEM), VM] + [ANY] * 17, out_specs=[VM] * len(outs), scratch_shapes=scratch,
        compiler_params=pltpu.CompilerParams(collective_id=1, has_side_effects=True, vmem_limit_bytes=67043328), name="backward_all",
    )(slopes, table, x, cot, a1, q, k, v, o, lse, x2, a2, by_block(u), gp, by_block(gdown), flat(qkv_w), flat(proj_w), flat(up_w), flat(down_w))

def finish_kernel(count, *refs):
    ins, outs, refs = refs[:count], refs[count : 2 * count], refs[2 * count :]
    gains_o, shifts_o, bufs, (in_sem, out_sem) = refs[0], refs[1], refs[2 : 2 + count], refs[2 + count :]
    reads = [pltpu.make_async_copy(a, b, in_sem.at[i]) for i, (a, b) in enumerate(zip(ins, bufs))]
    writes = [pltpu.make_async_copy(b, c, out_sem.at[i]) for i, (b, c) in enumerate(zip(bufs, outs))]
    for copy in reads:
        copy.start()
    for read, write in zip(reads, writes):
        read.wait()
        write.start()
    part = gains_o.shape[1]
    base = (2 * lax.axis_index("dp") + lax.axis_index("tensor")) * part
    block = bufs[-1][0:8, span(base // 128, 128)]
    turned = pltpu.roll(block, lax.rem(128 - lax.rem(base, 128), 128), 1)
    gains_o[...] = turned[0:2, 0:part]
    shifts_o[...] = turned[2:6, 0:part]
    for copy in writes:
        copy.wait()


def finish(arrays, part):
    count = len(arrays)
    vectors = (jax.ShapeDtypeStruct((2, part), F32), jax.ShapeDtypeStruct((4, part), F32))
    return pl.pallas_call(
        functools.partial(finish_kernel, count), out_shape=tuple(jax.ShapeDtypeStruct(a.shape, a.dtype) for a in arrays) + vectors,
        in_specs=[ANY] * count, out_specs=[ANY] * count + [VM] * 2,
        scratch_shapes=[pltpu.VMEM(a.shape, a.dtype) for a in arrays] + [pltpu.SemaphoreType.DMA((count,))] * 2, name="finish")(*arrays)


def on_device(layer_in, w_qkv, b_qv, w_proj, w_ff1, b_ff1, w_ff2, norm_gains, add_biases, cotangent):
    n = lax.axis_size("dp")
    i = lax.axis_index("dp")
    t = lax.axis_index("tensor")
    width = w_qkv.shape[2]
    model = layer_in.shape[1]
    hidden = w_ff1.shape[1]
    heads = b_qv.shape[1]
    part = norm_gains.shape[1]
    zero = jnp.int32(0)
    put = lambda shape, a, at: lax.dynamic_update_slice(jnp.zeros(shape, F32), a.astype(F32), at)
    up_grid = (b_ff1.shape[0], n * b_ff1.shape[1])
    qv_grid = (*b_qv.shape[:2], n * b_qv.shape[2])
    small = jnp.concatenate([
        put((8, model), jnp.concatenate([norm_gains, add_biases]), (zero, (2 * i + t) * part)),
        put(up_grid, b_ff1, (zero, i * b_ff1.shape[1])).reshape(-1, model),
        put(qv_grid, b_qv, (zero, zero, i * b_qv.shape[2])).reshape(-1, model),
        jnp.zeros((8 - (hidden + 2 * width) // model, model), F32)])
    slopes = 2.0 ** (-8.0 * (t * heads + jnp.arange(heads, dtype=jnp.int32) + 1).astype(F32) / H)
    (qkv_w, proj_w, up_w, down_w, vectors, cot, a1, q, k, v, o, lse, x2, a2, u, rise, grad_down) = forward_all(
        slopes, w_qkv, w_proj.T, w_ff1, w_ff2.T, small, layer_in, cotangent, n)
    layer_out, grad_in, out_qkv, out_proj, out_up, out_down, sums = backward_all(
        slopes, vectors, layer_in, cot, a1, q, k, v, o, lse, x2, a2, u, rise, grad_down, qkv_w, proj_w, up_w, down_w, n)
    layer_out, grad_in, out_qkv, out_proj, out_up, out_down, sums, out_gains, out_shifts = finish(
        (layer_out, grad_in, out_qkv, out_proj, out_up, out_down, sums), part)
    up_sums = lax.dynamic_slice_in_dim(sums[8 : 8 + hidden // model].reshape(up_grid), i * b_ff1.shape[1], b_ff1.shape[1], 1)
    qv_sums = lax.dynamic_slice_in_dim(sums[10].reshape(qv_grid), i * b_qv.shape[2], b_qv.shape[2], 2)
    return (layer_out, grad_in, out_qkv, qv_sums, out_proj.T, out_up, up_sums, out_down.T, out_gains, out_shifts)


def solution(mesh):
    rows, cols = P(("dp", "tensor"), None), P(None, ("dp", "tensor"))
    return jax.shard_map(
        on_device,
        mesh=mesh,
        in_specs=(rows, P(None, "dp", "tensor"), P(None, "tensor", "dp"), P("tensor", "dp"), P("dp", "tensor"),
                  P("tensor", "dp"), P("tensor", "dp"), cols, cols, rows),
        out_specs=(rows, rows, P(None, "dp", "tensor"), P(None, "tensor", "dp"), P("tensor", "dp"), P("dp", "tensor"),
                   P("tensor", "dp"), P("tensor", "dp"), cols, cols),
        check_vma=False,
    )
```
